128 devices in a mesh: bricks: 128 (over y, z, x, core).
Axes of the slice: x: 4, y: 4, z: 4, core: 2. Of those that a mesh axis runs over, the one named last changes fastest.
Arguments:
- calcium: float32 [256, 32, 1024], P('bricks'), may hold values from 0.2 to 1.5
- buffer: float32 [256, 32, 1024], P('bricks'), may hold values from 0.1 to 1.5
- fraction: float32 [256, 32, 1024], P('bricks'), may hold values from 0.1 to 0.4
- rates: float32 [256, 3, 2], P('bricks'), may hold values from 2 to 64
- inverses: float32 [256, 3, 2, 32, 32], P('bricks'), as said below
- neighbors: int32 [3, 2, 256], replicated, may hold values from -1 to 255, as said below
- ranks: int32 [3, 256], replicated, may hold values from 0 to 31, as said below
Outputs:
- calcium_next: float32 [256, 32, 1024], P('bricks')
- buffer_next: float32 [256, 32, 1024], P('bricks')
The draws below stay inside these ranges and needn't reach their ends.
Inputs may be any that keep to these rules, and one draw needn't show every extreme that they name: neighbors[d, 0, s] and neighbors[d, 1, s] are the slots of the active bricks adjacent to slot s before and after it along dimension d of a block of 32 x 16 x 2 brick positions, -1 where that position is inactive or outside; active bricks fill whole rows along the first dimension. ranks[d, s] is the number of consecutive active bricks before slot s along dimension d. inverses[s, d, k] is the inverse of I + rates[s, d, k] K, K the 32 x 32 second difference with diagonal 1, 2, ..., 2, 1 and off-diagonals -1.
All inputs are finite; a program needn't handle non-finite values.
Results may differ from the reference program's by a relative error of at most 0.00015.
Values sent between devices are 32-bit elements; how exact they have to be, the bound alone decides.
A program may use at most 128 MiB of HBM per device.

```python
import math
import jax
import jax.numpy as jnp
from jax import lax

BS = 32
GX = 32
GY = 16
NB = 256
ROWS = 8
GZ = 2


def chain_tables(key):
    key_start, key_cells, key_slots = jax.random.split(jax.random.fold_in(key, 7), 3)
    cells_all = GY * GZ
    run_length = max(2, 3 * ROWS // 4)
    y_start = jax.random.randint(key_start, (), 0, GY).astype(jnp.int32)
    cell_id = jnp.arange(cells_all, dtype=jnp.int32)
    along = (cell_id - y_start * GZ) % cells_all
    shuffled = jax.random.permutation(key_cells, cells_all).astype(jnp.int32)
    score = jnp.where(along < run_length, along, run_length + shuffled)
    cells = jnp.argsort(score)[:ROWS].astype(jnp.int32)
    brick = jnp.arange(NB, dtype=jnp.int32)
    cell = cells[brick // GX].astype(jnp.int32)
    position = jnp.stack([brick % GX, cell // GZ, cell % GZ], 0)
    slot = jax.random.permutation(key_slots, NB).astype(jnp.int32)
    grid = jnp.full((GX, GY, GZ), -1, jnp.int32).at[position[0], position[1], position[2]].set(slot)
    extent = [GX, GY, GZ]
    near_rows = []
    rank_rows = []
    for d in range(3):
        sides = []
        for delta in (-1, 1):
            moved = position.at[d].add(delta)
            inside = (moved[d] >= 0) & (moved[d] < extent[d])
            clipped = [jnp.clip(moved[a], 0, extent[a] - 1) for a in range(3)]
            sides.append(jnp.where(inside, grid[clipped[0], clipped[1], clipped[2]], -1))
        near_rows.append(jnp.stack(sides, 0))
        alive = jnp.ones((NB,), jnp.int32)
        run = jnp.zeros((NB,), jnp.int32)
        for step in range(1, extent[d]):
            moved = position.at[d].add(-step)
            inside = moved[d] >= 0
            clipped = [jnp.clip(moved[a], 0, extent[a] - 1) for a in range(3)]
            occupied = jnp.where(inside & (grid[clipped[0], clipped[1], clipped[2]] >= 0), 1, 0)
            alive = alive * occupied
            run = run + alive
        rank_rows.append(run)
    near = jnp.stack(near_rows, 0)
    rank = jnp.stack(rank_rows, 0)
    near_slot = jnp.zeros((3, 2, NB), jnp.int32).at[:, :, slot].set(near)
    rank_slot = jnp.zeros((3, NB), jnp.int32).at[:, slot].set(rank)
    return (near_slot, rank_slot)


def rate_tables(key):
    inner = jax.random.fold_in(key, 11)
    rate = jnp.exp(jax.random.uniform(inner, (NB, 3, 2), jnp.float32, jnp.log(2.0), jnp.log(64.0)))
    order = jnp.arange(BS, dtype=jnp.float32)
    wave = order[:, None]
    place = order[None, :]
    basis = jnp.where(wave == 0, jnp.sqrt(1.0 / BS), jnp.sqrt(2.0 / BS) * jnp.cos(jnp.pi * wave * (place + 0.5) / BS))
    eigen = 2.0 - 2.0 * jnp.cos(jnp.pi * order / BS)
    weight = 1.0 / (1.0 + rate[..., None] * eigen)
    inverse = jnp.einsum('ja,bdsj,jc->bdsac', basis, weight, basis, precision=lax.Precision.HIGHEST)
    return (rate, inverse)


def draw_rates(key, part):
    return rate_tables(key)[0]


def draw_inverses(key, part):
    return rate_tables(key)[1]


def draw_neighbors(key, part):
    return chain_tables(key)[0]


def draw_ranks(key, part):
    return chain_tables(key)[1]


def block_levels(key, shape, cuts, smallest, top_value):
    factor_of = 1.0
    for dim, blocks in cuts:
        steps = jax.random.uniform(jax.random.fold_in(jax.random.fold_in(key, 6), dim), (blocks,), jnp.float32, smallest / len(cuts), top_value / len(cuts))
        factor_of = factor_of * jnp.repeat(jnp.exp(steps), shape[dim] // blocks).reshape((-1,) + (1,) * (len(shape) - 1 - dim))
    return factor_of


def setup_inputs(seed: int = 0) -> dict:
    streams_of = jax.random.split(jax.random.key(seed), 8)
    calcium = jnp.clip(0.2 + 1.3 * jax.random.uniform(streams_of[0], (NB, BS, BS * BS), jnp.float32) ** block_levels(streams_of[0], (NB, BS, BS * BS), ((0, 128),), -0.2, 0.2), 0.2, 1.5)
    buffer = jnp.clip(0.1 + 1.4 * jax.random.uniform(streams_of[1], (NB, BS, BS * BS), jnp.float32) ** block_levels(streams_of[1], (NB, BS, BS * BS), ((0, 128),), -0.2, 0.2), 0.1, 1.5)
    fraction = jnp.clip(jnp.exp(math.log(0.4) - 1.3862944 * jax.random.uniform(streams_of[2], (NB, BS, BS * BS), jnp.float32) ** block_levels(streams_of[2], (NB, BS, BS * BS), ((0, 128),), -0.2, 0.2)), 0.1, 0.4)
    rates = draw_rates(jax.random.fold_in(streams_of[7], 71), 0)
    inverses = draw_inverses(jax.random.fold_in(streams_of[7], 71), 0)
    neighbors = draw_neighbors(jax.random.fold_in(streams_of[7], 71), 0)
    ranks = draw_ranks(jax.random.fold_in(streams_of[7], 71), 0)
    return dict(calcium=calcium, buffer=buffer, fraction=fraction, rates=rates, inverses=inverses, neighbors=neighbors, ranks=ranks)


KON = 0.5
KOFF = 0.3
BTOT = 2.0
INFLUX = 0.1


def fetch(table, index):
    rows = jnp.take(table, jnp.maximum(index, 0), axis=0)
    has = (index >= 0).reshape((-1,) + (1,) * (rows.ndim - 1))
    return jnp.where(has, rows, jnp.zeros_like(rows))


def lookup(planes, before, after):
    sides = []
    for d in range(3):
        lower = fetch(planes[:, d, 1], before[d])
        upper = fetch(planes[:, d, 0], after[d])
        sides.append(jnp.stack([lower, upper], 1))
    return jnp.stack(sides, 1)


def coupling(rate_all, neighbors):
    per_dim = []
    for d in range(3):
        mine = rate_all[:, d]
        sides = []
        for side in range(2):
            other = fetch(mine, neighbors[d, side])
            has = (neighbors[d, side] >= 0)[:, None]
            sides.append(jnp.where(has, 2.0 * mine * other / (mine + other), jnp.zeros_like(mine)))
        per_dim.append(jnp.stack(sides, 1))
    return jnp.stack(per_dim, 1)


def end_planes(field):
    count, edge = field.shape[0], field.shape[2]
    per_dim = []
    for d in range(3):
        first = lax.index_in_dim(field, 0, 2 + d, False).reshape(count, 2, edge * edge)
        last = lax.index_in_dim(field, edge - 1, 2 + d, False).reshape(count, 2, edge * edge)
        per_dim.append(jnp.stack([first, last], 1))
    return jnp.stack(per_dim, 1)


def operator(field, d, rate, glow, gup, hlow, hup):
    axis = 2 + d
    edge = field.shape[axis]
    plane_shape = lax.index_in_dim(field, 0, axis, False).shape
    lower_face = jnp.expand_dims(hlow.reshape(plane_shape), axis)
    upper_face = jnp.expand_dims(hup.reshape(plane_shape), axis)
    upper = jnp.concatenate([lax.slice_in_dim(field, 1, edge, axis=axis), upper_face], axis)
    lower = jnp.concatenate([lower_face, lax.slice_in_dim(field, 0, edge - 1, axis=axis)], axis)
    place = lax.broadcasted_iota(jnp.int32, field.shape, axis)
    inner = rate[:, :, None, None, None]
    c_up = jnp.where(place == edge - 1, gup[:, :, None, None, None], inner)
    c_down = jnp.where(place == 0, glow[:, :, None, None, None], inner)
    return c_up * (upper - field) + c_down * (lower - field)


def reaction(field, fraction):
    count, edge = field.shape[0], field.shape[2]
    alpha = fraction.reshape(count, edge, edge, edge)
    calc, bound = field[:, 0], field[:, 1]
    bind = KON * calc * (BTOT - bound) - KOFF * bound
    return jnp.stack([-bind + INFLUX * (1.0 - alpha) / alpha, bind], 1)


def apply_inverse(block, field, d):
    forms = ["psab,psbjk->psajk", "psab,psibk->psiak", "psab,psijb->psija"]
    return jnp.einsum(forms[d], block, field, precision=lax.Precision.HIGHEST)


def line_ends(field, d):
    count, edge = field.shape[0], field.shape[2]
    first = lax.index_in_dim(field, 0, 2 + d, False).reshape(count, 2, edge * edge)
    last = lax.index_in_dim(field, edge - 1, 2 + d, False).reshape(count, 2, edge * edge)
    return jnp.stack([first, last], 2)


def reduced_solve(ends, glow, gup, corner, before, after, rank, levels):
    v_first, v_last, w_first, w_last = corner[..., 0], corner[..., 1], corner[..., 2], corner[..., 3]
    a00 = 1.0 + glow * v_first
    a01 = gup * w_first
    a10 = glow * v_last
    a11 = 1.0 + gup * w_last
    lq0 = -glow * v_first
    lq1 = -glow * v_last
    up0 = -gup * w_first
    up1 = -gup * w_last
    y0 = ends[:, :, 0]
    y1 = ends[:, :, 1]
    has_b = before >= 0
    has_a = after >= 0
    idx_b = jnp.maximum(before, 0)
    idx_a = jnp.maximum(after, 0)

    def forward(t, carry):
        e0, e1, f0, f1 = carry
        fq = jnp.where(has_b[:, None], jnp.take(f1, idx_b, axis=0), jnp.zeros_like(f1))
        eq = jnp.where(has_b[:, None, None], jnp.take(e1, idx_b, axis=0), jnp.zeros_like(e1))
        b00 = a00 - lq0 * fq
        b10 = a10 - lq1 * fq
        z0 = y0 - lq0[:, :, None] * eq
        z1 = y1 - lq1[:, :, None] * eq
        det = b00 * a11 - a01 * b10
        n_e0 = (a11[:, :, None] * z0 - a01[:, :, None] * z1) / det[:, :, None]
        n_e1 = (b00[:, :, None] * z1 - b10[:, :, None] * z0) / det[:, :, None]
        n_f0 = (a11 * up0 - a01 * up1) / det
        n_f1 = (b00 * up1 - b10 * up0) / det
        now = rank == t
        return (jnp.where(now[:, None, None], n_e0, e0), jnp.where(now[:, None, None], n_e1, e1),
                jnp.where(now[:, None], n_f0, f0), jnp.where(now[:, None], n_f1, f1))

    start = (jnp.zeros_like(y0), jnp.zeros_like(y1), jnp.zeros_like(a00), jnp.zeros_like(a00))
    e0, e1, f0, f1 = lax.fori_loop(0, levels, forward, start)

    def backward(step, carry):
        t = levels - 1 - step
        zp, zq = carry
        pn = jnp.where(has_a[:, None, None], jnp.take(zp, idx_a, axis=0), jnp.zeros_like(zp))
        new_p = e0 - f0[:, :, None] * pn
        new_q = e1 - f1[:, :, None] * pn
        now = (rank == t)[:, None, None]
        return (jnp.where(now, new_p, zp), jnp.where(now, new_q, zq))

    zp, zq = lax.fori_loop(0, levels, backward, (jnp.zeros_like(y0), jnp.zeros_like(y1)))
    low = jnp.where(has_b[:, None, None], zp - jnp.take(zq, idx_b, axis=0), jnp.zeros_like(zp))
    high = jnp.where(has_a[:, None, None], zq - jnp.take(zp, idx_a, axis=0), jnp.zeros_like(zq))
    return jnp.stack([low, high], 2)


def correct(local, block, glow, gup, jumps, d):
    axis = 2 + d
    count, edge = local.shape[0], local.shape[2]
    shape_v = [count, 2, 1, 1, 1]
    shape_v[axis] = edge
    first_col = block[..., 0].reshape(shape_v)
    last_col = block[..., edge - 1].reshape(shape_v)
    plane_shape = lax.index_in_dim(local, 0, axis, False).shape
    low = jnp.expand_dims(jumps[:, :, 0].reshape(plane_shape), axis)
    high = jnp.expand_dims(jumps[:, :, 1].reshape(plane_shape), axis)
    return local - glow[:, :, None, None, None] * low * first_col - gup[:, :, None, None, None] * high * last_col


def reference(calcium, buffer, fraction, rates, inverses, neighbors, ranks):
    count, edge = calcium.shape[0], calcium.shape[1]
    levels = [GX, GY, GZ]
    couple = coupling(rates, neighbors)
    corner = jnp.stack([inverses[..., 0, 0], inverses[..., edge - 1, 0], inverses[..., 0, edge - 1], inverses[..., edge - 1, edge - 1]], -1)
    field = jnp.stack([calcium, buffer], 1).reshape(count, 2, edge, edge, edge)
    halos = lookup(end_planes(field), neighbors[:, 0], neighbors[:, 1])
    lams = [operator(field, d, rates[:, d], couple[:, d, 0], couple[:, d, 1], halos[:, d, 0], halos[:, d, 1]) for d in range(3)]
    rhs = field + lams[0] + 2.0 * lams[1] + 2.0 * lams[2] + reaction(field, fraction)

    def solve(right, d):
        block = inverses[:, d]
        local = apply_inverse(block, right, d)
        jumps = reduced_solve(line_ends(local, d), couple[:, d, 0], couple[:, d, 1], corner[:, d], neighbors[d, 0], neighbors[d, 1], ranks[d], levels[d])
        return correct(local, block, couple[:, d, 0], couple[:, d, 1], jumps, d)

    first = solve(rhs, 0)
    second = solve(first - lams[1], 1)
    third = solve(second - lams[2], 2)
    result = third.reshape(count, 2, edge, edge * edge)
    return result[:, 0], result[:, 1]
```

```python
from functools import partial

import jax
import jax.numpy as jnp
from jax import lax
from jax.experimental import pallas as pl
from jax.experimental.pallas import tpu as pltpu
from jax.sharding import PartitionSpec as P

GX = 32


KON = 0.5
KOFF = 0.3
BTOT = 2.0
INFLUX = 0.1


MESH = pl.DeviceIdType.MESH


def exchange_kernel(n, x_ref, o_ref, land, send_sem, recv_sem, own_sem):
    me = lax.axis_index("bricks")
    barrier = pltpu.get_barrier_semaphore()

    def greet(step, carry):
        pl.semaphore_signal(
            barrier, inc=1, device_id=(lax.rem(me + step, n),), device_id_type=MESH
        )
        return carry

    lax.fori_loop(1, n, greet, 0)
    pl.semaphore_wait(barrier, n - 1)

    def send(step, carry):
        to = lax.rem(me + step, n)
        pltpu.make_async_remote_copy(
            src_ref=x_ref.at[to],
            dst_ref=land.at[me],
            send_sem=send_sem,
            recv_sem=recv_sem,
            device_id=(to,),
            device_id_type=MESH,
        ).start()
        return carry

    lax.fori_loop(1, n, send, 0)
    own = pltpu.make_async_copy(x_ref.at[me], land.at[me], own_sem)
    own.start()
    own.wait()
    every = pltpu.make_async_remote_copy(
        src_ref=x_ref.at[pl.ds(0, n - 1)],
        dst_ref=land.at[pl.ds(0, n - 1)],
        send_sem=send_sem,
        recv_sem=recv_sem,
        device_id=(me,),
        device_id_type=MESH,
    )
    every.wait_recv()
    every.wait_send()
    o_ref[...] = land[...]


def exchange(blocks):
    n, size = blocks.shape
    rows = 2
    padded = jnp.pad(blocks, ((0, 0), (0, rows * 128 - size))).reshape(n, rows, 128)
    got = pl.pallas_call(
        partial(exchange_kernel, n),
        out_shape=jax.ShapeDtypeStruct((n, rows, 128), jnp.float32),
        in_specs=[pl.BlockSpec(memory_space=pltpu.VMEM)],
        out_specs=pl.BlockSpec(memory_space=pltpu.VMEM),
        scratch_shapes=[
            pltpu.VMEM((n, rows, 128), jnp.float32),
            pltpu.SemaphoreType.DMA,
            pltpu.SemaphoreType.DMA,
            pltpu.SemaphoreType.DMA,
        ],
        compiler_params=pltpu.CompilerParams(collective_id=0, has_side_effects=True),
    )(padded)
    return got.reshape(n, rows * 128)[:, :size]


def to_lines(values):
    split = values.ndim - 2
    n = values.shape[split]
    moved = jnp.moveaxis(values, split, 0)
    got = exchange(moved.reshape(n, -1))
    return got.reshape((n * values.shape[0],) + values.shape[1:split] + (1,) + values.shape[split + 1 :])


def to_bricks(values):
    split = values.ndim - 2
    n = lax.axis_size("bricks")
    got = exchange(values.reshape(n, -1))
    shaped = got.reshape((n, values.shape[0] // n) + values.shape[1:split] + values.shape[split + 1 :])
    return jnp.moveaxis(shaped, 0, split)


def fetch(table, index):
    rows = jnp.take(table, jnp.maximum(index, 0), axis=0)
    has = (index >= 0).reshape((-1,) + (1,) * (rows.ndim - 1))
    return jnp.where(has, rows, jnp.zeros_like(rows))


def lookup(planes, before, after):
    sides = []
    for d in range(3):
        lower = fetch(planes[:, d, 1], before[d])
        upper = fetch(planes[:, d, 0], after[d])
        sides.append(jnp.stack([lower, upper], 1))
    return jnp.stack(sides, 1)


def coupling(rate_all, neighbors):
    per_dim = []
    for d in range(3):
        mine = rate_all[:, d]
        sides = []
        for side in range(2):
            other = fetch(mine, neighbors[d, side])
            has = (neighbors[d, side] >= 0)[:, None]
            sides.append(jnp.where(has, 2.0 * mine * other / (mine + other), jnp.zeros_like(mine)))
        per_dim.append(jnp.stack(sides, 1))
    return jnp.stack(per_dim, 1)


def end_planes(field):
    count, edge = (field.shape[0], field.shape[2])
    per_dim = []
    for d in range(3):
        first = lax.index_in_dim(field, 0, 2 + d, False).reshape(count, 2, edge * edge)
        last = lax.index_in_dim(field, edge - 1, 2 + d, False).reshape(count, 2, edge * edge)
        per_dim.append(jnp.stack([first, last], 1))
    return jnp.stack(per_dim, 1)


def operator(field, d, rate, glow, gup, hlow, hup):
    axis = 2 + d
    edge = field.shape[axis]
    plane_shape = lax.index_in_dim(field, 0, axis, False).shape
    lower_face = jnp.expand_dims(hlow.reshape(plane_shape), axis)
    upper_face = jnp.expand_dims(hup.reshape(plane_shape), axis)
    upper = jnp.concatenate([lax.slice_in_dim(field, 1, edge, axis=axis), upper_face], axis)
    lower = jnp.concatenate([lower_face, lax.slice_in_dim(field, 0, edge - 1, axis=axis)], axis)
    place = lax.broadcasted_iota(jnp.int32, field.shape, axis)
    inner = rate[:, :, None, None, None]
    c_up = jnp.where(place == edge - 1, gup[:, :, None, None, None], inner)
    c_down = jnp.where(place == 0, glow[:, :, None, None, None], inner)
    return c_up * (upper - field) + c_down * (lower - field)


def reaction(field, fraction):
    count, edge = (field.shape[0], field.shape[2])
    alpha = fraction.reshape(count, edge, edge, edge)
    calc, bound = (field[:, 0], field[:, 1])
    bind = KON * calc * (BTOT - bound) - KOFF * bound
    return jnp.stack([-bind + INFLUX * (1.0 - alpha) / alpha, bind], 1)


def apply_inverse(block, field, d):
    forms = ["psab,psbjk->psajk", "psab,psibk->psiak", "psab,psijb->psija"]
    return jnp.einsum(forms[d], block, field, precision=lax.Precision.HIGHEST)


def line_ends(field, d):
    count, edge = (field.shape[0], field.shape[2])
    first = lax.index_in_dim(field, 0, 2 + d, False).reshape(count, 2, edge * edge)
    last = lax.index_in_dim(field, edge - 1, 2 + d, False).reshape(count, 2, edge * edge)
    return jnp.stack([first, last], 2)


def block_terms(glow, gup, corner):
    v_first, v_last, w_first, w_last = (
        corner[..., 0],
        corner[..., 1],
        corner[..., 2],
        corner[..., 3],
    )
    a00 = 1.0 + glow * v_first
    a01 = gup * w_first
    a10 = glow * v_last
    a11 = 1.0 + gup * w_last
    lq0 = -glow * v_first
    lq1 = -glow * v_last
    up0 = -gup * w_first
    up1 = -gup * w_last
    return (a00, a01, a10, a11, lq0, lq1, up0, up1)


def chain_order(before, rank):
    slots = jnp.arange(before.shape[0], dtype=jnp.int32)
    pointer = jnp.where(before >= 0, before, slots)
    for step in range(GX.bit_length()):
        pointer = jnp.take(pointer, pointer, axis=0)
    sort_key = pointer * GX + rank
    order = jnp.argsort(sort_key)
    inverse_order = jnp.argsort(order)
    return (order, inverse_order)


def shift_down(values):
    return jnp.concatenate([jnp.zeros_like(values[:1]), values[:-1]], 0)


def shift_up(values):
    return jnp.concatenate([values[1:], jnp.zeros_like(values[:1])], 0)


def compose_maps(first_map, second_map):
    e00, e01, e10, e11 = first_map
    l00, l01, l10, l11 = second_map
    n00 = l00 * e00 + l01 * e10
    n01 = l00 * e01 + l01 * e11
    n10 = l10 * e00 + l11 * e10
    n11 = l10 * e01 + l11 * e11
    scale = jnp.abs(n00) + jnp.abs(n01) + jnp.abs(n10) + jnp.abs(n11)
    return (n00 / scale, n01 / scale, n10 / scale, n11 / scale)


def compose_affine(first_map, second_map):
    first_q, first_p = first_map
    second_q, second_p = second_map
    return (first_q * second_q, second_p + second_q * first_p)


def sorted_solve(glow, gup, corner, before, after, order, inverse_order, ends):
    glow = jnp.take(glow, order, axis=0)
    gup = jnp.take(gup, order, axis=0)
    corner = jnp.take(corner, order, axis=0)
    has_b = jnp.take(before, order, axis=0) >= 0
    has_a = jnp.take(after, order, axis=0) >= 0
    arranged = jnp.take(ends, order, axis=0)
    y0 = arranged[:, :, 0]
    y1 = arranged[:, :, 1]
    a00, a01, a10, a11, lq0, lq1, up0, up1 = block_terms(glow, gup, corner)
    maps = (
        -(lq0 * up1 - lq1 * up0),
        a00 * up1 - a10 * up0,
        -(lq0 * a11 - a01 * lq1),
        a00 * a11 - a01 * a10,
    )
    summed = lax.associative_scan(compose_maps, maps, axis=0)
    f1_prev = summed[1] / summed[3]
    fq = shift_down(f1_prev)
    b00 = a00 - lq0 * fq
    b10 = a10 - lq1 * fq
    det = b00 * a11 - a01 * b10
    f0 = (a11 * up0 - a01 * up1) / det
    f1 = (b00 * up1 - b10 * up0) / det
    slope = (-(b00 * lq1 - b10 * lq0) / det)[:, :, None]
    offset = (b00[:, :, None] * y1 - b10[:, :, None] * y0) / det[:, :, None]
    e1 = lax.associative_scan(compose_affine, (slope, offset), axis=0)[1]
    eq = shift_down(e1)
    e0 = (
        a11[:, :, None] * y0 - a01[:, :, None] * y1 - (a11 * lq0 - a01 * lq1)[:, :, None] * eq
    ) / det[:, :, None]
    zp = lax.associative_scan(compose_affine, (-f0[:, :, None], e0), reverse=True, axis=0)[1]
    pn = shift_up(zp)
    zq = e1 - f1[:, :, None] * pn
    low = jnp.where(has_b[:, None, None], zp - shift_down(zq), jnp.zeros_like(zp))
    high = jnp.where(has_a[:, None, None], zq - pn, jnp.zeros_like(zq))
    return jnp.take(jnp.stack([low, high], 2), inverse_order, axis=0)


def correct(local, block, glow, gup, jumps, d):
    axis = 2 + d
    count, edge = (local.shape[0], local.shape[2])
    shape_v = [count, 2, 1, 1, 1]
    shape_v[axis] = edge
    first_col = block[..., 0].reshape(shape_v)
    last_col = block[..., edge - 1].reshape(shape_v)
    plane_shape = lax.index_in_dim(local, 0, axis, False).shape
    low = jnp.expand_dims(jumps[:, :, 0].reshape(plane_shape), axis)
    high = jnp.expand_dims(jumps[:, :, 1].reshape(plane_shape), axis)
    return (
        local
        - glow[:, :, None, None, None] * low * first_col
        - gup[:, :, None, None, None] * high * last_col
    )


def body(calcium, buffer, fraction, rates, inverses, neighbors, ranks):
    count, edge = (calcium.shape[0], calcium.shape[1])
    devices = lax.axis_size("bricks")
    square = edge * edge
    per_device = square // devices
    start = lax.axis_index("bricks") * count
    corners = jnp.stack(
        [
            inverses[..., 0, 0],
            inverses[..., edge - 1, 0],
            inverses[..., 0, edge - 1],
            inverses[..., edge - 1, edge - 1],
        ],
        -1,
    )
    rate_all, corner_all = (
        lax.all_gather(rates, "bricks", axis=0, tiled=True),
        lax.all_gather(corners, "bricks", axis=0, tiled=True),
    )
    couple_all = coupling(rate_all, neighbors)
    couple = lax.dynamic_slice_in_dim(couple_all, start, count, 0)
    field = jnp.stack([calcium, buffer], 1).reshape(count, 2, edge, edge, edge)
    planes = end_planes(field).reshape(count, 3, 2, 2, devices, per_device)
    lined = lookup(
        to_lines(planes),
        neighbors[:, 0],
        neighbors[:, 1],
    )
    halos = to_bricks(lined).reshape(
        count, 3, 2, 2, square
    )
    lams = [
        operator(
            field, d, rates[:, d], couple[:, d, 0], couple[:, d, 1], halos[:, d, 0], halos[:, d, 1]
        )
        for d in range(3)
    ]
    rhs = field + lams[0] + 2.0 * lams[1] + 2.0 * lams[2] + reaction(field, fraction)

    def solve(right, d):
        block = inverses[:, d]
        local = apply_inverse(block, right, d)
        ends = line_ends(local, d).reshape(count, 2, 2, devices, per_device)
        order, inverse_order = chain_order(neighbors[d, 0], ranks[d])
        chain_fn = partial(
            sorted_solve,
            couple_all[:, d, 0],
            couple_all[:, d, 1],
            corner_all[:, d],
            neighbors[d, 0],
            neighbors[d, 1],
            order,
            inverse_order,
        )
        lined_jumps = chain_fn(
            to_lines(ends)[:, :, :, 0]
        )[:, :, :, None]
        jumps = to_bricks(lined_jumps).reshape(count, 2, 2, square)
        return correct(local, block, couple[:, d, 0], couple[:, d, 1], jumps, d)

    first = solve(rhs, 0)
    second = solve(first - lams[1], 1)
    third = solve(second - lams[2], 2)
    result = third.reshape(count, 2, edge, edge * edge)
    return (result[:, 0], result[:, 1])


def solution(mesh):
    in_specs = (
        P("bricks", None, None),
        P("bricks", None, None),
        P("bricks", None, None),
        P("bricks", None, None),
        P("bricks", None, None, None, None),
        P(),
        P(),
    )
    out_specs = (P("bricks", None, None), P("bricks", None, None))
    return jax.shard_map(body, mesh=mesh, in_specs=in_specs, out_specs=out_specs, check_vma=False)
```

```python
import jax
import jax.numpy as jnp
from jax import lax
from jax.experimental import pallas as pl
from jax.experimental.pallas import tpu as pltpu
from jax.sharding import PartitionSpec as P

KON = 0.5
KOFF = 0.3
BTOT = 2.0
INFLUX = 0.1

MESH = pl.DeviceIdType.MESH
F32 = jnp.float32
BF16 = jnp.bfloat16
HIGH = lax.Precision.HIGHEST
N = 128
E = 32
OWNERS = 64


def iota(shape, axis):
    return lax.broadcasted_iota(jnp.int32, shape, axis)


def roll(x, shift, axis=-1):
    if axis < 0:
        axis += x.ndim
    if isinstance(shift, int):
        shift %= x.shape[axis]
        if shift == 0:
            return x
    return pltpu.roll(x, shift, axis)


def rho_of(r):
    h = 0.5 / r
    s = jnp.sqrt(h * (2.0 + h))
    return 1.0 + h - s, s - h


def power(log_rho, n):
    return jnp.exp(log_rho * n.astype(F32))


def corners(r):
    rho, gap = rho_of(r)
    p2 = rho * rho
    p4 = p2 * p2
    p8 = p4 * p4
    p16 = p8 * p8
    p32 = p16 * p16
    kappa = rho / (r * gap * (1.0 - p32 * p32))
    return kappa * (1.0 + p32 * p32 / rho), kappa * (p32 / rho + p32)


def column(r, index):
    rho, gap = rho_of(r)
    lr = jnp.log(rho)
    kappa = rho / (r * gap * (1.0 - jnp.exp(lr * 64.0)))
    return kappa * (power(lr, index) + power(lr, 63 - index))


def inverse_blocks(r):
    rho, gap = rho_of(r)
    lr = jnp.log(rho)
    scale = rho / (r * gap * (1.0 + rho) * (1.0 - jnp.exp(lr * 64.0)))
    row, col = iota((N, N), 0), iota((N, N), 1)
    a, b = row & 31, col & 31
    away = jnp.abs(a - b)
    total = power(lr, away) + power(lr, a + b + 1) + power(lr, 63 - a - b) + power(lr, 64 - away)
    return jnp.where((row >> 5) == (col >> 5), total * scale, 0.0)


def sweep_terms(r, index):
    rho, _ = rho_of(r)
    lr = jnp.log(rho)
    rho2 = rho * rho
    odd = power(lr, 2 * index + 1)
    ratio = rho * (1.0 + odd) / (1.0 + odd * rho2)
    last = jnp.exp(lr * 61.0)
    ratio30 = rho * (1.0 + last) / (1.0 + last * rho2)
    m = jnp.where(index == E - 1, 1.0 / (1.0 + r - r * ratio30), ratio / r)
    return m, m * r


def swap_blocks(x, grp):
    low = grp < 2
    even = (grp & 1) == 0
    y = [None] * 4
    for q in range(2):
        a, b = x[q], x[q + 2]
        y[q] = jnp.where(low, a, roll(b, 64))
        y[q + 2] = jnp.where(low, roll(a, 64), b)
    z = [None] * 4
    for q in (0, 2):
        a, b = y[q], y[q + 1]
        z[q] = jnp.where(even, a, roll(b, 32))
        z[q + 1] = jnp.where(even, roll(a, -32), b)
    return z


def split3(x):
    a = x.astype(BF16)
    rest = x - a.astype(F32)
    b = rest.astype(BF16)
    c = (rest - b.astype(F32)).astype(BF16)
    return a, b, c


def pick(select, x):
    out = None
    for part in split3(x):
        term = jnp.dot(select, part, preferred_element_type=F32)
        out = term if out is None else out + term
    return out


def pick_right(x, select):
    out = None
    for part in split3(x):
        term = jnp.dot(part, select, preferred_element_type=F32)
        out = term if out is None else out + term
    return out


def dot(a, b):
    return jnp.dot(a, b, precision=HIGH, preferred_element_type=F32)


def dot_first(a, b):
    return lax.dot_general(
        a, b, (((0,), (0,)), ((), ())), precision=HIGH, preferred_element_type=F32
    )


def one_hot(cond):
    return jnp.where(cond, 1.0, 0.0).astype(BF16)


def total(x, axis):
    return jnp.sum(x, axis=axis, keepdims=True)


def step_kernel(
    rates, nbs, nbv, rkv, cal, buf, frac, out_c, out_b,
    u_ref, f_ref, t_ref, g_ref, msg0, rt, send1, land1, send2, land2,
    co0, co1, ecm, ece, e_ref, pl_ref, perm, permt, kk, chain,
    ss0, rs0, ss1, rs1, ss2, rs2, own_sem,
):
    me = lax.axis_index("bricks")
    barrier = pltpu.get_barrier_semaphore()

    def greet(step, carry):
        pl.semaphore_signal(
            barrier, inc=1, device_id=(lax.rem(me + step, N),), device_id_type=MESH
        )
        return carry

    lax.fori_loop(1, N, greet, 0)

    lane = iota((1, N), 1)
    lane32 = lane & 31
    grp = lane >> 5
    sub8 = iota((8, N), 0)
    row32 = iota((E, N), 0)

    own = []
    for d in range(3):
        r = jnp.zeros((1, N), F32)
        for q in range(4):
            r = jnp.where(grp == q, rates[q // 2, d, q % 2], r)
        own.append(r)
    message = jnp.where(lane32 == 0, own[0], jnp.where(lane32 == 1, own[1], own[2]))
    msg0[0] = message
    near = {}
    for name, d, side in (("yl", 1, 0), ("yu", 1, 1), ("zl", 2, 0), ("zu", 2, 1)):
        near[name] = [nbs[d, side, 2 * me + b] for b in range(2)]
    near["z"] = [jnp.maximum(near["zl"][b], near["zu"][b]) for b in range(2)]

    def by_brick(pair):
        return jnp.where(lane < 64, pair[0], pair[1])

    up = by_brick([jnp.where(v >= 0, 1, 0) for v in near["zu"]]) == 1
    upf = jnp.where(up, 1.0, 0.0)
    face_lane = lane32 == jnp.where(up, E - 1, 0)

    def lay(t, carry):
        cols = pl.ds(pl.multiple_of(t * N, N), N)
        us, fs = [], []
        for b in range(2):
            ca, bo, al = cal[b, :, cols], buf[b, :, cols], frac[b, :, cols]
            bind = KON * ca * (BTOT - bo) - KOFF * bo
            us += [ca, bo]
            fs += [2.0 * ca - bind + INFLUX * (1.0 - al) / al, 2.0 * bo + bind]
        us = swap_blocks(us, grp)
        fs = swap_blocks(fs, grp)
        for m in range(4):
            at = pl.ds(pl.multiple_of((t * 4 + m) * E, E), E)
            u_ref[at, :] = us[m]
            f_ref[at, :] = fs[m]
        return carry

    lax.fori_loop(0, 8, lay, 0)

    m, e = sweep_terms(own[0], row32)
    co0[0] = m
    co0[1] = e
    m, e = sweep_terms(own[1], row32)
    co1[0] = m
    co1[1] = e

    pl.semaphore_wait(barrier, N - 1)

    def send_rates(step, carry):
        to = lax.rem(me + step, N)
        pltpu.make_async_remote_copy(
            msg0, rt.at[pl.ds(me, 1)], ss0, rs0, device_id=(to,), device_id_type=MESH
        ).start()
        return carry

    lax.fori_loop(1, N, send_rates, 0)
    keep = pltpu.make_async_copy(msg0, rt.at[pl.ds(me, 1)], own_sem.at[0])
    keep.start()

    def face(j, plane):
        u = u_ref[pl.ds(pl.multiple_of(j * E, E), E), :]
        first = roll(u, j)
        last = roll(u, j + (N - E + 1))
        return jnp.where(lane32 == j, jnp.where(up, last, first), plane)

    wz = lax.fori_loop(0, E, face, jnp.zeros((E, N), F32))

    owner = lax.rem(me, 2) == 0

    @pl.when(owner)
    def _():
        s2, l2 = iota((256, 256), 0), iota((256, 256), 1)
        lane256 = iota((1, 256), 1)

        def heads(before, doublings):
            target = jnp.where(before < 0, lane256, before)
            step = one_hot(s2 == target)
            for _ in range(doublings):
                step = jnp.dot(step, step, preferred_element_type=F32).astype(BF16)
            return step

        before0, before1 = nbv[0, 0:1, :], nbv[1, 0:1, :]
        znear = jnp.maximum(nbv[2, 0:1, :], nbv[2, 1:2, :]).astype(F32)
        rank0, rank1 = rkv[0:1, :].astype(F32), rkv[1:2, :].astype(F32)
        lead = jnp.dot(heads(before1, 3), heads(before0, 5), preferred_element_type=F32)
        key = total(lead * s2.astype(F32), 0) * 32.0 + rank1
        keyed = total(jnp.where(s2 == l2, key + rank0 * 1e5, 0.0), 1)
        row = total(jnp.where(keyed < key, 1.0, 0.0), 0)
        pos = rank0 * 8.0 + row
        at = s2.astype(F32) == pos
        slot_at = total(jnp.where(at, lane256.astype(F32), 0.0), 1)
        rank_at = total(jnp.where(at, rank1, 0.0), 1)
        z_at = total(jnp.where(at, znear, 0.0), 1)
        kk[0] = jnp.where(rank_at > 0.5, 1.0, jnp.zeros((256, N), F32))
        dev = lane.astype(F32) * 2.0
        s1, l1 = iota((N, 256), 0), iota((N, 256), 1)
        lf = l1.astype(F32)
        for b in range(2):
            perm[b] = one_hot(slot_at == dev + b)
            perm[2 + b] = one_hot(z_at == dev + b)
            mine = l1 == 2 * s1 + b
            pos_b = total(jnp.where(mine, pos, 0.0), 1)
            z_b = total(jnp.where(mine, znear, 0.0), 1)
            posz_b = total(jnp.where(lf == z_b, pos + 1.0, 0.0), 1) - 1.0
            permt[b] = one_hot(lf == pos_b)
            permt[2 + b] = one_hot(lf == posz_b)

    keep.wait()
    arrive = pltpu.make_async_remote_copy(
        rt.at[pl.ds(0, N - 1)], rt.at[pl.ds(0, N - 1)], ss0, rs0, device_id=(me,), device_id_type=MESH
    )
    arrive.wait_recv()

    def rates_of(indices):
        rows = []
        for b in range(2):
            index = jnp.maximum(indices[b], 0)
            got = rt[index >> 1]
            cross = (index & 1) != b
            rows.append(jnp.where(cross, roll(got, 64), got))
        got = jnp.where(lane < 64, rows[0], rows[1])
        has = by_brick([jnp.where(indices[b] >= 0, 1.0, 0.0) for b in range(2)])
        return got, has

    stack = jnp.ones((8, N), F32)
    has = jnp.zeros((8, N), F32)
    for at, name in ((0, "yu"), (1, "yl"), (2, "z")):
        got, there = rates_of(near[name])
        stack = jnp.where(sub8 == at, got, stack)
        has = jnp.where(sub8 == at, there, has)
    stack = jnp.where(sub8 == 3, message, stack)
    near_r = []
    for d in range(3):
        x = roll(jnp.where(lane32 == d, stack, 0.0), -d)
        for shift in (1, 2, 4, 8, 16):
            x = x + roll(x, shift)
        near_r.append(x)
    g1 = has * 2.0 * own[1] * near_r[1] / (own[1] + near_r[1])
    g2 = has * 2.0 * own[2] * near_r[2] / (own[2] + near_r[2])
    gyu, gyl, gz = g1[0:1], g1[1:2], g2[2:3]

    cu2 = jnp.where(lane32 < E - 1, 2.0 * own[2], 0.0)
    cd2 = jnp.where(lane32 > 0, 2.0 * own[2], 0.0)
    dg2 = cu2 + cd2 + jnp.where(face_lane, 2.0 * gz, 0.0)
    r1x2 = 2.0 * own[1]

    def right_side(j, prev):
        at = pl.ds(pl.multiple_of(j * E, E), E)
        u = u_ref[at, :]
        nxt = u_ref[pl.ds(pl.multiple_of(jnp.minimum(j + 1, E - 1) * E, E), E), :]
        low = jnp.where(j == 0, 0.0, r1x2)
        high = jnp.where(j == E - 1, 0.0, r1x2)
        out_low = jnp.where(j == 0, 2.0 * gyl, r1x2)
        out_high = jnp.where(j == E - 1, 2.0 * gyu, r1x2)
        f_ref[at, :] = (
            f_ref[at, :]
            + cu2 * roll(u, -1)
            + cd2 * roll(u, 1)
            + low * prev
            + high * nxt
            - (dg2 + out_low + out_high) * u
        )
        return u

    lax.fori_loop(0, E, right_side, jnp.zeros((E, N), F32))

    u_first, u_last = u_ref[0:E, :], u_ref[(E - 1) * E : E * E, :]
    s_up = 2.0 * gyu * u_last
    s_low = 2.0 * gyl * u_first
    s_z = 2.0 * gz * wz

    i8 = iota((E, 8, N), 0)
    mm, ee = sweep_terms(near_r[0][None], i8)
    ecm[...] = mm
    ece[...] = ee

    def solve_i(load_plane_row):
        def forward(i, carry):
            g, h = carry
            at = pl.ds(i, E, stride=E)
            g = co0[0, pl.ds(i, 1), :] * f_ref[at, :] + co0[1, pl.ds(i, 1), :] * g
            t_ref[at, :] = g
            h = ecm[i] * load_plane_row(i) + ece[i] * h
            e_ref[i] = h
            return g, h

        g, h = lax.fori_loop(0, E, forward, (jnp.zeros((E, N), F32), jnp.zeros((8, N), F32)))

        def backward(step, carry):
            i = E - 2 - step
            x, h = carry
            at = pl.ds(i, E, stride=E)
            x = t_ref[at, :] + co0[1, pl.ds(i, 1), :] * x
            t_ref[at, :] = x
            h = e_ref[i] + ece[i] * h
            e_ref[i] = h
            return x, h

        lax.fori_loop(0, E - 1, backward, (g, h))

    def solve_j(extra_first, extra_last):
        def forward(j, g):
            at = pl.ds(pl.multiple_of(j * E, E), E)
            d = t_ref[at, :] - 2.0 * u_ref[at, :]
            if extra_first is not None:
                d = d + jnp.where(j == 0, extra_first, 0.0) + jnp.where(j == E - 1, extra_last, 0.0)
            g = co1[0, pl.ds(j, 1), :] * d + co1[1, pl.ds(j, 1), :] * g
            g_ref[at, :] = g
            return g

        g = lax.fori_loop(0, E, forward, jnp.zeros((E, N), F32))

        def backward(step, x):
            j = E - 2 - step
            at = pl.ds(pl.multiple_of(j * E, E), E)
            x = g_ref[at, :] + co1[1, pl.ds(j, 1), :] * x
            g_ref[at, :] = x
            return x

        lax.fori_loop(0, E - 1, backward, g)

    pl_ref[0] = s_up
    pl_ref[1] = s_low
    pl_ref[2] = s_z

    def first_rows(i):
        x = jnp.where(sub8 == 0, pl_ref[0, pl.ds(i, 1), :], 0.0)
        x = jnp.where(sub8 == 1, pl_ref[1, pl.ds(i, 1), :], x)
        return jnp.where(sub8 == 2, pl_ref[2, pl.ds(i, 1), :], x)

    solve_i(first_rows)
    for p in range(3):
        pl_ref[p] = e_ref[:, p, :]
    solve_j(None, None)

    rowN, colN = iota((N, N), 0), iota((N, N), 1)
    kin = rowN & 31
    weight = column(own[2], jnp.where(up, E - 1 - kin, kin))
    weight = jnp.where((rowN >> 5) == (colN >> 5), weight, 0.0)

    def face_mean(j, plane):
        y = g_ref[pl.ds(pl.multiple_of(j * E, E), E), :]
        return jnp.where(lane32 == j, dot(y, weight), plane)

    t_own = lax.fori_loop(0, E, face_mean, jnp.zeros((E, N), F32))

    y0f = t_ref[pl.ds(0, E, stride=E), :]
    y0l = t_ref[pl.ds(E - 1, E, stride=E), :]
    y1f, y1l = g_ref[0:E, :], g_ref[(E - 1) * E : E * E, :]
    rows_a = jnp.transpose(jnp.concatenate([y0f, y0l, y1f, y1l], 0))
    rows_b = jnp.transpose(jnp.concatenate([s_up, s_low, pl_ref[0], pl_ref[1]], 0))
    pz = pl_ref[2]
    v1z = column(near_r[1][2:3], lane32)
    w1z = column(near_r[1][2:3], E - 1 - lane32)
    ends = jnp.where(
        (sub8 & 3) == grp, jnp.where(sub8 < 4, v1z, w1z), 0.0
    )
    ends_i = lax.dot_general(
        ends, pz, (((1,), (1,)), ((), ())), precision=HIGH, preferred_element_type=F32
    )
    ends_i = jnp.concatenate([ends_i, jnp.zeros((8, N - E), F32)], 1)
    for q in range(4):
        b, sp = q // 2, q % 2
        base = sp * 8 + b * 4
        send1[pl.ds(base, E, stride=16), :] = rows_a[q * E : (q + 1) * E]
        send1[pl.ds(base + 1, E, stride=16), :] = rows_b[q * E : (q + 1) * E]
        c = jnp.where(lane < 32, roll(pz[0:1], -E * q), roll(pz[E - 1 : E], E - E * q))
        c = jnp.where(lane < 64, c, roll(ends_i[q : q + 1], 64))
        c = jnp.where(lane < 96, c, roll(ends_i[q + 4 : q + 5], 96))
        kf = jnp.where(near["zu"][b] >= 0, 0, E - 1)
        send1[pl.ds(base + 2, E, stride=16), :] = jnp.where(row32 == kf, c, 0.0)
        dd = jnp.where(
            lane < 32, roll(s_z, -E * q), jnp.where(lane < 64, roll(t_own, E - E * q), 0.0)
        )
        send1[pl.ds(base + 3, E, stride=16), :] = roll(dd, 64)

    def block(ref, index):
        return ref.at[pl.ds(pl.multiple_of(index * 8, 8), 8)]

    mine = me // 2

    def send_ends(step, carry):
        o = lax.rem(mine + step, OWNERS)
        pltpu.make_async_remote_copy(
            block(send1, o), block(land1, me), ss1, rs1, device_id=(2 * o,), device_id_type=MESH
        ).start()
        return carry

    lax.fori_loop(1, OWNERS, send_ends, 0)

    @pl.when(jnp.logical_not(owner))
    def _():
        pltpu.make_async_remote_copy(
            block(send1, mine), block(land1, me), ss1, rs1, device_id=(2 * mine,), device_id_type=MESH
        ).start()

    @pl.when(owner)
    def _():
        local = pltpu.make_async_copy(block(send1, mine), block(land1, me), own_sem.at[1])
        local.start()
        sp32 = lax.rem(mine, 2) * 32
        table = rt[:, 0, :]
        ordered = pick(perm[0], table) + pick(perm[1], roll(table, 64))
        pick_at = iota((N, 2 * N), 0)
        pick_to = iota((N, 2 * N), 1) >> 7
        both = pick_right(ordered, one_hot(pick_at == sp32 + pick_to))
        r0, r1 = both[:, 0:N], both[:, N : 2 * N]
        p256 = iota((256, N), 0)
        linked = kk[0]
        dims = []
        for d, r in ((0, r0), (1, r1)):
            alpha, eps = corners(r)
            if d == 0:
                before = jnp.concatenate([r[0:8], r[0:248]], 0)
                gl = jnp.where(p256 >= 8, 2.0 * r * before / (r + before), 0.0)
                gr = jnp.concatenate([gl[8:256], jnp.zeros((8, N), F32)], 0)
            else:
                before = roll(r, 1, 0)
                gl = linked * 2.0 * r * before / (r + before)
                gr = roll(gl, -1, 0)
            dims.append((alpha, eps, gl, gr))
            chain[0 + 4 * d] = alpha
            chain[1 + 4 * d] = eps
            chain[2 + 4 * d] = gl
            chain[3 + 4 * d] = gr

        def elimination(alpha, eps, gl, gr, fq):
            b00 = 1.0 + gl * alpha * (1.0 + fq)
            b10 = gl * eps * (1.0 + fq)
            det = b00 * (1.0 + gr * alpha) - gr * eps * b10
            return b00, b10, 1.0 / det

        def along(x, fq):
            at = pl.ds(pl.multiple_of(x * 8, 8), 8)
            alpha, eps, gl, gr = [chain[c, at, :] for c in range(4)]
            kk[1, at, :] = fq
            b00, b10, inv = elimination(alpha, eps, gl, gr, fq)
            return -gr * (b00 * alpha - b10 * eps) * inv

        lax.fori_loop(0, E, along, jnp.zeros((8, N), F32))
        alpha, eps, gl, gr = dims[1]
        fq = jnp.zeros((256, N), F32)
        for _ in range(7):
            b00, b10, inv = elimination(alpha, eps, gl, gr, fq)
            fq = linked * roll(-gr * (b00 * alpha - b10 * eps) * inv, 1, 0)
        kk[2] = fq

        def terms(d, fq):
            alpha, eps, gl, gr = [chain[4 * d + c] for c in range(4)]
            b00, b10, inv = elimination(alpha, eps, gl, gr, fq)
            a01, a11 = gr * eps, 1.0 + gr * alpha
            base = 3 + 8 * d
            kk[base] = b00 * inv
            kk[base + 1] = -b10 * inv
            kk[base + 2] = a11 * inv
            kk[base + 3] = -a01 * inv
            kk[base + 4] = gl * (a11 * alpha - a01 * eps) * inv
            kk[base + 5] = -gr * (b00 * alpha - b10 * eps) * inv
            kk[base + 6] = gl * (b00 * eps - b10 * alpha) * inv
            kk[base + 7] = gr * eps * inv

        terms(0, kk[1])
        terms(1, kk[2])
        both_l = lane32 + 0 * p256
        j_of = jnp.where((grp & 1) == 0, both_l, E - 1 - both_l)
        chain[8] = column(r1, j_of)
        chain[9] = column(r0, both_l)
        chain[10] = column(r0, E - 1 - both_l)
        local.wait()
        got = pltpu.make_async_remote_copy(
            land1.at[pl.ds(0, 8 * (N - 1))], land1.at[pl.ds(0, 8 * (N - 1))], ss1, rs1,
            device_id=(me,), device_id_type=MESH,
        )
        got.wait_recv()

        def ordered_rows(kind, which):
            return pick(perm[which], land1[pl.ds(kind, N, stride=8), :]) + pick(
                perm[which + 1], land1[pl.ds(4 + kind, N, stride=8), :]
            )

        link_next = roll(kk[0], -1, 0)
        ya = ordered_rows(0, 0) + ordered_rows(2, 2)
        yb = ordered_rows(1, 0)
        yd = ordered_rows(3, 0)
        bl = kk[0] * roll(yb, 1, 0)
        bu = link_next * roll(yb, -1, 0)
        out2 = jnp.where(lane < 32, bl, jnp.where(lane < 64, bu, yd))
        straight = jnp.where(lane < 96, bl, bu)
        crossed = jnp.where(lane < 96, roll(bu, -32), roll(bl, 32))
        ya = ya + jnp.where(lane >= 64, chain[4] * straight + chain[5] * crossed, 0.0)
        ya = ya + jnp.where(lane == 0, roll(bl, 64), 0.0) + jnp.where(lane == 32, roll(bl, 65), 0.0)
        ya = ya + jnp.where(lane == 31, roll(bu, 63), 0.0) + jnp.where(lane == 63, roll(bu, 64), 0.0)

        def before_x(v, n):
            return jnp.concatenate([jnp.zeros((8 * n, N), F32), v[0 : 256 - 8 * n]], 0)

        def after_x(v, n):
            return jnp.concatenate([v[8 * n : 256], jnp.zeros((8 * n, N), F32)], 0)

        def before_y(v, n):
            return roll(v, n, 0)

        def after_y(v, n):
            return roll(v, -n, 0)

        def chains(y0, y1, d, gl, gr, before, after, steps):
            base = 3 + 8 * d
            e1 = kk[base] * y1 + kk[base + 1] * y0
            slope = kk[base + 6]
            for n in steps:
                e1 = e1 + slope * before(e1, n)
                slope = slope * before(slope, n)
            e0 = kk[base + 2] * y0 + kk[base + 3] * y1 + kk[base + 4] * before(e1, 1)
            slope = kk[base + 7]
            zp = e0
            for n in steps:
                zp = zp + slope * after(zp, n)
                slope = slope * after(slope, n)
            zp_next = after(zp, 1)
            zq = e1 + -kk[base + 5] * zp_next
            return -gl * (zp - before(zq, 1)), -gr * (zq - zp_next)

        al, ar = chains(
            ya, roll(ya, -32), 0, chain[2], chain[3], before_x, after_x, (1, 2, 4, 8, 16)
        )
        spread = jnp.where(
            lane < 64,
            jnp.where(lane < 32, al, roll(al, 32)),
            jnp.where(lane < 96, roll(ar, 64), roll(ar, 96)),
        )
        src = iota((N, 2 * N), 0) >> 5
        dst = iota((N, 2 * N), 1)
        side, part = dst >> 7, (dst >> 5) & 3
        sums = pick_right(
            spread * chain[8], one_hot((part >= 2) & (src == 2 * side + part - 2))
        )
        ya = ya + chain[9] * sums[:, 0:N] + chain[10] * sums[:, N : 2 * N]
        bl_c, br_c = chains(ya, roll(ya, -32), 1, chain[6], chain[7], before_y, after_y, (1, 2, 4))
        out1 = jnp.where(
            lane < 64,
            jnp.where(lane < 32, al, roll(ar, 32)),
            jnp.where(lane < 96, bl_c, roll(br_c, 32)),
        )
        for b in range(2):
            for kind, which, what in ((0, b, out1), (1, b, out2), (2, 2 + b, out1), (3, 2 + b, out2)):
                send2[pl.ds(b * 4 + kind, N, stride=8), :] = pick(permt[which], what)

        def send_back(step, carry):
            to = lax.rem(me + step, N)
            pltpu.make_async_remote_copy(
                block(send2, to), block(land2, mine), ss2, rs2, device_id=(to,), device_id_type=MESH
            ).start()
            return carry

        lax.fori_loop(1, N, send_back, 0)
        local = pltpu.make_async_copy(block(send2, me), block(land2, mine), own_sem.at[2])
        local.start()
        local.wait()

    def arrived2(count):
        part = land2.at[pl.ds(0, 8 * count)]
        pltpu.make_async_remote_copy(
            part, part, ss2, rs2, device_id=(me,), device_id_type=MESH
        ).wait_recv()

    @pl.when(owner)
    def _():
        arrived2(OWNERS - 1)

    @pl.when(jnp.logical_not(owner))
    def _():
        arrived2(OWNERS)

    def gathered(kind):
        return jnp.concatenate(
            [land2[pl.ds((q % 2) * 8 + (q // 2) * 4 + kind, E, stride=16), :] for q in range(4)], 0
        )

    own_ab, own_h, near_ab, near_h = [gathered(kind) for kind in range(4)]
    ab = jnp.transpose(own_ab)
    halo = jnp.transpose(own_h)
    w_near = jnp.zeros((E, N), F32)
    t_near = jnp.zeros((E, N), F32)
    for q in range(4):
        part = near_h[q * E : (q + 1) * E]
        w_near = jnp.where(grp == q, roll(part, E * q - 64), w_near)
        t_near = jnp.where(grp == q, roll(part, E * q - 96), t_near)

    kz_own = jnp.where(up, E - 1 - lane32, lane32)
    kz_near = jnp.where(up, lane32, E - 1 - lane32)
    alpha_z = [corners(near_r[2][at : at + 1])[0] for at in (3, 2)]
    planes, outer = [], []
    for which, at, kz, rows_ab, rows_h, wplane in (
        (0, 3, kz_own, own_ab, own_h, w_near),
        (1, 2, kz_near, near_ab, near_h, s_z),
    ):
        weights = jnp.where(sub8 == grp, column(near_r[2][at : at + 1], kz), 0.0)
        ca = dot(weights, rows_ab)
        ch = dot(weights, rows_h)
        first_row = jnp.zeros((1, N), F32)
        last_row = jnp.zeros((1, N), F32)
        for q in range(4):
            first_row = jnp.where(grp == q, roll(ca[q : q + 1], E * q), first_row)
            last_row = jnp.where(grp == q, roll(ca[q : q + 1], E * q - E), last_row)
        mark = jnp.concatenate(
            [
                jnp.where((sub8 == grp) & (lane32 == 0), 1.0, 0.0),
                jnp.where((sub8 == grp) & (lane32 == E - 1), 1.0, 0.0),
            ],
            1,
        )
        marked = dot_first(ch, mark)
        plane = marked[0:E, 0:N] + marked[E : 2 * E, N : 2 * N] + alpha_z[which] * wplane
        plane = plane + jnp.where(row32 == 0, first_row, 0.0)
        plane = plane + jnp.where(row32 == E - 1, last_row, 0.0)
        pl_ref[which] = plane
        cols = jnp.concatenate(
            [
                jnp.where(sub8 == grp, column(near_r[1][at : at + 1], lane32), 0.0),
                jnp.where(sub8 == grp, column(near_r[1][at : at + 1], E - 1 - lane32), 0.0),
            ],
            1,
        )
        sides = dot_first(ca, cols)
        outer.append(sides[64:96, 0:N] + sides[96:128, N : 2 * N])

    halo_low, halo_up = halo[0:E], halo[E : 2 * E]
    f_ref[0:E, :] = f_ref[0:E, :] + halo_low
    f_ref[(E - 1) * E : E * E, :] = f_ref[(E - 1) * E : E * E, :] + halo_up
    at = pl.ds(0, E, stride=E)
    f_ref[at, :] = f_ref[at, :] + ab[0:E]
    at = pl.ds(E - 1, E, stride=E)
    f_ref[at, :] = f_ref[at, :] + ab[E : 2 * E]

    def on_face(plane, j):
        first = roll(plane, N - j)
        last = roll(plane, lax.rem(N + E - 1 - j, N))
        return jnp.where(face_lane, jnp.where(up, last, first), 0.0)

    def z_halo(j, carry):
        at = pl.ds(pl.multiple_of(j * E, E), E)
        f_ref[at, :] = f_ref[at, :] + on_face(w_near, j)
        return carry

    lax.fori_loop(0, E, z_halo, 0)

    def last_rows(i):
        x = jnp.where(sub8 == 3, pl_ref[0, pl.ds(i, 1), :], 0.0)
        return jnp.where(sub8 == 2, pl_ref[1, pl.ds(i, 1), :], x)

    solve_i(last_rows)
    ends_z = []
    for which, at in ((0, 3), (1, 2)):
        blocks = inverse_blocks(near_r[1][at : at + 1])
        ends_z.append(dot(e_ref[:, at, :], blocks) + outer[which])
    sigma = ends_z[0] + t_own
    tau = ends_z[1] + t_near
    c_plane = -gz * (sigma - tau) / (1.0 + gz * (alpha_z[0] + alpha_z[1]))

    solve_j(ab[64:96], ab[96:128])
    zblocks = inverse_blocks(own[2])

    def finish(t, carry):
        outs = []
        for m in range(4):
            j = t * 4 + m
            at = pl.ds(pl.multiple_of(j * E, E), E)
            d2 = g_ref[at, :] + on_face(c_plane, j)
            outs.append(u_ref[at, :] + dot(d2, zblocks))
        outs = swap_blocks(outs, grp)
        cols = pl.ds(pl.multiple_of(t * N, N), N)
        for b in range(2):
            out_c[b, :, cols] = outs[2 * b]
            out_b[b, :, cols] = outs[2 * b + 1]
        return carry

    lax.fori_loop(0, 8, finish, 0)

    arrive.wait_send()

    def left1(count):
        part = send1.at[pl.ds(0, 8 * count)]
        pltpu.make_async_remote_copy(
            part, part, ss1, rs1, device_id=(me,), device_id_type=MESH
        ).wait_send()

    @pl.when(owner)
    def _():
        left1(OWNERS - 1)
        part = send2.at[pl.ds(0, 8 * (N - 1))]
        pltpu.make_async_remote_copy(
            part, part, ss2, rs2, device_id=(me,), device_id_type=MESH
        ).wait_send()

    @pl.when(jnp.logical_not(owner))
    def _():
        left1(OWNERS)


def body(calcium, buffer, fraction, rates, inverses, neighbors, ranks):
    vmem = pl.BlockSpec(memory_space=pltpu.VMEM)
    smem = pl.BlockSpec(memory_space=pltpu.SMEM)
    shape = jax.ShapeDtypeStruct(calcium.shape, F32)
    field = pltpu.VMEM((E * E, N), F32)
    return pl.pallas_call(
        step_kernel,
        out_shape=(shape, shape),
        in_specs=[smem, smem, vmem, vmem, vmem, vmem, vmem],
        out_specs=(vmem, vmem),
        scratch_shapes=[
            field,
            field,
            field,
            field,
            pltpu.VMEM((1, 1, N), F32),
            pltpu.VMEM((N, 1, N), F32),
            pltpu.VMEM((8 * OWNERS, N), F32),
            pltpu.VMEM((8 * N, N), F32),
            pltpu.VMEM((8 * N, N), F32),
            pltpu.VMEM((8 * OWNERS, N), F32),
            pltpu.VMEM((2, E, N), F32),
            pltpu.VMEM((2, E, N), F32),
            pltpu.VMEM((E, 8, N), F32),
            pltpu.VMEM((E, 8, N), F32),
            pltpu.VMEM((E, 8, N), F32),
            pltpu.VMEM((3, E, N), F32),
            pltpu.VMEM((4, 256, N), BF16),
            pltpu.VMEM((4, N, 256), BF16),
            pltpu.VMEM((19, 256, N), F32),
            pltpu.VMEM((11, 256, N), F32),
        ]
        + [pltpu.SemaphoreType.DMA] * 6
        + [pltpu.SemaphoreType.DMA((3,))],
        compiler_params=pltpu.CompilerParams(
            collective_id=0, has_side_effects=True, vmem_limit_bytes=60 * 1024 * 1024
        ),
    )(rates, neighbors, neighbors, ranks, calcium, buffer, fraction)


def solution(mesh):
    in_specs = (
        P("bricks", None, None),
        P("bricks", None, None),
        P("bricks", None, None),
        P("bricks", None, None),
        P("bricks", None, None, None, None),
        P(),
        P(),
    )
    out_specs = (P("bricks", None, None), P("bricks", None, None))
    return jax.shard_map(body, mesh=mesh, in_specs=in_specs, out_specs=out_specs, check_vma=False)
```

```python
import jax
import jax.numpy as jnp
from jax import lax
from jax.experimental import pallas as pl
from jax.experimental.pallas import tpu as pltpu
from jax.sharding import PartitionSpec as P

KON = 0.5
KOFF = 0.3
BTOT = 2.0
INFLUX = 0.1

MESH = pl.DeviceIdType.MESH
F32 = jnp.float32
BF16 = jnp.bfloat16
HIGH = lax.Precision.HIGHEST
N = 128
E = 32
OWNERS = 64


def iota(shape, axis):
    return lax.broadcasted_iota(jnp.int32, shape, axis)


def roll(x, shift, axis=-1):
    if axis < 0:
        axis += x.ndim
    if isinstance(shift, int):
        shift %= x.shape[axis]
        if shift == 0:
            return x
    return pltpu.roll(x, shift, axis)


def rho_of(r):
    h = 0.5 / r
    s = jnp.sqrt(h * (2.0 + h))
    return 1.0 + h - s, s - h


def power(log_rho, n):
    return jnp.exp(log_rho * n.astype(F32))


def corners(r):
    rho, gap = rho_of(r)
    p2 = rho * rho
    p4 = p2 * p2
    p8 = p4 * p4
    p16 = p8 * p8
    p32 = p16 * p16
    kappa = rho / (r * gap * (1.0 - p32 * p32))
    return kappa * (1.0 + p32 * p32 / rho), kappa * (p32 / rho + p32)


def column(r, index):
    rho, gap = rho_of(r)
    lr = jnp.log(rho)
    kappa = rho / (r * gap * (1.0 - jnp.exp(lr * 64.0)))
    return kappa * (power(lr, index) + power(lr, 63 - index))


def inverse_blocks(r):
    rho, gap = rho_of(r)
    lr = jnp.log(rho)
    scale = rho / (r * gap * (1.0 + rho) * (1.0 - jnp.exp(lr * 64.0)))
    row, col = iota((N, N), 0), iota((N, N), 1)
    a, b = row & 31, col & 31
    away = jnp.abs(a - b)
    total = power(lr, away) + power(lr, a + b + 1) + power(lr, 63 - a - b) + power(lr, 64 - away)
    return jnp.where((row >> 5) == (col >> 5), total * scale, 0.0)


def sweep_terms(r, index):
    rho, _ = rho_of(r)
    lr = jnp.log(rho)
    rho2 = rho * rho
    odd = power(lr, 2 * index + 1)
    ratio = rho * (1.0 + odd) / (1.0 + odd * rho2)
    last = jnp.exp(lr * 61.0)
    ratio30 = rho * (1.0 + last) / (1.0 + last * rho2)
    m = jnp.where(index == E - 1, 1.0 / (1.0 + r - r * ratio30), ratio / r)
    return m, m * r


def swap_blocks(x, grp):
    low = grp < 2
    even = (grp & 1) == 0
    y = [None] * 4
    for q in range(2):
        a, b = x[q], x[q + 2]
        y[q] = jnp.where(low, a, roll(b, 64))
        y[q + 2] = jnp.where(low, roll(a, 64), b)
    z = [None] * 4
    for q in (0, 2):
        a, b = y[q], y[q + 1]
        z[q] = jnp.where(even, a, roll(b, 32))
        z[q + 1] = jnp.where(even, roll(a, -32), b)
    return z


def split3(x):
    a = x.astype(BF16)
    rest = x - a.astype(F32)
    b = rest.astype(BF16)
    c = (rest - b.astype(F32)).astype(BF16)
    return a, b, c


def pick(select, x):
    out = None
    for part in split3(x):
        term = jnp.dot(select, part, preferred_element_type=F32)
        out = term if out is None else out + term
    return out


def pick_right(x, select):
    out = None
    for part in split3(x):
        term = jnp.dot(part, select, preferred_element_type=F32)
        out = term if out is None else out + term
    return out


def split2(x):
    a = x.astype(BF16)
    return a, (x - a.astype(F32)).astype(BF16)


def contract(a, b, dims):
    ah, al = split2(a)
    bh, bl = split2(b)
    dims = (dims, ((), ()))
    out = lax.dot_general(ah, bh, dims, preferred_element_type=F32)
    out = out + lax.dot_general(al, bh, dims, preferred_element_type=F32)
    return out + lax.dot_general(ah, bl, dims, preferred_element_type=F32)


def dot(a, b):
    return contract(a, b, ((1,), (0,)))


def dot_first(a, b):
    return contract(a, b, ((0,), (0,)))


def dot_last(a, b):
    return contract(a, b, ((1,), (1,)))


def packed_weights(w):
    h, l = split2(w)
    return jnp.concatenate(
        [jnp.concatenate([h, l], 1), jnp.concatenate([h, jnp.zeros_like(h)], 1)], 0
    )


def packed_dot(x, weights):
    out = jnp.dot(jnp.concatenate(split2(x), 1), weights, preferred_element_type=F32)
    return out[:, 0:N] + out[:, N : 2 * N]


def one_hot(cond):
    return jnp.where(cond, 1.0, 0.0).astype(BF16)


def total(x, axis):
    return jnp.sum(x, axis=axis, keepdims=True)


def step_kernel(
    rates, nbs, nbv, rkv, cal, buf, frac, out_c, out_b,
    u_ref, f_ref, t_ref, g_ref, msg0, rt, send1, land1, send2, land2,
    co0, co1, ecm, ece, e_ref, pl_ref, perm, permt, kk, chain,
    ss0, rs0, ss1, rs1, ss2, rs2, own_sem,
):
    me = lax.axis_index("bricks")
    barrier = pltpu.get_barrier_semaphore()

    def greet(step, carry):
        pl.semaphore_signal(
            barrier, inc=1, device_id=((me + step) & (N - 1),), device_id_type=MESH
        )
        return carry

    lax.fori_loop(1, N, greet, 0)

    lane = iota((1, N), 1)
    lane32 = lane & 31
    grp = lane >> 5
    sub8 = iota((8, N), 0)
    row32 = iota((E, N), 0)

    own = []
    for d in range(3):
        r = jnp.zeros((1, N), F32)
        for q in range(4):
            r = jnp.where(grp == q, rates[q // 2, q % 2, d], r)
        own.append(r)
    message = jnp.where(lane32 == 0, own[0], jnp.where(lane32 == 1, own[1], own[2]))
    msg0[0] = message
    near = {}
    for name, d, side in (("yl", 1, 0), ("yu", 1, 1), ("zl", 2, 0), ("zu", 2, 1)):
        near[name] = [nbs[d, side, 2 * me + b] for b in range(2)]
    near["z"] = [jnp.maximum(near["zl"][b], near["zu"][b]) for b in range(2)]

    def by_brick(pair):
        return jnp.where(lane < 64, pair[0], pair[1])

    up = by_brick([jnp.where(v >= 0, 1, 0) for v in near["zu"]]) == 1
    upf = jnp.where(up, 1.0, 0.0)
    face_lane = lane32 == jnp.where(up, E - 1, 0)

    def lay(t, carry):
        cols = pl.ds(pl.multiple_of(t * N, N), N)
        us, fs = [], []
        for b in range(2):
            ca, bo, al = cal[b, :, cols], buf[b, :, cols], frac[b, :, cols]
            bind = KON * ca * (BTOT - bo) - KOFF * bo
            us += [ca, bo]
            fs += [2.0 * ca - bind + INFLUX * (1.0 - al) / al, 2.0 * bo + bind]
        us = swap_blocks(us, grp)
        fs = swap_blocks(fs, grp)
        for m in range(4):
            at = pl.ds(pl.multiple_of((t * 4 + m) * E, E), E)
            u_ref[at, :] = us[m]
            f_ref[at, :] = fs[m]
        return carry

    lax.fori_loop(0, 8, lay, 0)

    for co, r in ((co0, own[0]), (co1, own[1])):
        m, e = sweep_terms(r, row32)
        co[0] = m
        co[1] = e
        co[2] = jnp.where(row32 == E - 1, 0.0, e)

    pl.semaphore_wait(barrier, N - 1)

    def send_rates(step, carry):
        to = (me + step) & (N - 1)
        pltpu.make_async_remote_copy(
            msg0, rt.at[pl.ds(me, 1)], ss0, rs0, device_id=(to,), device_id_type=MESH
        ).start()
        return carry

    lax.fori_loop(1, N, send_rates, 0)
    keep = pltpu.make_async_copy(msg0, rt.at[pl.ds(me, 1)], own_sem.at[0])
    keep.start()

    def face(j, plane):
        u = u_ref[pl.ds(pl.multiple_of(j * E, E), E), :]
        first = roll(u, j)
        last = roll(u, j + (N - E + 1))
        return jnp.where(lane32 == j, jnp.where(up, last, first), plane)

    wz = lax.fori_loop(0, E, face, jnp.zeros((E, N), F32))

    owner = (me & 1) == 0

    @pl.when(owner)
    def _():
        s2, l2 = iota((256, 256), 0), iota((256, 256), 1)
        lane256 = iota((1, 256), 1)

        def heads(before, doublings):
            target = jnp.where(before < 0, lane256, before)
            step = one_hot(s2 == target)
            for _ in range(doublings):
                step = jnp.dot(step, step, preferred_element_type=F32).astype(BF16)
            return step

        before0, before1 = nbv[0, 0:1, :], nbv[1, 0:1, :]
        znear = jnp.maximum(nbv[2, 0:1, :], nbv[2, 1:2, :]).astype(F32)
        rank0, rank1 = rkv[0:1, :].astype(F32), rkv[1:2, :].astype(F32)
        lead = jnp.dot(heads(before1, 3), heads(before0, 5), preferred_element_type=F32)
        key = total(lead * s2.astype(F32), 0) * 32.0 + rank1
        keyed = total(jnp.where(s2 == l2, key + rank0 * 1e5, 0.0), 1)
        row = total(jnp.where(keyed < key, 1.0, 0.0), 0)
        pos = rank0 * 8.0 + row
        at = s2.astype(F32) == pos
        slot_at = total(jnp.where(at, lane256.astype(F32), 0.0), 1)
        rank_at = total(jnp.where(at, rank1, 0.0), 1)
        z_at = total(jnp.where(at, znear, 0.0), 1)
        kk[0] = jnp.where(rank_at > 0.5, 1.0, jnp.zeros((256, N), F32))
        dev = lane.astype(F32) * 2.0
        s1, l1 = iota((N, 256), 0), iota((N, 256), 1)
        lf = l1.astype(F32)
        for b in range(2):
            perm[b] = one_hot(slot_at == dev + b)
            perm[2 + b] = one_hot(z_at == dev + b)
            mine = l1 == 2 * s1 + b
            pos_b = total(jnp.where(mine, pos, 0.0), 1)
            z_b = total(jnp.where(mine, znear, 0.0), 1)
            posz_b = total(jnp.where(lf == z_b, pos + 1.0, 0.0), 1) - 1.0
            permt[b] = one_hot(lf == pos_b)
            permt[2 + b] = one_hot(lf == posz_b)

    cu2 = jnp.where(lane32 < E - 1, 2.0 * own[2], 0.0)
    cd2 = jnp.where(lane32 > 0, 2.0 * own[2], 0.0)
    dg2 = cu2 + cd2
    r1x2 = 2.0 * own[1]

    def right_side(t, prev):
        us = []
        for m in range(5):
            j = jnp.minimum(t * 4 + m, E - 1)
            us.append(u_ref[pl.ds(pl.multiple_of(j * E, E), E), :])
        for m in range(4):
            j = t * 4 + m
            at = pl.ds(pl.multiple_of(j * E, E), E)
            u = us[m]
            low = jnp.where(j == 0, 0.0, r1x2)
            high = jnp.where(j == E - 1, 0.0, r1x2)
            f_ref[at, :] = (
                f_ref[at, :]
                + cu2 * roll(u, -1)
                + cd2 * roll(u, 1)
                + low * prev
                + high * us[m + 1]
                - (dg2 + low + high) * u
            )
            prev = u
        return prev

    lax.fori_loop(0, E // 4, right_side, jnp.zeros((E, N), F32))

    def solve_i(load_plane_row):
        def forward(t, carry):
            g, h = carry
            for m in range(4):
                i = t * 4 + m
                at = pl.ds(i, E, stride=E)
                g = co0[0, pl.ds(i, 1), :] * f_ref[at, :] + co0[1, pl.ds(i, 1), :] * g
                t_ref[at, :] = g
                if load_plane_row is not None:
                    h = ecm[i] * load_plane_row(i) + ece[i] * h
                    e_ref[i] = h
            return g, h

        lax.fori_loop(0, E // 4, forward, (jnp.zeros((E, N), F32), jnp.zeros((8, N), F32)))

        def backward(t, carry):
            x, h = carry
            for m in range(4):
                i = E - 1 - t * 4 - m
                at = pl.ds(i, E, stride=E)
                x = t_ref[at, :] + co0[2, pl.ds(i, 1), :] * x
                t_ref[at, :] = x
                if load_plane_row is not None:
                    h = e_ref[i] + jnp.where(i == E - 1, 0.0, ece[i]) * h
                    e_ref[i] = h
            return x, h

        lax.fori_loop(0, E // 4, backward, (jnp.zeros((E, N), F32), jnp.zeros((8, N), F32)))

    def solve_j(extra_first, extra_last):
        def forward(t, g):
            for m in range(4):
                j = t * 4 + m
                at = pl.ds(pl.multiple_of(j * E, E), E)
                d = t_ref[at, :] - 2.0 * u_ref[at, :]
                if extra_first is not None and m == 0:
                    d = d + jnp.where(j == 0, extra_first, 0.0)
                if extra_last is not None and m == 3:
                    d = d + jnp.where(j == E - 1, extra_last, 0.0)
                g = co1[0, pl.ds(j, 1), :] * d + co1[1, pl.ds(j, 1), :] * g
                g_ref[at, :] = g
            return g

        lax.fori_loop(0, E // 4, forward, jnp.zeros((E, N), F32))

        def backward(t, x):
            for m in range(4):
                j = E - 1 - t * 4 - m
                at = pl.ds(pl.multiple_of(j * E, E), E)
                x = g_ref[at, :] + co1[2, pl.ds(j, 1), :] * x
                g_ref[at, :] = x
            return x

        lax.fori_loop(0, E // 4, backward, jnp.zeros((E, N), F32))

    solve_i(None)
    solve_j(None, None)

    rowN, colN = iota((N, N), 0), iota((N, N), 1)
    kin = rowN & 31
    weight = column(own[2], jnp.where(up, E - 1 - kin, kin))
    weight = packed_weights(jnp.where((rowN >> 5) == (colN >> 5), weight, 0.0))

    def face_mean(t, plane):
        y = packed_dot(g_ref[pl.ds(pl.multiple_of(t * 8 * E, 8 * E), 8 * E), :], weight)
        for m in range(8):
            plane = jnp.where(lane32 == t * 8 + m, y[m * E : (m + 1) * E], plane)
        return plane

    t_own = lax.fori_loop(0, 4, face_mean, jnp.zeros((E, N), F32))

    keep.wait()
    arrive = pltpu.make_async_remote_copy(
        rt.at[pl.ds(0, N - 1)], rt.at[pl.ds(0, N - 1)], ss0, rs0, device_id=(me,), device_id_type=MESH
    )
    arrive.wait_recv()

    def rates_of(indices):
        rows = []
        for b in range(2):
            index = jnp.maximum(indices[b], 0)
            got = rt[index >> 1]
            cross = (index & 1) != b
            rows.append(jnp.where(cross, roll(got, 64), got))
        got = jnp.where(lane < 64, rows[0], rows[1])
        has = by_brick([jnp.where(indices[b] >= 0, 1.0, 0.0) for b in range(2)])
        return got, has

    stack = jnp.ones((8, N), F32)
    has = jnp.zeros((8, N), F32)
    for at, name in ((0, "yu"), (1, "yl"), (2, "z")):
        got, there = rates_of(near[name])
        stack = jnp.where(sub8 == at, got, stack)
        has = jnp.where(sub8 == at, there, has)
    stack = jnp.where((sub8 >= 3) & (sub8 < 6), message, stack)
    near_r = []
    for d in range(3):
        x = roll(jnp.where(lane32 == d, stack, 0.0), -d)
        for shift in (1, 2, 4, 8, 16):
            x = x + roll(x, shift)
        near_r.append(x)
    g1 = has * 2.0 * own[1] * near_r[1] / (own[1] + near_r[1])
    g2 = has * 2.0 * own[2] * near_r[2] / (own[2] + near_r[2])
    gyu, gyl, gz = g1[0:1], g1[1:2], g2[2:3]

    u_first, u_last = u_ref[0:E, :], u_ref[(E - 1) * E : E * E, :]
    s_up = 2.0 * gyu * u_last
    s_low = 2.0 * gyl * u_first
    s_z = 2.0 * gz * wz
    i8 = iota((E, 8, N), 0)
    mm, ee = sweep_terms(near_r[0][None], i8)
    ecm[...] = mm
    ece[...] = ee
    pl_ref[0] = s_up
    pl_ref[1] = s_low
    pl_ref[2] = s_z

    h = jnp.zeros((8, N), F32)
    for i in range(E):
        x_up, x_low, x_z = [pl_ref[p, i : i + 1, :] for p in range(3)]
        x = jnp.where(sub8 == 0, x_up, jnp.where(sub8 == 1, x_low, x_z))
        x = jnp.where(sub8 == 3, -x_z, jnp.where(sub8 == 4, -x_low, jnp.where(sub8 == 5, -x_up, x)))
        h = ecm[i] * x + ece[i] * h
        e_ref[i] = h
    for i in range(E - 2, -1, -1):
        h = e_ref[i] + ece[i] * h
        e_ref[i] = h
    p_up, p_low, p_z, p_out, p_first, p_last = [e_ref[:, p, :] for p in range(6)]

    alpha_1, eps_1 = corners(own[1])
    out_first = jnp.where(row32 == 0, 1.0, 0.0)
    out_last = jnp.where(row32 == E - 1, 1.0, 0.0)
    y0f = t_ref[pl.ds(0, E, stride=E), :] + out_first * p_first[0:1] + out_last * p_last[0:1]
    y0l = (
        t_ref[pl.ds(E - 1, E, stride=E), :]
        + out_first * p_first[E - 1 : E]
        + out_last * p_last[E - 1 : E]
    )
    y1f = g_ref[0:E, :] + alpha_1 * p_first + eps_1 * p_last
    y1l = g_ref[(E - 1) * E : E * E, :] + eps_1 * p_first + alpha_1 * p_last
    rows_a = jnp.transpose(jnp.concatenate([y0f, y0l, y1f, y1l], 0))
    rows_b = jnp.transpose(jnp.concatenate([s_up, s_low, p_up, p_low], 0))
    group8 = (sub8 & 3) == grp
    ends_i = []
    for p, at in ((p_z, 2), (p_out, 3)):
        r1 = near_r[1][at : at + 1]
        ends = jnp.where(sub8 < 4, column(r1, lane32), column(r1, E - 1 - lane32))
        x = dot_last(jnp.where(group8, ends, 0.0), p)
        ends_i.append(jnp.concatenate([x, jnp.zeros((8, N - E), F32)], 1))

    def end_row(p, x, q):
        c = jnp.where(lane < 32, roll(p[0:1], -E * q), roll(p[E - 1 : E], E - E * q))
        c = jnp.where(lane < 64, c, roll(x[q : q + 1], 64))
        return jnp.where(lane < 96, c, roll(x[q + 4 : q + 5], 96))

    for q in range(4):
        b, sp = q // 2, q % 2
        base = sp * 8 + b * 4
        mine_up = near["zu"][b] >= 0
        kf = jnp.where(mine_up, E - 1, 0)
        kn = jnp.where(mine_up, 0, E - 1)
        part_a, part_b = rows_a[q * E : (q + 1) * E], rows_b[q * E : (q + 1) * E]
        send1[pl.ds(base, E, stride=16), :] = part_a + jnp.where(
            row32 == kf, end_row(p_out, ends_i[1], q), 0.0
        )
        send1[pl.ds(base + 1, E, stride=16), :] = part_b
        send1[pl.ds(base + 2, E, stride=16), :] = jnp.where(
            row32 == kn, end_row(p_z, ends_i[0], q), 0.0
        )
        out = jnp.where(lane < 32, -roll(part_b, -E), -roll(part_b, E))
        zt = jnp.where(lane < 96, roll(s_z, 64 - E * q), roll(t_own, 96 - E * q))
        send1[pl.ds(base + 3, E, stride=16), :] = jnp.where(lane < 64, out, zt)

    mine = me >> 1

    def block(ref, index):
        return ref.at[pl.ds(pl.multiple_of(index * 8, 8), 8)]

    mine = me >> 1

    def send_ends(step, carry):
        o = (mine + step) & (OWNERS - 1)
        pltpu.make_async_remote_copy(
            block(send1, o), block(land1, me), ss1, rs1, device_id=(2 * o,), device_id_type=MESH
        ).start()
        return carry

    lax.fori_loop(1, OWNERS, send_ends, 0)

    @pl.when(jnp.logical_not(owner))
    def _():
        pltpu.make_async_remote_copy(
            block(send1, mine), block(land1, me), ss1, rs1, device_id=(2 * mine,), device_id_type=MESH
        ).start()

    @pl.when(owner)
    def _():
        local = pltpu.make_async_copy(block(send1, mine), block(land1, me), own_sem.at[1])
        local.start()
        sp32 = (mine & 1) * 32
        table = rt[:, 0, :]
        ordered = pick(perm[0], table) + pick(perm[1], roll(table, 64))
        pick_at = iota((N, 2 * N), 0)
        pick_to = iota((N, 2 * N), 1) >> 7
        both = pick_right(ordered, one_hot(pick_at == sp32 + pick_to))
        r0, r1 = both[:, 0:N], both[:, N : 2 * N]
        p256 = iota((256, N), 0)
        linked = kk[0]
        dims = []
        for d, r in ((0, r0), (1, r1)):
            alpha, eps = corners(r)
            if d == 0:
                before = jnp.concatenate([r[0:8], r[0:248]], 0)
                gl = jnp.where(p256 >= 8, 2.0 * r * before / (r + before), 0.0)
                gr = jnp.concatenate([gl[8:256], jnp.zeros((8, N), F32)], 0)
            else:
                before = roll(r, 1, 0)
                gl = linked * 2.0 * r * before / (r + before)
                gr = roll(gl, -1, 0)
            dims.append((alpha, eps, gl, gr))
            chain[0 + 4 * d] = alpha
            chain[1 + 4 * d] = eps
            chain[2 + 4 * d] = gl
            chain[3 + 4 * d] = gr

        def elimination(alpha, eps, gl, gr, fq):
            b00 = 1.0 + gl * alpha * (1.0 + fq)
            b10 = gl * eps * (1.0 + fq)
            det = b00 * (1.0 + gr * alpha) - gr * eps * b10
            return b00, b10, 1.0 / det

        def along(x, fq):
            at = pl.ds(pl.multiple_of(x * 8, 8), 8)
            alpha, eps, gl, gr = [chain[c, at, :] for c in range(4)]
            kk[1, at, :] = fq
            b00, b10, inv = elimination(alpha, eps, gl, gr, fq)
            return -gr * (b00 * alpha - b10 * eps) * inv

        lax.fori_loop(0, E, along, jnp.zeros((8, N), F32))
        alpha, eps, gl, gr = dims[1]
        fq = jnp.zeros((256, N), F32)
        for _ in range(7):
            b00, b10, inv = elimination(alpha, eps, gl, gr, fq)
            fq = linked * roll(-gr * (b00 * alpha - b10 * eps) * inv, 1, 0)
        kk[2] = fq

        def terms(d, fq):
            alpha, eps, gl, gr = [chain[4 * d + c] for c in range(4)]
            b00, b10, inv = elimination(alpha, eps, gl, gr, fq)
            a01, a11 = gr * eps, 1.0 + gr * alpha
            base = 3 + 8 * d
            kk[base] = b00 * inv
            kk[base + 1] = -b10 * inv
            kk[base + 2] = a11 * inv
            kk[base + 3] = -a01 * inv
            kk[base + 4] = gl * (a11 * alpha - a01 * eps) * inv
            kk[base + 5] = -gr * (b00 * alpha - b10 * eps) * inv
            kk[base + 6] = gl * (b00 * eps - b10 * alpha) * inv
            kk[base + 7] = gr * eps * inv

        terms(0, kk[1])
        terms(1, kk[2])
        both_l = lane32 + 0 * p256
        j_of = jnp.where((grp & 1) == 0, both_l, E - 1 - both_l)
        chain[8] = column(r1, j_of)
        chain[9] = column(r0, both_l)
        chain[10] = column(r0, E - 1 - both_l)
        local.wait()
        got = pltpu.make_async_remote_copy(
            land1.at[pl.ds(0, 8 * (N - 1))], land1.at[pl.ds(0, 8 * (N - 1))], ss1, rs1,
            device_id=(me,), device_id_type=MESH,
        )
        got.wait_recv()

        def ordered_rows(kind, which):
            return pick(perm[which], land1[pl.ds(kind, N, stride=8), :]) + pick(
                perm[which + 1], land1[pl.ds(4 + kind, N, stride=8), :]
            )

        link_next = roll(kk[0], -1, 0)
        ya = ordered_rows(0, 0) + ordered_rows(2, 2)
        yb = ordered_rows(1, 0)
        yd = ordered_rows(3, 0)
        bl = kk[0] * roll(yb, 1, 0)
        bu = link_next * roll(yb, -1, 0)
        out2 = jnp.where(lane < 32, bl, jnp.where(lane < 64, bu, 0.0)) + yd
        straight = jnp.where(lane < 96, bl, bu)
        crossed = jnp.where(lane < 96, roll(bu, -32), roll(bl, 32))
        ya = ya + jnp.where(lane >= 64, chain[4] * straight + chain[5] * crossed, 0.0)
        ya = ya + jnp.where(lane == 0, roll(bl, 64), 0.0) + jnp.where(lane == 32, roll(bl, 65), 0.0)
        ya = ya + jnp.where(lane == 31, roll(bu, 63), 0.0) + jnp.where(lane == 63, roll(bu, 64), 0.0)

        def before_x(v, n):
            return jnp.concatenate([jnp.zeros((8 * n, N), F32), v[0 : 256 - 8 * n]], 0)

        def after_x(v, n):
            return jnp.concatenate([v[8 * n : 256], jnp.zeros((8 * n, N), F32)], 0)

        def before_y(v, n):
            return roll(v, n, 0)

        def after_y(v, n):
            return roll(v, -n, 0)

        def chains(y0, y1, d, gl, gr, before, after, steps):
            base = 3 + 8 * d
            e1 = kk[base] * y1 + kk[base + 1] * y0
            slope = kk[base + 6]
            for n in steps:
                e1 = e1 + slope * before(e1, n)
                slope = slope * before(slope, n)
            e0 = kk[base + 2] * y0 + kk[base + 3] * y1 + kk[base + 4] * before(e1, 1)
            slope = kk[base + 7]
            zp = e0
            for n in steps:
                zp = zp + slope * after(zp, n)
                slope = slope * after(slope, n)
            zp_next = after(zp, 1)
            zq = e1 + -kk[base + 5] * zp_next
            return -gl * (zp - before(zq, 1)), -gr * (zq - zp_next)

        al, ar = chains(
            ya, roll(ya, -32), 0, chain[2], chain[3], before_x, after_x, (1, 2, 4, 8, 16)
        )
        spread = jnp.where(
            lane < 64,
            jnp.where(lane < 32, al, roll(al, 32)),
            jnp.where(lane < 96, roll(ar, 64), roll(ar, 96)),
        )
        src = iota((N, 2 * N), 0) >> 5
        dst = iota((N, 2 * N), 1)
        side, part = dst >> 7, (dst >> 5) & 3
        sums = pick_right(
            spread * chain[8], one_hot((part >= 2) & (src == 2 * side + part - 2))
        )
        ya = ya + chain[9] * sums[:, 0:N] + chain[10] * sums[:, N : 2 * N]
        bl_c, br_c = chains(ya, roll(ya, -32), 1, chain[6], chain[7], before_y, after_y, (1, 2, 4))
        out1 = jnp.where(
            lane < 64,
            jnp.where(lane < 32, al, roll(ar, 32)),
            jnp.where(lane < 96, bl_c, roll(br_c, 32)),
        )
        for b in range(2):
            for kind, which, what in ((0, b, out1), (1, b, out2), (2, 2 + b, out1), (3, 2 + b, out2)):
                send2[pl.ds(b * 4 + kind, N, stride=8), :] = pick(permt[which], what)

        def send_back(step, carry):
            to = (me + step) & (N - 1)
            pltpu.make_async_remote_copy(
                block(send2, to), block(land2, mine), ss2, rs2, device_id=(to,), device_id_type=MESH
            ).start()
            return carry

        lax.fori_loop(1, N, send_back, 0)
        local = pltpu.make_async_copy(block(send2, me), block(land2, mine), own_sem.at[2])
        local.start()
        local.wait()

    def arrived2(count):
        part = land2.at[pl.ds(0, 8 * count)]
        pltpu.make_async_remote_copy(
            part, part, ss2, rs2, device_id=(me,), device_id_type=MESH
        ).wait_recv()

    @pl.when(owner)
    def _():
        arrived2(OWNERS - 1)

    @pl.when(jnp.logical_not(owner))
    def _():
        arrived2(OWNERS)

    def gathered(kind):
        return jnp.concatenate(
            [land2[pl.ds((q % 2) * 8 + (q // 2) * 4 + kind, E, stride=16), :] for q in range(4)], 0
        )

    own_ab, own_h, near_ab, near_h = [gathered(kind) for kind in range(4)]
    ab = jnp.transpose(own_ab)
    halo = jnp.transpose(own_h)
    w_near = jnp.zeros((E, N), F32)
    t_near = jnp.zeros((E, N), F32)
    for q in range(4):
        part = near_h[q * E : (q + 1) * E]
        w_near = jnp.where(grp == q, roll(part, E * q - 64), w_near)
        t_near = jnp.where(grp == q, roll(part, E * q - 96), t_near)

    kz_own = jnp.where(up, E - 1 - lane32, lane32)
    kz_near = jnp.where(up, lane32, E - 1 - lane32)
    delta_z = w_near - s_z
    alpha_z = [corners(near_r[2][at : at + 1])[0] for at in (3, 2)]
    planes, outer = [], []
    for which, at, kz, rows_ab, rows_h, wplane in (
        (0, 3, kz_own, own_ab, own_h, delta_z),
        (1, 2, kz_near, near_ab, near_h, -delta_z),
    ):
        weights = jnp.where(sub8 == grp, column(near_r[2][at : at + 1], kz), 0.0)
        ca = dot(weights, rows_ab)
        ch = dot(weights, rows_h)
        first_row = jnp.zeros((1, N), F32)
        last_row = jnp.zeros((1, N), F32)
        for q in range(4):
            first_row = jnp.where(grp == q, roll(ca[q : q + 1], E * q), first_row)
            last_row = jnp.where(grp == q, roll(ca[q : q + 1], E * q - E), last_row)
        mark = jnp.concatenate(
            [
                jnp.where((sub8 == grp) & (lane32 == 0), 1.0, 0.0),
                jnp.where((sub8 == grp) & (lane32 == E - 1), 1.0, 0.0),
            ],
            1,
        )
        marked = dot_first(ch, mark)
        plane = marked[0:E, 0:N] + marked[E : 2 * E, N : 2 * N] + alpha_z[which] * wplane
        plane = plane + jnp.where(row32 == 0, first_row, 0.0)
        plane = plane + jnp.where(row32 == E - 1, last_row, 0.0)
        pl_ref[which] = plane
        cols = jnp.concatenate(
            [
                jnp.where(sub8 == grp, column(near_r[1][at : at + 1], lane32), 0.0),
                jnp.where(sub8 == grp, column(near_r[1][at : at + 1], E - 1 - lane32), 0.0),
            ],
            1,
        )
        sides = dot_first(ca, cols)
        outer.append(sides[64:96, 0:N] + sides[96:128, N : 2 * N])

    halo_low, halo_up = halo[0:E], halo[E : 2 * E]
    f_ref[0:E, :] = f_ref[0:E, :] + halo_low
    f_ref[(E - 1) * E : E * E, :] = f_ref[(E - 1) * E : E * E, :] + halo_up
    at = pl.ds(0, E, stride=E)
    f_ref[at, :] = f_ref[at, :] + ab[0:E]
    at = pl.ds(E - 1, E, stride=E)
    f_ref[at, :] = f_ref[at, :] + ab[E : 2 * E]

    def on_face(plane, j):
        first = roll(plane, N - j)
        last = roll(plane, (N + E - 1 - j) & (N - 1))
        return jnp.where(face_lane, jnp.where(up, last, first), 0.0)

    def z_halo(t, carry):
        for m in range(4):
            j = t * 4 + m
            at = pl.ds(pl.multiple_of(j * E, E), E)
            f_ref[at, :] = f_ref[at, :] + on_face(delta_z, j)
        return carry

    lax.fori_loop(0, E // 4, z_halo, 0)

    def last_rows(i):
        x = jnp.where(sub8 == 3, pl_ref[0, pl.ds(i, 1), :], 0.0)
        return jnp.where(sub8 == 2, pl_ref[1, pl.ds(i, 1), :], x)

    solve_i(last_rows)
    ends_z = []
    for which, at in ((0, 3), (1, 2)):
        blocks = inverse_blocks(near_r[1][at : at + 1])
        ends_z.append(dot(e_ref[:, at, :], blocks) + outer[which])
    sigma = ends_z[0] + t_own
    tau = ends_z[1] + t_near
    c_plane = -gz * (sigma - tau) / (1.0 + gz * (alpha_z[0] + alpha_z[1]))

    solve_j(ab[64:96], ab[96:128])
    zblocks = packed_weights(inverse_blocks(own[2]))

    def finish(t, carry):
        d2 = []
        for m in range(8):
            at = pl.ds(pl.multiple_of((t * 8 + m) * E, E), E)
            d2.append(g_ref[at, :] + on_face(c_plane, t * 8 + m))
        d3 = packed_dot(jnp.concatenate(d2, 0), zblocks)
        d3 = d3 + u_ref[pl.ds(pl.multiple_of(t * 8 * E, 8 * E), 8 * E), :]
        for half in range(2):
            outs = swap_blocks(
                [d3[(half * 4 + m) * E : (half * 4 + m + 1) * E] for m in range(4)], grp
            )
            cols = pl.ds(pl.multiple_of((t * 2 + half) * N, N), N)
            for b in range(2):
                out_c[b, :, cols] = outs[2 * b]
                out_b[b, :, cols] = outs[2 * b + 1]
        return carry

    lax.fori_loop(0, 4, finish, 0)

    arrive.wait_send()

    def left1(count):
        part = send1.at[pl.ds(0, 8 * count)]
        pltpu.make_async_remote_copy(
            part, part, ss1, rs1, device_id=(me,), device_id_type=MESH
        ).wait_send()

    @pl.when(owner)
    def _():
        left1(OWNERS - 1)
        part = send2.at[pl.ds(0, 8 * (N - 1))]
        pltpu.make_async_remote_copy(
            part, part, ss2, rs2, device_id=(me,), device_id_type=MESH
        ).wait_send()

    @pl.when(jnp.logical_not(owner))
    def _():
        left1(OWNERS)


def body(calcium, buffer, fraction, rates, inverses, neighbors, ranks):
    vmem = pl.BlockSpec(memory_space=pltpu.VMEM)
    smem = pl.BlockSpec(memory_space=pltpu.SMEM)
    shape = jax.ShapeDtypeStruct(calcium.shape, F32)
    field = pltpu.VMEM((E * E, N), F32)
    return pl.pallas_call(
        step_kernel,
        out_shape=(shape, shape),
        in_specs=[smem, smem, vmem, vmem, vmem, vmem, vmem],
        out_specs=(vmem, vmem),
        scratch_shapes=[
            field,
            field,
            field,
            field,
            pltpu.VMEM((1, 1, N), F32),
            pltpu.VMEM((N, 1, N), F32),
            pltpu.VMEM((8 * OWNERS, N), F32),
            pltpu.VMEM((8 * N, N), F32),
            pltpu.VMEM((8 * N, N), F32),
            pltpu.VMEM((8 * OWNERS, N), F32),
            pltpu.VMEM((3, E, N), F32),
            pltpu.VMEM((3, E, N), F32),
            pltpu.VMEM((E, 8, N), F32),
            pltpu.VMEM((E, 8, N), F32),
            pltpu.VMEM((E, 8, N), F32),
            pltpu.VMEM((3, E, N), F32),
            pltpu.VMEM((4, 256, N), BF16),
            pltpu.VMEM((4, N, 256), BF16),
            pltpu.VMEM((19, 256, N), F32),
            pltpu.VMEM((11, 256, N), F32),
        ]
        + [pltpu.SemaphoreType.DMA] * 6
        + [pltpu.SemaphoreType.DMA((3,))],
        compiler_params=pltpu.CompilerParams(
            collective_id=0, has_side_effects=True, vmem_limit_bytes=60 * 1024 * 1024
        ),
    )(jnp.transpose(rates, (0, 2, 1)), neighbors, neighbors, ranks, calcium, buffer, fraction)


def solution(mesh):
    in_specs = (
        P("bricks", None, None),
        P("bricks", None, None),
        P("bricks", None, None),
        P("bricks", None, None),
        P("bricks", None, None, None, None),
        P(),
        P(),
    )
    out_specs = (P("bricks", None, None), P("bricks", None, None))
    return jax.shard_map(body, mesh=mesh, in_specs=in_specs, out_specs=out_specs, check_vma=False)
```

```python
import jax
import jax.numpy as jnp
from jax import lax
from jax.experimental import pallas as pl
from jax.experimental.pallas import tpu as pltpu
from jax.sharding import PartitionSpec as P

KON = 0.5
KOFF = 0.3
BTOT = 2.0
INFLUX = 0.1

MESH = pl.DeviceIdType.MESH
F32 = jnp.float32
BF16 = jnp.bfloat16
HIGH = lax.Precision.HIGHEST
N = 128
E = 32
OWNERS = 64


def iota(shape, axis):
    return lax.broadcasted_iota(jnp.int32, shape, axis)


def roll(x, shift, axis=-1):
    if axis < 0:
        axis += x.ndim
    if isinstance(shift, int):
        shift %= x.shape[axis]
        if shift == 0:
            return x
    return pltpu.roll(x, shift, axis)


def rho_of(r):
    h = 0.5 / r
    s = jnp.sqrt(h * (2.0 + h))
    return 1.0 + h - s, s - h


def power(log_rho, n):
    return jnp.exp(log_rho * n.astype(F32))


def corners(r):
    rho, gap = rho_of(r)
    p2 = rho * rho
    p4 = p2 * p2
    p8 = p4 * p4
    p16 = p8 * p8
    p32 = p16 * p16
    kappa = rho / (r * gap * (1.0 - p32 * p32))
    return kappa * (1.0 + p32 * p32 / rho), kappa * (p32 / rho + p32)


def column(r, index):
    rho, gap = rho_of(r)
    lr = jnp.log(rho)
    kappa = rho / (r * gap * (1.0 - jnp.exp(lr * 64.0)))
    return kappa * (power(lr, index) + power(lr, 63 - index))


def inverse_blocks(r):
    rho, gap = rho_of(r)
    lr = jnp.log(rho)
    scale = rho / (r * gap * (1.0 + rho) * (1.0 - jnp.exp(lr * 64.0)))
    row, col = iota((N, N), 0), iota((N, N), 1)
    a, b = row & 31, col & 31
    away = jnp.abs(a - b)
    total = power(lr, away) + power(lr, a + b + 1) + power(lr, 63 - a - b) + power(lr, 64 - away)
    return jnp.where((row >> 5) == (col >> 5), total * scale, 0.0)


def sweep_terms(r, index):
    rho, _ = rho_of(r)
    lr = jnp.log(rho)
    rho2 = rho * rho
    odd = power(lr, 2 * index + 1)
    ratio = rho * (1.0 + odd) / (1.0 + odd * rho2)
    last = jnp.exp(lr * 61.0)
    ratio30 = rho * (1.0 + last) / (1.0 + last * rho2)
    m = jnp.where(index == E - 1, 1.0 / (1.0 + r - r * ratio30), ratio / r)
    return m, m * r


def swap_blocks(x, grp):
    low = grp < 2
    even = (grp & 1) == 0
    y = [None] * 4
    for q in range(2):
        a, b = x[q], x[q + 2]
        y[q] = jnp.where(low, a, roll(b, 64))
        y[q + 2] = jnp.where(low, roll(a, 64), b)
    z = [None] * 4
    for q in (0, 2):
        a, b = y[q], y[q + 1]
        z[q] = jnp.where(even, a, roll(b, 32))
        z[q + 1] = jnp.where(even, roll(a, -32), b)
    return z


def split3(x):
    a = x.astype(BF16)
    rest = x - a.astype(F32)
    b = rest.astype(BF16)
    c = (rest - b.astype(F32)).astype(BF16)
    return a, b, c


def pick(select, x):
    out = None
    for part in split3(x):
        term = jnp.dot(select, part, preferred_element_type=F32)
        out = term if out is None else out + term
    return out


def pick_right(x, select):
    out = None
    for part in split3(x):
        term = jnp.dot(part, select, preferred_element_type=F32)
        out = term if out is None else out + term
    return out


def split2(x):
    a = x.astype(BF16)
    return a, (x - a.astype(F32)).astype(BF16)


def contract(a, b, dims):
    ah, al = split2(a)
    bh, bl = split2(b)
    dims = (dims, ((), ()))
    out = lax.dot_general(ah, bh, dims, preferred_element_type=F32)
    out = out + lax.dot_general(al, bh, dims, preferred_element_type=F32)
    return out + lax.dot_general(ah, bl, dims, preferred_element_type=F32)


def dot(a, b):
    return contract(a, b, ((1,), (0,)))


def dot_first(a, b):
    return contract(a, b, ((0,), (0,)))


def dot_last(a, b):
    return contract(a, b, ((1,), (1,)))


def packed_weights(w):
    h, l = split2(w)
    return jnp.concatenate(
        [jnp.concatenate([h, l], 1), jnp.concatenate([h, jnp.zeros_like(h)], 1)], 0
    )


def packed_dot(x, weights):
    out = jnp.dot(jnp.concatenate(split2(x), 1), weights, preferred_element_type=F32)
    return out[:, 0:N] + out[:, N : 2 * N]


def one_hot(cond):
    return jnp.where(cond, 1.0, 0.0).astype(BF16)


def total(x, axis):
    return jnp.sum(x, axis=axis, keepdims=True)


def step_kernel(
    rates, nbs, nbv, rkv, cal, buf, frac, out_c, out_b,
    u_ref, f_ref, t_ref, g_ref, rt, send1, land1, send2, land2,
    co0, co1, ecm, ece, e_ref, pl_ref, perm, permt, kk, chain,
    ss0, rs0, ss1, rs1, ss2, rs2, own_sem,
):
    me = lax.axis_index("bricks")
    barrier = pltpu.get_barrier_semaphore()

    stages = [(1, [me ^ t for t in range(1, 8)]), (8, [me ^ (8 * t) for t in range(1, 16)])]
    greeted = [to for _, group in stages for to in group]
    for to in greeted:
        pl.semaphore_signal(barrier, inc=1, device_id=(to,), device_id_type=MESH)

    lane = iota((1, N), 1)
    lane32 = lane & 31
    grp = lane >> 5
    sub8 = iota((8, N), 0)
    row32 = iota((E, N), 0)

    own = []
    for d in range(3):
        r = jnp.zeros((1, N), F32)
        for q in range(4):
            r = jnp.where(grp == q, rates[q // 2, q % 2, d], r)
        own.append(r)
    message = jnp.where(lane32 == 0, own[0], jnp.where(lane32 == 1, own[1], own[2]))
    rt[me] = message
    near = {}
    for name, d, side in (("yl", 1, 0), ("yu", 1, 1), ("zl", 2, 0), ("zu", 2, 1)):
        near[name] = [nbs[d, side, 2 * me + b] for b in range(2)]
    near["z"] = [jnp.maximum(near["zl"][b], near["zu"][b]) for b in range(2)]

    def by_brick(pair):
        return jnp.where(lane < 64, pair[0], pair[1])

    up = by_brick([jnp.where(v >= 0, 1, 0) for v in near["zu"]]) == 1
    upf = jnp.where(up, 1.0, 0.0)
    face_lane = lane32 == jnp.where(up, E - 1, 0)

    def lay(t, carry):
        cols = pl.ds(pl.multiple_of(t * N, N), N)
        us, fs = [], []
        for b in range(2):
            ca, bo, al = cal[b, :, cols], buf[b, :, cols], frac[b, :, cols]
            bind = KON * ca * (BTOT - bo) - KOFF * bo
            us += [ca, bo]
            fs += [2.0 * ca - bind + INFLUX * (1.0 - al) / al, 2.0 * bo + bind]
        us = swap_blocks(us, grp)
        fs = swap_blocks(fs, grp)
        for m in range(4):
            at = pl.ds(pl.multiple_of((t * 4 + m) * E, E), E)
            u_ref[at, :] = us[m]
            f_ref[at, :] = fs[m]
        return carry

    lax.fori_loop(0, 8, lay, 0)

    for co, r in ((co0, own[0]), (co1, own[1])):
        m, e = sweep_terms(r, row32)
        co[0] = m
        co[1] = e
        co[2] = jnp.where(row32 == E - 1, 0.0, e)

    pl.semaphore_wait(barrier, len(greeted))

    def rates_block(unit):
        return rt.at[pl.ds(me & (N - unit), unit)]

    def gather_start(at):
        unit, group = stages[at]
        for to in group:
            pltpu.make_async_remote_copy(
                rates_block(unit), rates_block(unit), ss0.at[at], rs0.at[at],
                device_id=(to,), device_id_type=MESH,
            ).start()

    def gather_all(at):
        unit, group = stages[at]
        part = rt.at[pl.ds(0, unit * len(group))]
        return pltpu.make_async_remote_copy(
            part, part, ss0.at[at], rs0.at[at], device_id=(me,), device_id_type=MESH
        )

    gather_start(0)

    def face(j, plane):
        u = u_ref[pl.ds(pl.multiple_of(j * E, E), E), :]
        first = roll(u, j)
        last = roll(u, j + (N - E + 1))
        return jnp.where(lane32 == j, jnp.where(up, last, first), plane)

    wz = lax.fori_loop(0, E, face, jnp.zeros((E, N), F32))

    gather_all(0).wait_recv()
    gather_start(1)

    owner = (me & 1) == 0

    @pl.when(owner)
    def _():
        s2, l2 = iota((256, 256), 0), iota((256, 256), 1)
        lane256 = iota((1, 256), 1)

        def heads(before, doublings):
            target = jnp.where(before < 0, lane256, before)
            step = one_hot(s2 == target)
            for _ in range(doublings):
                step = jnp.dot(step, step, preferred_element_type=F32).astype(BF16)
            return step

        before0, before1 = nbv[0, 0:1, :], nbv[1, 0:1, :]
        znear = jnp.maximum(nbv[2, 0:1, :], nbv[2, 1:2, :]).astype(F32)
        rank0, rank1 = rkv[0:1, :].astype(F32), rkv[1:2, :].astype(F32)
        lead = jnp.dot(heads(before1, 3), heads(before0, 5), preferred_element_type=F32)
        key = total(lead * s2.astype(F32), 0) * 32.0 + rank1
        keyed = total(jnp.where(s2 == l2, key + rank0 * 1e5, 0.0), 1)
        row = total(jnp.where(keyed < key, 1.0, 0.0), 0)
        pos = rank0 * 8.0 + row
        at = s2.astype(F32) == pos
        slot_at = total(jnp.where(at, lane256.astype(F32), 0.0), 1)
        rank_at = total(jnp.where(at, rank1, 0.0), 1)
        z_at = total(jnp.where(at, znear, 0.0), 1)
        kk[0] = jnp.where(rank_at > 0.5, 1.0, jnp.zeros((256, N), F32))
        dev = lane.astype(F32) * 2.0
        s1, l1 = iota((N, 256), 0), iota((N, 256), 1)
        lf = l1.astype(F32)
        for b in range(2):
            perm[b] = one_hot(slot_at == dev + b)
            perm[2 + b] = one_hot(z_at == dev + b)
            mine = l1 == 2 * s1 + b
            pos_b = total(jnp.where(mine, pos, 0.0), 1)
            z_b = total(jnp.where(mine, znear, 0.0), 1)
            posz_b = total(jnp.where(lf == z_b, pos + 1.0, 0.0), 1) - 1.0
            permt[b] = one_hot(lf == pos_b)
            permt[2 + b] = one_hot(lf == posz_b)

    cu2 = jnp.where(lane32 < E - 1, 2.0 * own[2], 0.0)
    cd2 = jnp.where(lane32 > 0, 2.0 * own[2], 0.0)
    dg2 = cu2 + cd2
    r1x2 = 2.0 * own[1]

    def right_side(t, prev):
        us = []
        for m in range(5):
            j = jnp.minimum(t * 4 + m, E - 1)
            us.append(u_ref[pl.ds(pl.multiple_of(j * E, E), E), :])
        for m in range(4):
            j = t * 4 + m
            at = pl.ds(pl.multiple_of(j * E, E), E)
            u = us[m]
            low = jnp.where(j == 0, 0.0, r1x2)
            high = jnp.where(j == E - 1, 0.0, r1x2)
            f_ref[at, :] = (
                f_ref[at, :]
                + cu2 * roll(u, -1)
                + cd2 * roll(u, 1)
                + low * prev
                + high * us[m + 1]
                - (dg2 + low + high) * u
            )
            prev = u
        return prev

    lax.fori_loop(0, E // 4, right_side, jnp.zeros((E, N), F32))

    def solve_i(load_plane_row):
        def forward(t, carry):
            g, h = carry
            for m in range(4):
                i = t * 4 + m
                at = pl.ds(i, E, stride=E)
                g = co0[0, pl.ds(i, 1), :] * f_ref[at, :] + co0[1, pl.ds(i, 1), :] * g
                t_ref[at, :] = g
                if load_plane_row is not None:
                    h = ecm[i] * load_plane_row(i) + ece[i] * h
                    e_ref[i] = h
            return g, h

        lax.fori_loop(0, E // 4, forward, (jnp.zeros((E, N), F32), jnp.zeros((8, N), F32)))

        def backward(t, carry):
            x, h = carry
            for m in range(4):
                i = E - 1 - t * 4 - m
                at = pl.ds(i, E, stride=E)
                x = t_ref[at, :] + co0[2, pl.ds(i, 1), :] * x
                t_ref[at, :] = x
                if load_plane_row is not None:
                    h = e_ref[i] + jnp.where(i == E - 1, 0.0, ece[i]) * h
                    e_ref[i] = h
            return x, h

        lax.fori_loop(0, E // 4, backward, (jnp.zeros((E, N), F32), jnp.zeros((8, N), F32)))

    def solve_j(extra_first, extra_last):
        def forward(t, g):
            for m in range(4):
                j = t * 4 + m
                at = pl.ds(pl.multiple_of(j * E, E), E)
                d = t_ref[at, :] - 2.0 * u_ref[at, :]
                if extra_first is not None and m == 0:
                    d = d + jnp.where(j == 0, extra_first, 0.0)
                if extra_last is not None and m == 3:
                    d = d + jnp.where(j == E - 1, extra_last, 0.0)
                g = co1[0, pl.ds(j, 1), :] * d + co1[1, pl.ds(j, 1), :] * g
                g_ref[at, :] = g
            return g

        lax.fori_loop(0, E // 4, forward, jnp.zeros((E, N), F32))

        def backward(t, x):
            for m in range(4):
                j = E - 1 - t * 4 - m
                at = pl.ds(pl.multiple_of(j * E, E), E)
                x = g_ref[at, :] + co1[2, pl.ds(j, 1), :] * x
                g_ref[at, :] = x
            return x

        lax.fori_loop(0, E // 4, backward, jnp.zeros((E, N), F32))

    solve_i(None)
    solve_j(None, None)

    rowN, colN = iota((N, N), 0), iota((N, N), 1)
    kin = rowN & 31
    weight = column(own[2], jnp.where(up, E - 1 - kin, kin))
    weight = packed_weights(jnp.where((rowN >> 5) == (colN >> 5), weight, 0.0))

    def face_mean(t, plane):
        y = packed_dot(g_ref[pl.ds(pl.multiple_of(t * 8 * E, 8 * E), 8 * E), :], weight)
        for m in range(8):
            plane = jnp.where(lane32 == t * 8 + m, y[m * E : (m + 1) * E], plane)
        return plane

    t_own = lax.fori_loop(0, 4, face_mean, jnp.zeros((E, N), F32))

    gather_all(1).wait_recv()

    def rates_of(indices):
        rows = []
        for b in range(2):
            index = jnp.maximum(indices[b], 0)
            got = rt[index >> 1]
            cross = (index & 1) != b
            rows.append(jnp.where(cross, roll(got, 64), got))
        got = jnp.where(lane < 64, rows[0], rows[1])
        has = by_brick([jnp.where(indices[b] >= 0, 1.0, 0.0) for b in range(2)])
        return got, has

    stack = jnp.ones((8, N), F32)
    has = jnp.zeros((8, N), F32)
    for at, name in ((0, "yu"), (1, "yl"), (2, "z")):
        got, there = rates_of(near[name])
        stack = jnp.where(sub8 == at, got, stack)
        has = jnp.where(sub8 == at, there, has)
    stack = jnp.where((sub8 >= 3) & (sub8 < 6), message, stack)
    near_r = []
    for d in range(3):
        x = roll(jnp.where(lane32 == d, stack, 0.0), -d)
        for shift in (1, 2, 4, 8, 16):
            x = x + roll(x, shift)
        near_r.append(x)
    g1 = has * 2.0 * own[1] * near_r[1] / (own[1] + near_r[1])
    g2 = has * 2.0 * own[2] * near_r[2] / (own[2] + near_r[2])
    gyu, gyl, gz = g1[0:1], g1[1:2], g2[2:3]

    u_first, u_last = u_ref[0:E, :], u_ref[(E - 1) * E : E * E, :]
    s_up = 2.0 * gyu * u_last
    s_low = 2.0 * gyl * u_first
    s_z = 2.0 * gz * wz
    i8 = iota((E, 8, N), 0)
    mm, ee = sweep_terms(near_r[0][None], i8)
    ecm[...] = mm
    ece[...] = ee
    pl_ref[0] = s_up
    pl_ref[1] = s_low
    pl_ref[2] = s_z

    h = jnp.zeros((8, N), F32)
    for i in range(E):
        x_up, x_low, x_z = [pl_ref[p, i : i + 1, :] for p in range(3)]
        x = jnp.where(sub8 == 0, x_up, jnp.where(sub8 == 1, x_low, x_z))
        x = jnp.where(sub8 == 3, -x_z, jnp.where(sub8 == 4, -x_low, jnp.where(sub8 == 5, -x_up, x)))
        h = ecm[i] * x + ece[i] * h
        e_ref[i] = h
    for i in range(E - 2, -1, -1):
        h = e_ref[i] + ece[i] * h
        e_ref[i] = h
    p_up, p_low, p_z, p_out, p_first, p_last = [e_ref[:, p, :] for p in range(6)]

    alpha_1, eps_1 = corners(own[1])
    out_first = jnp.where(row32 == 0, 1.0, 0.0)
    out_last = jnp.where(row32 == E - 1, 1.0, 0.0)
    y0f = t_ref[pl.ds(0, E, stride=E), :] + out_first * p_first[0:1] + out_last * p_last[0:1]
    y0l = (
        t_ref[pl.ds(E - 1, E, stride=E), :]
        + out_first * p_first[E - 1 : E]
        + out_last * p_last[E - 1 : E]
    )
    y1f = g_ref[0:E, :] + alpha_1 * p_first + eps_1 * p_last
    y1l = g_ref[(E - 1) * E : E * E, :] + eps_1 * p_first + alpha_1 * p_last
    rows_a = jnp.transpose(jnp.concatenate([y0f, y0l, y1f, y1l], 0))
    rows_b = jnp.transpose(jnp.concatenate([s_up, s_low, p_up, p_low], 0))
    group8 = (sub8 & 3) == grp
    ends_i = []
    for p, at in ((p_z, 2), (p_out, 3)):
        r1 = near_r[1][at : at + 1]
        ends = jnp.where(sub8 < 4, column(r1, lane32), column(r1, E - 1 - lane32))
        x = dot_last(jnp.where(group8, ends, 0.0), p)
        ends_i.append(jnp.concatenate([x, jnp.zeros((8, N - E), F32)], 1))

    def end_row(p, x, q):
        c = jnp.where(lane < 32, roll(p[0:1], -E * q), roll(p[E - 1 : E], E - E * q))
        c = jnp.where(lane < 64, c, roll(x[q : q + 1], 64))
        return jnp.where(lane < 96, c, roll(x[q + 4 : q + 5], 96))

    for q in range(4):
        b, sp = q // 2, q % 2
        base = sp * 8 + b * 4
        mine_up = near["zu"][b] >= 0
        kf = jnp.where(mine_up, E - 1, 0)
        kn = jnp.where(mine_up, 0, E - 1)
        part_a, part_b = rows_a[q * E : (q + 1) * E], rows_b[q * E : (q + 1) * E]
        send1[pl.ds(base, E, stride=16), :] = part_a + jnp.where(
            row32 == kf, end_row(p_out, ends_i[1], q), 0.0
        )
        send1[pl.ds(base + 1, E, stride=16), :] = part_b
        send1[pl.ds(base + 2, E, stride=16), :] = jnp.where(
            row32 == kn, end_row(p_z, ends_i[0], q), 0.0
        )
        out = jnp.where(lane < 32, -roll(part_b, -E), -roll(part_b, E))
        zt = jnp.where(lane < 96, roll(s_z, 64 - E * q), roll(t_own, 96 - E * q))
        send1[pl.ds(base + 3, E, stride=16), :] = jnp.where(lane < 64, out, zt)

    mine = me >> 1

    def block(ref, index):
        return ref.at[pl.ds(pl.multiple_of(index * 8, 8), 8)]

    mine = me >> 1

    def send_ends(step, carry):
        o = (mine + step) & (OWNERS - 1)
        pltpu.make_async_remote_copy(
            block(send1, o), block(land1, me), ss1, rs1, device_id=(2 * o,), device_id_type=MESH
        ).start()
        return carry

    lax.fori_loop(1, OWNERS, send_ends, 0)

    @pl.when(jnp.logical_not(owner))
    def _():
        pltpu.make_async_remote_copy(
            block(send1, mine), block(land1, me), ss1, rs1, device_id=(2 * mine,), device_id_type=MESH
        ).start()

    @pl.when(owner)
    def _():
        local = pltpu.make_async_copy(block(send1, mine), block(land1, me), own_sem.at[0])
        local.start()
        sp32 = (mine & 1) * 32
        table = rt[:, 0, :]
        ordered = pick(perm[0], table) + pick(perm[1], roll(table, 64))
        pick_at = iota((N, 2 * N), 0)
        pick_to = iota((N, 2 * N), 1) >> 7
        both = pick_right(ordered, one_hot(pick_at == sp32 + pick_to))
        r0, r1 = both[:, 0:N], both[:, N : 2 * N]
        p256 = iota((256, N), 0)
        linked = kk[0]
        dims = []
        for d, r in ((0, r0), (1, r1)):
            alpha, eps = corners(r)
            if d == 0:
                before = jnp.concatenate([r[0:8], r[0:248]], 0)
                gl = jnp.where(p256 >= 8, 2.0 * r * before / (r + before), 0.0)
                gr = jnp.concatenate([gl[8:256], jnp.zeros((8, N), F32)], 0)
            else:
                before = roll(r, 1, 0)
                gl = linked * 2.0 * r * before / (r + before)
                gr = roll(gl, -1, 0)
            dims.append((alpha, eps, gl, gr))
            chain[0 + 4 * d] = alpha
            chain[1 + 4 * d] = eps
            chain[2 + 4 * d] = gl
            chain[3 + 4 * d] = gr

        def elimination(alpha, eps, gl, gr, fq):
            b00 = 1.0 + gl * alpha * (1.0 + fq)
            b10 = gl * eps * (1.0 + fq)
            det = b00 * (1.0 + gr * alpha) - gr * eps * b10
            return b00, b10, 1.0 / det

        def along(x, fq):
            at = pl.ds(pl.multiple_of(x * 8, 8), 8)
            alpha, eps, gl, gr = [chain[c, at, :] for c in range(4)]
            kk[1, at, :] = fq
            b00, b10, inv = elimination(alpha, eps, gl, gr, fq)
            return -gr * (b00 * alpha - b10 * eps) * inv

        lax.fori_loop(0, E, along, jnp.zeros((8, N), F32))
        alpha, eps, gl, gr = dims[1]
        fq = jnp.zeros((256, N), F32)
        for _ in range(7):
            b00, b10, inv = elimination(alpha, eps, gl, gr, fq)
            fq = linked * roll(-gr * (b00 * alpha - b10 * eps) * inv, 1, 0)
        kk[2] = fq

        def terms(d, fq):
            alpha, eps, gl, gr = [chain[4 * d + c] for c in range(4)]
            b00, b10, inv = elimination(alpha, eps, gl, gr, fq)
            a01, a11 = gr * eps, 1.0 + gr * alpha
            base = 3 + 8 * d
            kk[base] = b00 * inv
            kk[base + 1] = -b10 * inv
            kk[base + 2] = a11 * inv
            kk[base + 3] = -a01 * inv
            kk[base + 4] = gl * (a11 * alpha - a01 * eps) * inv
            kk[base + 5] = -gr * (b00 * alpha - b10 * eps) * inv
            kk[base + 6] = gl * (b00 * eps - b10 * alpha) * inv
            kk[base + 7] = gr * eps * inv

        terms(0, kk[1])
        terms(1, kk[2])
        both_l = lane32 + 0 * p256
        j_of = jnp.where((grp & 1) == 0, both_l, E - 1 - both_l)
        chain[8] = column(r1, j_of)
        chain[9] = column(r0, both_l)
        chain[10] = column(r0, E - 1 - both_l)
        local.wait()
        got = pltpu.make_async_remote_copy(
            land1.at[pl.ds(0, 8 * (N - 1))], land1.at[pl.ds(0, 8 * (N - 1))], ss1, rs1,
            device_id=(me,), device_id_type=MESH,
        )
        got.wait_recv()

        def ordered_rows(kind, which):
            return pick(perm[which], land1[pl.ds(kind, N, stride=8), :]) + pick(
                perm[which + 1], land1[pl.ds(4 + kind, N, stride=8), :]
            )

        link_next = roll(kk[0], -1, 0)
        ya = ordered_rows(0, 0) + ordered_rows(2, 2)
        yb = ordered_rows(1, 0)
        yd = ordered_rows(3, 0)
        bl = kk[0] * roll(yb, 1, 0)
        bu = link_next * roll(yb, -1, 0)
        out2 = jnp.where(lane < 32, bl, jnp.where(lane < 64, bu, 0.0)) + yd
        straight = jnp.where(lane < 96, bl, bu)
        crossed = jnp.where(lane < 96, roll(bu, -32), roll(bl, 32))
        ya = ya + jnp.where(lane >= 64, chain[4] * straight + chain[5] * crossed, 0.0)
        ya = ya + jnp.where(lane == 0, roll(bl, 64), 0.0) + jnp.where(lane == 32, roll(bl, 65), 0.0)
        ya = ya + jnp.where(lane == 31, roll(bu, 63), 0.0) + jnp.where(lane == 63, roll(bu, 64), 0.0)

        def before_x(v, n):
            return jnp.concatenate([jnp.zeros((8 * n, N), F32), v[0 : 256 - 8 * n]], 0)

        def after_x(v, n):
            return jnp.concatenate([v[8 * n : 256], jnp.zeros((8 * n, N), F32)], 0)

        def before_y(v, n):
            return roll(v, n, 0)

        def after_y(v, n):
            return roll(v, -n, 0)

        def chains(y0, y1, d, gl, gr, before, after, steps):
            base = 3 + 8 * d
            e1 = kk[base] * y1 + kk[base + 1] * y0
            slope = kk[base + 6]
            for n in steps:
                e1 = e1 + slope * before(e1, n)
                slope = slope * before(slope, n)
            e0 = kk[base + 2] * y0 + kk[base + 3] * y1 + kk[base + 4] * before(e1, 1)
            slope = kk[base + 7]
            zp = e0
            for n in steps:
                zp = zp + slope * after(zp, n)
                slope = slope * after(slope, n)
            zp_next = after(zp, 1)
            zq = e1 + -kk[base + 5] * zp_next
            return -gl * (zp - before(zq, 1)), -gr * (zq - zp_next)

        al, ar = chains(
            ya, roll(ya, -32), 0, chain[2], chain[3], before_x, after_x, (1, 2, 4, 8, 16)
        )
        spread = jnp.where(
            lane < 64,
            jnp.where(lane < 32, al, roll(al, 32)),
            jnp.where(lane < 96, roll(ar, 64), roll(ar, 96)),
        )
        src = iota((N, 2 * N), 0) >> 5
        dst = iota((N, 2 * N), 1)
        side, part = dst >> 7, (dst >> 5) & 3
        sums = pick_right(
            spread * chain[8], one_hot((part >= 2) & (src == 2 * side + part - 2))
        )
        ya = ya + chain[9] * sums[:, 0:N] + chain[10] * sums[:, N : 2 * N]
        bl_c, br_c = chains(ya, roll(ya, -32), 1, chain[6], chain[7], before_y, after_y, (1, 2, 4))
        out1 = jnp.where(
            lane < 64,
            jnp.where(lane < 32, al, roll(ar, 32)),
            jnp.where(lane < 96, bl_c, roll(br_c, 32)),
        )
        for b in range(2):
            for kind, which, what in ((0, b, out1), (1, b, out2), (2, 2 + b, out1), (3, 2 + b, out2)):
                send2[pl.ds(b * 4 + kind, N, stride=8), :] = pick(permt[which], what)

        def send_back(step, carry):
            to = (me + step) & (N - 1)
            pltpu.make_async_remote_copy(
                block(send2, to), block(land2, mine), ss2, rs2, device_id=(to,), device_id_type=MESH
            ).start()
            return carry

        lax.fori_loop(1, N, send_back, 0)
        local = pltpu.make_async_copy(block(send2, me), block(land2, mine), own_sem.at[1])
        local.start()
        local.wait()

    def arrived2(count):
        part = land2.at[pl.ds(0, 8 * count)]
        pltpu.make_async_remote_copy(
            part, part, ss2, rs2, device_id=(me,), device_id_type=MESH
        ).wait_recv()

    @pl.when(owner)
    def _():
        arrived2(OWNERS - 1)

    @pl.when(jnp.logical_not(owner))
    def _():
        arrived2(OWNERS)

    def gathered(kind):
        return jnp.concatenate(
            [land2[pl.ds((q % 2) * 8 + (q // 2) * 4 + kind, E, stride=16), :] for q in range(4)], 0
        )

    own_ab, own_h, near_ab, near_h = [gathered(kind) for kind in range(4)]
    ab = jnp.transpose(own_ab)
    halo = jnp.transpose(own_h)
    w_near = jnp.zeros((E, N), F32)
    t_near = jnp.zeros((E, N), F32)
    for q in range(4):
        part = near_h[q * E : (q + 1) * E]
        w_near = jnp.where(grp == q, roll(part, E * q - 64), w_near)
        t_near = jnp.where(grp == q, roll(part, E * q - 96), t_near)

    kz_own = jnp.where(up, E - 1 - lane32, lane32)
    kz_near = jnp.where(up, lane32, E - 1 - lane32)
    delta_z = w_near - s_z
    alpha_z = [corners(near_r[2][at : at + 1])[0] for at in (3, 2)]
    planes, outer = [], []
    for which, at, kz, rows_ab, rows_h, wplane in (
        (0, 3, kz_own, own_ab, own_h, delta_z),
        (1, 2, kz_near, near_ab, near_h, -delta_z),
    ):
        weights = jnp.where(sub8 == grp, column(near_r[2][at : at + 1], kz), 0.0)
        ca = dot(weights, rows_ab)
        ch = dot(weights, rows_h)
        first_row = jnp.zeros((1, N), F32)
        last_row = jnp.zeros((1, N), F32)
        for q in range(4):
            first_row = jnp.where(grp == q, roll(ca[q : q + 1], E * q), first_row)
            last_row = jnp.where(grp == q, roll(ca[q : q + 1], E * q - E), last_row)
        mark = jnp.concatenate(
            [
                jnp.where((sub8 == grp) & (lane32 == 0), 1.0, 0.0),
                jnp.where((sub8 == grp) & (lane32 == E - 1), 1.0, 0.0),
            ],
            1,
        )
        marked = dot_first(ch, mark)
        plane = marked[0:E, 0:N] + marked[E : 2 * E, N : 2 * N] + alpha_z[which] * wplane
        plane = plane + jnp.where(row32 == 0, first_row, 0.0)
        plane = plane + jnp.where(row32 == E - 1, last_row, 0.0)
        pl_ref[which] = plane
        cols = jnp.concatenate(
            [
                jnp.where(sub8 == grp, column(near_r[1][at : at + 1], lane32), 0.0),
                jnp.where(sub8 == grp, column(near_r[1][at : at + 1], E - 1 - lane32), 0.0),
            ],
            1,
        )
        sides = dot_first(ca, cols)
        outer.append(sides[64:96, 0:N] + sides[96:128, N : 2 * N])

    halo_low, halo_up = halo[0:E], halo[E : 2 * E]
    f_ref[0:E, :] = f_ref[0:E, :] + halo_low
    f_ref[(E - 1) * E : E * E, :] = f_ref[(E - 1) * E : E * E, :] + halo_up
    at = pl.ds(0, E, stride=E)
    f_ref[at, :] = f_ref[at, :] + ab[0:E]
    at = pl.ds(E - 1, E, stride=E)
    f_ref[at, :] = f_ref[at, :] + ab[E : 2 * E]

    def on_face(plane, j):
        first = roll(plane, N - j)
        last = roll(plane, (N + E - 1 - j) & (N - 1))
        return jnp.where(face_lane, jnp.where(up, last, first), 0.0)

    def z_halo(t, carry):
        for m in range(4):
            j = t * 4 + m
            at = pl.ds(pl.multiple_of(j * E, E), E)
            f_ref[at, :] = f_ref[at, :] + on_face(delta_z, j)
        return carry

    lax.fori_loop(0, E // 4, z_halo, 0)

    def last_rows(i):
        x = jnp.where(sub8 == 3, pl_ref[0, pl.ds(i, 1), :], 0.0)
        return jnp.where(sub8 == 2, pl_ref[1, pl.ds(i, 1), :], x)

    solve_i(last_rows)
    ends_z = []
    for which, at in ((0, 3), (1, 2)):
        blocks = inverse_blocks(near_r[1][at : at + 1])
        ends_z.append(dot(e_ref[:, at, :], blocks) + outer[which])
    sigma = ends_z[0] + t_own
    tau = ends_z[1] + t_near
    c_plane = -gz * (sigma - tau) / (1.0 + gz * (alpha_z[0] + alpha_z[1]))

    solve_j(ab[64:96], ab[96:128])
    zblocks = packed_weights(inverse_blocks(own[2]))

    def finish(t, carry):
        d2 = []
        for m in range(8):
            at = pl.ds(pl.multiple_of((t * 8 + m) * E, E), E)
            d2.append(g_ref[at, :] + on_face(c_plane, t * 8 + m))
        d3 = packed_dot(jnp.concatenate(d2, 0), zblocks)
        d3 = d3 + u_ref[pl.ds(pl.multiple_of(t * 8 * E, 8 * E), 8 * E), :]
        for half in range(2):
            outs = swap_blocks(
                [d3[(half * 4 + m) * E : (half * 4 + m + 1) * E] for m in range(4)], grp
            )
            cols = pl.ds(pl.multiple_of((t * 2 + half) * N, N), N)
            for b in range(2):
                out_c[b, :, cols] = outs[2 * b]
                out_b[b, :, cols] = outs[2 * b + 1]
        return carry

    lax.fori_loop(0, 4, finish, 0)

    for at in range(2):
        gather_all(at).wait_send()

    def left1(count):
        part = send1.at[pl.ds(0, 8 * count)]
        pltpu.make_async_remote_copy(
            part, part, ss1, rs1, device_id=(me,), device_id_type=MESH
        ).wait_send()

    @pl.when(owner)
    def _():
        left1(OWNERS - 1)
        part = send2.at[pl.ds(0, 8 * (N - 1))]
        pltpu.make_async_remote_copy(
            part, part, ss2, rs2, device_id=(me,), device_id_type=MESH
        ).wait_send()

    @pl.when(jnp.logical_not(owner))
    def _():
        left1(OWNERS)


def body(calcium, buffer, fraction, rates, inverses, neighbors, ranks):
    vmem = pl.BlockSpec(memory_space=pltpu.VMEM)
    smem = pl.BlockSpec(memory_space=pltpu.SMEM)
    shape = jax.ShapeDtypeStruct(calcium.shape, F32)
    field = pltpu.VMEM((E * E, N), F32)
    return pl.pallas_call(
        step_kernel,
        out_shape=(shape, shape),
        in_specs=[smem, smem, vmem, vmem, vmem, vmem, vmem],
        out_specs=(vmem, vmem),
        scratch_shapes=[
            field,
            field,
            field,
            field,
            pltpu.VMEM((N, 1, N), F32),
            pltpu.VMEM((8 * OWNERS, N), F32),
            pltpu.VMEM((8 * N, N), F32),
            pltpu.VMEM((8 * N, N), F32),
            pltpu.VMEM((8 * OWNERS, N), F32),
            pltpu.VMEM((3, E, N), F32),
            pltpu.VMEM((3, E, N), F32),
            pltpu.VMEM((E, 8, N), F32),
            pltpu.VMEM((E, 8, N), F32),
            pltpu.VMEM((E, 8, N), F32),
            pltpu.VMEM((3, E, N), F32),
            pltpu.VMEM((4, 256, N), BF16),
            pltpu.VMEM((4, N, 256), BF16),
            pltpu.VMEM((19, 256, N), F32),
            pltpu.VMEM((11, 256, N), F32),
        ]
        + [pltpu.SemaphoreType.DMA((2,))] * 2
        + [pltpu.SemaphoreType.DMA] * 4
        + [pltpu.SemaphoreType.DMA((2,))],
        compiler_params=pltpu.CompilerParams(
            collective_id=0, has_side_effects=True, vmem_limit_bytes=60 * 1024 * 1024
        ),
    )(jnp.transpose(rates, (0, 2, 1)), neighbors, neighbors, ranks, calcium, buffer, fraction)


def solution(mesh):
    in_specs = (
        P("bricks", None, None),
        P("bricks", None, None),
        P("bricks", None, None),
        P("bricks", None, None),
        P("bricks", None, None, None, None),
        P(),
        P(),
    )
    out_specs = (P("bricks", None, None), P("bricks", None, None))
    return jax.shard_map(body, mesh=mesh, in_specs=in_specs, out_specs=out_specs, check_vma=False)
```

```python
import jax
import jax.numpy as jnp
from jax import lax
from jax.experimental import pallas as pl
from jax.experimental.pallas import tpu as pltpu
from jax.sharding import PartitionSpec as P

KON = 0.5
KOFF = 0.3
BTOT = 2.0
INFLUX = 0.1

MESH = pl.DeviceIdType.MESH
F32 = jnp.float32
BF16 = jnp.bfloat16
HIGH = lax.Precision.HIGHEST
N = 128
E = 32
OWNERS = 64


def iota(shape, axis):
    return lax.broadcasted_iota(jnp.int32, shape, axis)


def roll(x, shift, axis=-1):
    if axis < 0:
        axis += x.ndim
    if isinstance(shift, int):
        shift %= x.shape[axis]
        if shift == 0:
            return x
    return pltpu.roll(x, shift, axis)


def rho_of(r):
    h = 0.5 / r
    s = jnp.sqrt(h * (2.0 + h))
    return 1.0 + h - s, s - h


def power(log_rho, n):
    return jnp.exp(log_rho * n.astype(F32))


def corners(r):
    rho, gap = rho_of(r)
    p2 = rho * rho
    p4 = p2 * p2
    p8 = p4 * p4
    p16 = p8 * p8
    p32 = p16 * p16
    kappa = rho / (r * gap * (1.0 - p32 * p32))
    return kappa * (1.0 + p32 * p32 / rho), kappa * (p32 / rho + p32)


def column(r, index):
    rho, gap = rho_of(r)
    lr = jnp.log(rho)
    kappa = rho / (r * gap * (1.0 - jnp.exp(lr * 64.0)))
    return kappa * (power(lr, index) + power(lr, 63 - index))


def inverse_blocks(r):
    rho, gap = rho_of(r)
    lr = jnp.log(rho)
    scale = rho / (r * gap * (1.0 + rho) * (1.0 - jnp.exp(lr * 64.0)))
    row, col = iota((N, N), 0), iota((N, N), 1)
    a, b = row & 31, col & 31
    away = jnp.abs(a - b)
    total = power(lr, away) + power(lr, a + b + 1) + power(lr, 63 - a - b) + power(lr, 64 - away)
    return jnp.where((row >> 5) == (col >> 5), total * scale, 0.0)


def sweep_terms(r, index):
    rho, _ = rho_of(r)
    lr = jnp.log(rho)
    rho2 = rho * rho
    odd = power(lr, 2 * index + 1)
    ratio = rho * (1.0 + odd) / (1.0 + odd * rho2)
    last = jnp.exp(lr * 61.0)
    ratio30 = rho * (1.0 + last) / (1.0 + last * rho2)
    m = jnp.where(index == E - 1, 1.0 / (1.0 + r - r * ratio30), ratio / r)
    return m, m * r


def swap_blocks(x, grp):
    low = grp < 2
    even = (grp & 1) == 0
    y = [None] * 4
    for q in range(2):
        a, b = x[q], x[q + 2]
        y[q] = jnp.where(low, a, roll(b, 64))
        y[q + 2] = jnp.where(low, roll(a, 64), b)
    z = [None] * 4
    for q in (0, 2):
        a, b = y[q], y[q + 1]
        z[q] = jnp.where(even, a, roll(b, 32))
        z[q + 1] = jnp.where(even, roll(a, -32), b)
    return z


def split3(x):
    a = x.astype(BF16)
    rest = x - a.astype(F32)
    b = rest.astype(BF16)
    c = (rest - b.astype(F32)).astype(BF16)
    return a, b, c


def pick(select, x):
    out = None
    for part in split3(x):
        term = jnp.dot(select, part, preferred_element_type=F32)
        out = term if out is None else out + term
    return out


def pick_right(x, select):
    out = None
    for part in split3(x):
        term = jnp.dot(part, select, preferred_element_type=F32)
        out = term if out is None else out + term
    return out


def split2(x):
    a = x.astype(BF16)
    return a, (x - a.astype(F32)).astype(BF16)


def contract(a, b, dims):
    ah, al = split2(a)
    bh, bl = split2(b)
    dims = (dims, ((), ()))
    out = lax.dot_general(ah, bh, dims, preferred_element_type=F32)
    out = out + lax.dot_general(al, bh, dims, preferred_element_type=F32)
    return out + lax.dot_general(ah, bl, dims, preferred_element_type=F32)


def dot(a, b):
    return contract(a, b, ((1,), (0,)))


def dot_first(a, b):
    return contract(a, b, ((0,), (0,)))


def dot_last(a, b):
    return contract(a, b, ((1,), (1,)))


def packed_weights(w):
    h, l = split2(w)
    return jnp.concatenate(
        [jnp.concatenate([h, l], 1), jnp.concatenate([h, jnp.zeros_like(h)], 1)], 0
    )


def packed_dot(x, weights):
    out = jnp.dot(jnp.concatenate(split2(x), 1), weights, preferred_element_type=F32)
    return out[:, 0:N] + out[:, N : 2 * N]


def one_hot(cond):
    return jnp.where(cond, 1.0, 0.0).astype(BF16)


def total(x, axis):
    return jnp.sum(x, axis=axis, keepdims=True)


def step_kernel(
    rates, nbs, nbv, rkv, cal, buf, frac, out_c, out_b,
    u_ref, f_ref, t_ref, g_ref, rt, send1b, land1b, send1c, land1c,
    send2a, land2a, send2b, land2b, blocks_1,
    co0, co1, ecm, ece, e_ref, pl_ref, ab_ref, perm, permt, kk, chain,
    ss0, rs0, ss1b, rs1b, ss1c, rs1c, ss2a, rs2a, ss2b, rs2b, own_sem,
):
    me = lax.axis_index("bricks")
    barrier = pltpu.get_barrier_semaphore()

    stages = [(1, [me ^ t for t in range(1, 8)]), (8, [me ^ (8 * t) for t in range(1, 16)])]
    greeted = [to for _, group in stages for to in group]
    for to in greeted:
        pl.semaphore_signal(barrier, inc=1, device_id=(to,), device_id_type=MESH)

    lane = iota((1, N), 1)
    lane32 = lane & 31
    grp = lane >> 5
    sub8 = iota((8, N), 0)
    row32 = iota((E, N), 0)

    own = []
    for d in range(3):
        r = jnp.zeros((1, N), F32)
        for q in range(4):
            r = jnp.where(grp == q, rates[q // 2, q % 2, d], r)
        own.append(r)
    message = jnp.where(lane32 == 0, own[0], jnp.where(lane32 == 1, own[1], own[2]))
    rt[me] = message
    near = {}
    for name, d, side in (("yl", 1, 0), ("yu", 1, 1), ("zl", 2, 0), ("zu", 2, 1)):
        near[name] = [nbs[d, side, 2 * me + b] for b in range(2)]
    near["z"] = [jnp.maximum(near["zl"][b], near["zu"][b]) for b in range(2)]

    def by_brick(pair):
        return jnp.where(lane < 64, pair[0], pair[1])

    up = by_brick([jnp.where(v >= 0, 1, 0) for v in near["zu"]]) == 1
    upf = jnp.where(up, 1.0, 0.0)
    face_lane = lane32 == jnp.where(up, E - 1, 0)

    def lay(t, carry):
        cols = pl.ds(pl.multiple_of(t * N, N), N)
        us, fs = [], []
        for b in range(2):
            ca, bo, al = cal[b, :, cols], buf[b, :, cols], frac[b, :, cols]
            bind = KON * ca * (BTOT - bo) - KOFF * bo
            us += [ca, bo]
            fs += [2.0 * ca - bind + INFLUX * (1.0 - al) / al, 2.0 * bo + bind]
        us = swap_blocks(us, grp)
        fs = swap_blocks(fs, grp)
        for m in range(4):
            at = pl.ds(pl.multiple_of((t * 4 + m) * E, E), E)
            u_ref[at, :] = us[m]
            f_ref[at, :] = fs[m]
        return carry

    lax.fori_loop(0, 8, lay, 0)

    for co, r in ((co0, own[0]), (co1, own[1])):
        m, e = sweep_terms(r, row32)
        co[0] = m
        co[1] = e
        co[2] = jnp.where(row32 == E - 1, 0.0, e)

    pl.semaphore_wait(barrier, len(greeted))

    def rates_block(unit):
        return rt.at[pl.ds(me & (N - unit), unit)]

    def gather_start(at):
        unit, group = stages[at]
        for to in group:
            pltpu.make_async_remote_copy(
                rates_block(unit), rates_block(unit), ss0.at[at], rs0.at[at],
                device_id=(to,), device_id_type=MESH,
            ).start()

    def gather_all(at):
        unit, group = stages[at]
        part = rt.at[pl.ds(0, unit * len(group))]
        return pltpu.make_async_remote_copy(
            part, part, ss0.at[at], rs0.at[at], device_id=(me,), device_id_type=MESH
        )

    gather_start(0)

    def face(j, plane):
        u = u_ref[pl.ds(pl.multiple_of(j * E, E), E), :]
        first = roll(u, j)
        last = roll(u, j + (N - E + 1))
        return jnp.where(lane32 == j, jnp.where(up, last, first), plane)

    wz = lax.fori_loop(0, E, face, jnp.zeros((E, N), F32))

    gather_all(0).wait_recv()
    gather_start(1)

    cu2 = jnp.where(lane32 < E - 1, 2.0 * own[2], 0.0)
    cd2 = jnp.where(lane32 > 0, 2.0 * own[2], 0.0)
    dg2 = cu2 + cd2
    r1x2 = 2.0 * own[1]

    def right_side(t, prev):
        us = []
        for m in range(5):
            j = jnp.minimum(t * 4 + m, E - 1)
            us.append(u_ref[pl.ds(pl.multiple_of(j * E, E), E), :])
        for m in range(4):
            j = t * 4 + m
            at = pl.ds(pl.multiple_of(j * E, E), E)
            u = us[m]
            low = jnp.where(j == 0, 0.0, r1x2)
            high = jnp.where(j == E - 1, 0.0, r1x2)
            f_ref[at, :] = (
                f_ref[at, :]
                + cu2 * roll(u, -1)
                + cd2 * roll(u, 1)
                + low * prev
                + high * us[m + 1]
                - (dg2 + low + high) * u
            )
            prev = u
        return prev

    lax.fori_loop(0, E // 4, right_side, jnp.zeros((E, N), F32))

    def solve_i(load_plane_row):
        def forward(t, carry):
            g, h = carry
            for m in range(4):
                i = t * 4 + m
                at = pl.ds(i, E, stride=E)
                g = co0[0, pl.ds(i, 1), :] * f_ref[at, :] + co0[1, pl.ds(i, 1), :] * g
                t_ref[at, :] = g
                if load_plane_row is not None:
                    h = ecm[i] * load_plane_row(i) + ece[i] * h
                    e_ref[i] = h
            return g, h

        lax.fori_loop(0, E // 4, forward, (jnp.zeros((E, N), F32), jnp.zeros((8, N), F32)))

        def backward(t, carry):
            x, h = carry
            for m in range(4):
                i = E - 1 - t * 4 - m
                at = pl.ds(i, E, stride=E)
                x = t_ref[at, :] + co0[2, pl.ds(i, 1), :] * x
                t_ref[at, :] = x
                if load_plane_row is not None:
                    h = e_ref[i] + jnp.where(i == E - 1, 0.0, ece[i]) * h
                    e_ref[i] = h
            return x, h

        lax.fori_loop(0, E // 4, backward, (jnp.zeros((E, N), F32), jnp.zeros((8, N), F32)))

    def solve_j(extra, extra_first, extra_last):
        def forward(t, g):
            for m in range(4):
                j = t * 4 + m
                at = pl.ds(pl.multiple_of(j * E, E), E)
                d = t_ref[at, :] - 2.0 * u_ref[at, :]
                if extra is not None:
                    d = d + extra(j)
                if extra_first is not None and m == 0:
                    d = d + jnp.where(j == 0, extra_first, 0.0)
                if extra_last is not None and m == 3:
                    d = d + jnp.where(j == E - 1, extra_last, 0.0)
                g = co1[0, pl.ds(j, 1), :] * d + co1[1, pl.ds(j, 1), :] * g
                g_ref[at, :] = g
            return g

        lax.fori_loop(0, E // 4, forward, jnp.zeros((E, N), F32))

        def backward(t, x):
            for m in range(4):
                j = E - 1 - t * 4 - m
                at = pl.ds(pl.multiple_of(j * E, E), E)
                x = g_ref[at, :] + co1[2, pl.ds(j, 1), :] * x
                g_ref[at, :] = x
            return x

        lax.fori_loop(0, E // 4, backward, jnp.zeros((E, N), F32))

    solve_i(None)
    solve_j(None, None, None)

    rowN, colN = iota((N, N), 0), iota((N, N), 1)
    kin = rowN & 31
    weight = column(own[2], jnp.where(up, E - 1 - kin, kin))
    weight = packed_weights(jnp.where((rowN >> 5) == (colN >> 5), weight, 0.0))

    def face_mean(t, plane):
        y = packed_dot(g_ref[pl.ds(pl.multiple_of(t * 8 * E, 8 * E), 8 * E), :], weight)
        for m in range(8):
            plane = jnp.where(lane32 == t * 8 + m, y[m * E : (m + 1) * E], plane)
        return plane

    t_own = lax.fori_loop(0, 4, face_mean, jnp.zeros((E, N), F32))

    rows_a = jnp.transpose(
        jnp.concatenate(
            [
                t_ref[pl.ds(0, E, stride=E), :],
                t_ref[pl.ds(E - 1, E, stride=E), :],
                g_ref[0:E, :],
                g_ref[(E - 1) * E : E * E, :],
            ],
            0,
        )
    )
    for q in range(4):
        send1b[pl.ds(8 * (q % 2) + 3 * (q // 2), E, stride=16), :] = rows_a[q * E : (q + 1) * E]
    mine = me >> 1

    def block(ref, index, rows):
        pitch = 8 if rows == 6 else rows
        return ref.at[pl.ds(pl.multiple_of(index * pitch, pitch), rows)]

    def to_owners(src, dst, rows, send_sem, recv_sem, local_sem):
        def send(step, carry):
            o = (mine + step) & (OWNERS - 1)
            pltpu.make_async_remote_copy(
                block(src, o, rows), block(dst, me, rows), send_sem, recv_sem,
                device_id=(2 * o,), device_id_type=MESH,
            ).start()
            return carry

        lax.fori_loop(1, OWNERS, send, 0)

        @pl.when(jnp.logical_not(owner))
        def _():
            pltpu.make_async_remote_copy(
                block(src, mine, rows), block(dst, me, rows), send_sem, recv_sem,
                device_id=(2 * mine,), device_id_type=MESH,
            ).start()

        @pl.when(owner)
        def _():
            pltpu.make_async_copy(block(src, mine, rows), block(dst, me, rows), local_sem).start()

    def to_owners_wait(src, rows, send_sem):
        def left(count):
            part = src.at[pl.ds(0, count * rows)]
            pltpu.make_async_remote_copy(
                part, part, send_sem, send_sem, device_id=(me,), device_id_type=MESH
            ).wait_send()

        @pl.when(owner)
        def _():
            left(OWNERS - 1)

        @pl.when(jnp.logical_not(owner))
        def _():
            left(OWNERS)

    def owner_wait(src, dst, rows, recv_sem, local_sem):
        pltpu.make_async_copy(block(src, mine, rows), block(dst, me, rows), local_sem).wait()
        part = dst.at[pl.ds(0, rows * (N - 1))]
        pltpu.make_async_remote_copy(
            part, part, recv_sem, recv_sem, device_id=(me,), device_id_type=MESH
        ).wait_recv()

    def to_bricks(src, dst, rows, send_sem, recv_sem, local_sem):
        def send(step, carry):
            to = (me + step) & (N - 1)
            pltpu.make_async_remote_copy(
                block(src, to, rows), block(dst, mine, rows), send_sem, recv_sem,
                device_id=(to,), device_id_type=MESH,
            ).start()
            return carry

        lax.fori_loop(1, N, send, 0)
        pltpu.make_async_copy(block(src, me, rows), block(dst, mine, rows), local_sem).start()

    def to_bricks_wait(src, rows, send_sem):
        part = src.at[pl.ds(0, rows * (N - 1))]
        pltpu.make_async_remote_copy(
            part, part, send_sem, send_sem, device_id=(me,), device_id_type=MESH
        ).wait_send()

    def brick_wait(src, dst, rows, recv_sem, local_sem):
        def arrived(count):
            part = dst.at[pl.ds(0, count * rows)]
            pltpu.make_async_remote_copy(
                part, part, recv_sem, recv_sem, device_id=(me,), device_id_type=MESH
            ).wait_recv()

        @pl.when(owner)
        def _():
            pltpu.make_async_copy(block(src, me, rows), block(dst, mine, rows), local_sem).wait()
            arrived(OWNERS - 1)

        @pl.when(jnp.logical_not(owner))
        def _():
            arrived(OWNERS)

    owner = (me & 1) == 0

    @pl.when(owner)
    def _():
        s2, l2 = iota((256, 256), 0), iota((256, 256), 1)
        lane256 = iota((1, 256), 1)

        def heads(before, doublings):
            target = jnp.where(before < 0, lane256, before)
            step = one_hot(s2 == target)
            for _ in range(doublings):
                step = jnp.dot(step, step, preferred_element_type=F32).astype(BF16)
            return step

        before0, before1 = nbv[0, 0:1, :], nbv[1, 0:1, :]
        znear = jnp.maximum(nbv[2, 0:1, :], nbv[2, 1:2, :]).astype(F32)
        rank0, rank1 = rkv[0:1, :].astype(F32), rkv[1:2, :].astype(F32)
        lead = jnp.dot(heads(before1, 3), heads(before0, 5), preferred_element_type=F32)
        key = total(lead * s2.astype(F32), 0) * 32.0 + rank1
        keyed = total(jnp.where(s2 == l2, key + rank0 * 1e5, 0.0), 1)
        row = total(jnp.where(keyed < key, 1.0, 0.0), 0)
        pos = rank0 * 8.0 + row
        at = s2.astype(F32) == pos
        slot_at = total(jnp.where(at, lane256.astype(F32), 0.0), 1)
        rank_at = total(jnp.where(at, rank1, 0.0), 1)
        z_at = total(jnp.where(at, znear, 0.0), 1)
        kk[0] = jnp.where(rank_at > 0.5, 1.0, jnp.zeros((256, N), F32))
        dev = lane.astype(F32) * 2.0
        s1, l1 = iota((N, 256), 0), iota((N, 256), 1)
        lf = l1.astype(F32)
        for b in range(2):
            perm[b] = one_hot(slot_at == dev + b)
            perm[2 + b] = one_hot(z_at == dev + b)
            mine = l1 == 2 * s1 + b
            pos_b = total(jnp.where(mine, pos, 0.0), 1)
            z_b = total(jnp.where(mine, znear, 0.0), 1)
            posz_b = total(jnp.where(lf == z_b, pos + 1.0, 0.0), 1) - 1.0
            permt[b] = one_hot(lf == pos_b)
            permt[2 + b] = one_hot(lf == posz_b)

    gather_all(1).wait_recv()

    def rates_of(indices):
        rows = []
        for b in range(2):
            index = jnp.maximum(indices[b], 0)
            got = rt[index >> 1]
            cross = (index & 1) != b
            rows.append(jnp.where(cross, roll(got, 64), got))
        got = jnp.where(lane < 64, rows[0], rows[1])
        has = by_brick([jnp.where(indices[b] >= 0, 1.0, 0.0) for b in range(2)])
        return got, has

    stack = jnp.ones((8, N), F32)
    has = jnp.zeros((8, N), F32)
    for at, name in ((0, "yu"), (1, "yl"), (2, "z")):
        got, there = rates_of(near[name])
        stack = jnp.where(sub8 == at, got, stack)
        has = jnp.where(sub8 == at, there, has)
    stack = jnp.where((sub8 >= 3) & (sub8 < 7), message, stack)
    near_r = []
    for d in range(3):
        x = roll(jnp.where(lane32 == d, stack, 0.0), -d)
        for shift in (1, 2, 4, 8, 16):
            x = x + roll(x, shift)
        near_r.append(x)
    g1 = has * 2.0 * own[1] * near_r[1] / (own[1] + near_r[1])
    g2 = has * 2.0 * own[2] * near_r[2] / (own[2] + near_r[2])
    gyu, gyl, gz = g1[0:1], g1[1:2], g2[2:3]

    u_first, u_last = u_ref[0:E, :], u_ref[(E - 1) * E : E * E, :]
    s_up = 2.0 * gyu * u_last
    s_low = 2.0 * gyl * u_first
    s_z = 2.0 * gz * wz
    i8 = iota((E, 8, N), 0)
    mm, ee = sweep_terms(near_r[0][None], i8)
    ecm[...] = mm
    ece[...] = ee
    pl_ref[0] = s_up
    pl_ref[1] = s_low
    pl_ref[2] = s_z

    h = jnp.zeros((8, N), F32)
    for i in range(E):
        x_up, x_low, x_z = [pl_ref[p, i : i + 1, :] for p in range(3)]
        x = jnp.where(sub8 == 0, x_up, jnp.where(sub8 == 1, x_low, x_z))
        x = jnp.where(sub8 == 3, -x_z, jnp.where(sub8 == 4, -x_low, jnp.where(sub8 == 5, -x_up, x)))
        h = ecm[i] * x + ece[i] * h
        e_ref[i] = h
    for i in range(E - 2, -1, -1):
        h = e_ref[i] + ece[i] * h
        e_ref[i] = h
    p_up, p_low, p_z, p_out, p_first, p_last = [e_ref[:, p, :] for p in range(6)]

    rows_b = jnp.transpose(jnp.concatenate([s_up, s_low, p_up, p_low], 0))
    rows_d = jnp.transpose(jnp.concatenate([p_first, p_last], 0))
    group8 = (sub8 & 3) == grp
    ends_i = []
    for p, at in ((p_z, 2), (p_out, 3)):
        r1 = near_r[1][at : at + 1]
        ends = jnp.where(sub8 < 4, column(r1, lane32), column(r1, E - 1 - lane32))
        x = dot_last(jnp.where(group8, ends, 0.0), p)
        ends_i.append(jnp.concatenate([x, jnp.zeros((8, N - E), F32)], 1))

    def end_row(p, x, q):
        c = jnp.where(lane < 32, roll(p[0:1], -E * q), roll(p[E - 1 : E], E - E * q))
        c = jnp.where(lane < 64, c, roll(x[q : q + 1], 64))
        return jnp.where(lane < 96, c, roll(x[q + 4 : q + 5], 96))

    for q in range(4):
        b, sp = q // 2, q % 2
        mine_up = near["zu"][b] >= 0
        first_face = jnp.where(mine_up, 0.0, 1.0)
        c_near, c_own = end_row(p_z, ends_i[0], q), end_row(p_out, ends_i[1], q)
        send1c[4 * sp + 2 * b : 4 * sp + 2 * b + 1, :] = c_near * (1.0 - first_face)
        send1c[4 * sp + 2 * b + 1 : 4 * sp + 2 * b + 2, :] = c_own * first_face
        send1c[8 + 4 * sp + 2 * b : 8 + 4 * sp + 2 * b + 1, :] = c_near * first_face
        send1c[8 + 4 * sp + 2 * b + 1 : 8 + 4 * sp + 2 * b + 2, :] = c_own * (1.0 - first_face)
        send1b[pl.ds(8 * sp + 3 * b + 1, E, stride=16), :] = rows_b[q * E : (q + 1) * E]
        zt = jnp.where(lane < 96, roll(s_z, 64 - E * q), roll(t_own, 96 - E * q))
        part = jnp.concatenate([rows_d[q * E : (q + 1) * E], jnp.zeros((E, 64), F32)], 1)
        send1b[pl.ds(8 * sp + 3 * b + 2, E, stride=16), :] = jnp.where(lane < 64, part, zt)

    to_owners(send1b, land1b, 6, ss1b, rs1b, own_sem.at[1])

    face_owners = [0, 1, OWNERS - 2, OWNERS - 1]
    for c, o in enumerate(face_owners):

        @pl.when(me != 2 * o)
        def _(c=c, o=o):
            pltpu.make_async_remote_copy(
                block(send1c, c, 4), block(land1c, me, 4), ss1c, rs1c,
                device_id=(2 * o,), device_id_type=MESH,
            ).start()

        @pl.when(me == 2 * o)
        def _(c=c):
            pltpu.make_async_copy(block(send1c, c, 4), block(land1c, me, 4), own_sem.at[2]).start()

    at_face = jnp.logical_and(owner, jnp.logical_or(mine < 2, mine >= OWNERS - 2))

    @pl.when(owner)
    def _():
        sp32 = (mine & 1) * 32
        table = rt[:, 0, :]
        ordered = pick(perm[0], table) + pick(perm[1], roll(table, 64))
        pick_at = iota((N, 2 * N), 0)
        pick_to = iota((N, 2 * N), 1) >> 7
        both = pick_right(ordered, one_hot(pick_at == sp32 + pick_to))
        r0, r1 = both[:, 0:N], both[:, N : 2 * N]
        p256 = iota((256, N), 0)
        linked = kk[0]
        dims = []
        for d, r in ((0, r0), (1, r1)):
            alpha, eps = corners(r)
            if d == 0:
                before = jnp.concatenate([r[0:8], r[0:248]], 0)
                gl = jnp.where(p256 >= 8, 2.0 * r * before / (r + before), 0.0)
                gr = jnp.concatenate([gl[8:256], jnp.zeros((8, N), F32)], 0)
            else:
                before = roll(r, 1, 0)
                gl = linked * 2.0 * r * before / (r + before)
                gr = roll(gl, -1, 0)
            dims.append((alpha, eps, gl, gr))
            chain[0 + 4 * d] = alpha
            chain[1 + 4 * d] = eps
            chain[2 + 4 * d] = gl
            chain[3 + 4 * d] = gr

        def elimination(alpha, eps, gl, gr, fq):
            b00 = 1.0 + gl * alpha * (1.0 + fq)
            b10 = gl * eps * (1.0 + fq)
            det = b00 * (1.0 + gr * alpha) - gr * eps * b10
            return b00, b10, 1.0 / det

        def along(x, fq):
            at = pl.ds(pl.multiple_of(x * 8, 8), 8)
            alpha, eps, gl, gr = [chain[c, at, :] for c in range(4)]
            kk[1, at, :] = fq
            b00, b10, inv = elimination(alpha, eps, gl, gr, fq)
            return -gr * (b00 * alpha - b10 * eps) * inv

        lax.fori_loop(0, E, along, jnp.zeros((8, N), F32))
        alpha, eps, gl, gr = dims[1]
        fq = jnp.zeros((256, N), F32)
        for _ in range(7):
            b00, b10, inv = elimination(alpha, eps, gl, gr, fq)
            fq = linked * roll(-gr * (b00 * alpha - b10 * eps) * inv, 1, 0)
        kk[2] = fq

        def terms(d, fq):
            alpha, eps, gl, gr = [chain[4 * d + c] for c in range(4)]
            b00, b10, inv = elimination(alpha, eps, gl, gr, fq)
            a01, a11 = gr * eps, 1.0 + gr * alpha
            base = 3 + 8 * d
            kk[base] = b00 * inv
            kk[base + 1] = -b10 * inv
            kk[base + 2] = a11 * inv
            kk[base + 3] = -a01 * inv
            kk[base + 4] = gl * (a11 * alpha - a01 * eps) * inv
            kk[base + 5] = -gr * (b00 * alpha - b10 * eps) * inv
            kk[base + 6] = gl * (b00 * eps - b10 * alpha) * inv
            kk[base + 7] = gr * eps * inv

        terms(0, kk[1])
        terms(1, kk[2])
        both_l = lane32 + 0 * p256
        j_of = jnp.where((grp & 1) == 0, both_l, E - 1 - both_l)
        chain[8] = column(r1, j_of)
        chain[9] = column(r0, both_l)
        chain[10] = column(r0, E - 1 - both_l)

        def ordered_rows(land, row, which):
            rows = land.shape[0] // N
            second = 3 if rows == 8 else 2
            return pick(perm[which], land[pl.ds(row, N, stride=rows), :]) + pick(
                perm[which + 1], land[pl.ds(row + second, N, stride=rows), :]
            )

        kk[0] = linked
        owner_wait(send1b, land1b, 6, rs1b, own_sem.at[1])
        yb = ordered_rows(land1b, 1, 0)
        yd = ordered_rows(land1b, 2, 0)
        bl = linked * roll(yb, 1, 0)
        bu = roll(linked, -1, 0) * roll(yb, -1, 0)
        swap = jnp.where(lane < 32, roll(yb, -32), roll(yb, 32))
        out2 = jnp.where(lane < 64, jnp.where(lane < 32, bl, bu) - swap, yd)
        for b in range(2):
            for kind, which in ((0, b), (1, 2 + b)):
                send2a[pl.ds(2 * b + kind, N, stride=4), :] = pick(permt[which], out2)
        to_bricks(send2a, land2a, 4, ss2a, rs2a, own_sem.at[3])
        straight = jnp.where(lane < 96, bl, bu) + roll(yd, 64)
        crossed = jnp.where(lane < 96, roll(straight, -32), roll(straight, 32))
        ends0 = jnp.where(
            (lane == 0) | (lane == 63),
            roll(straight, 64),
            jnp.where(lane == 32, roll(straight, 65), jnp.where(lane == 31, roll(straight, 63), 0.0)),
        )
        chain[11] = ordered_rows(land1b, 0, 0) + jnp.where(
            lane >= 64, chain[4] * straight + chain[5] * crossed, ends0
        )

        @pl.when(at_face)
        def _():
            pltpu.make_async_copy(block(send1c, 0, 4), block(land1c, me, 4), own_sem.at[2]).wait()
            part = land1c.at[pl.ds(0, 4 * (N - 1))]
            pltpu.make_async_remote_copy(
                part, part, rs1c, rs1c, device_id=(me,), device_id_type=MESH
            ).wait_recv()
            chain[11] = chain[11] + ordered_rows(land1c, 0, 2) + ordered_rows(land1c, 1, 0)

        ya = chain[11]

        def before_x(v, n):
            return jnp.concatenate([jnp.zeros((8 * n, N), F32), v[0 : 256 - 8 * n]], 0)

        def after_x(v, n):
            return jnp.concatenate([v[8 * n : 256], jnp.zeros((8 * n, N), F32)], 0)

        def before_y(v, n):
            return roll(v, n, 0)

        def after_y(v, n):
            return roll(v, -n, 0)

        def chains(y0, y1, d, gl, gr, before, after, steps):
            base = 3 + 8 * d
            e1 = kk[base] * y1 + kk[base + 1] * y0
            slope = kk[base + 6]
            for n in steps:
                e1 = e1 + slope * before(e1, n)
                slope = slope * before(slope, n)
            e0 = kk[base + 2] * y0 + kk[base + 3] * y1 + kk[base + 4] * before(e1, 1)
            slope = kk[base + 7]
            zp = e0
            for n in steps:
                zp = zp + slope * after(zp, n)
                slope = slope * after(slope, n)
            zp_next = after(zp, 1)
            zq = e1 + -kk[base + 5] * zp_next
            return -gl * (zp - before(zq, 1)), -gr * (zq - zp_next)

        al, ar = chains(
            ya, roll(ya, -32), 0, chain[2], chain[3], before_x, after_x, (1, 2, 4, 8, 16)
        )
        spread = jnp.where(
            lane < 64,
            jnp.where(lane < 32, al, roll(al, 32)),
            jnp.where(lane < 96, roll(ar, 64), roll(ar, 96)),
        )
        src = iota((N, 2 * N), 0) >> 5
        dst = iota((N, 2 * N), 1)
        side, part = dst >> 7, (dst >> 5) & 3
        sums = pick_right(
            spread * chain[8], one_hot((part >= 2) & (src == 2 * side + part - 2))
        )
        ya = ya + chain[9] * sums[:, 0:N] + chain[10] * sums[:, N : 2 * N]
        bl_c, br_c = chains(ya, roll(ya, -32), 1, chain[6], chain[7], before_y, after_y, (1, 2, 4))
        out1 = jnp.where(
            lane < 64,
            jnp.where(lane < 32, al, roll(ar, 32)),
            jnp.where(lane < 96, bl_c, roll(br_c, 32)),
        )
        for b in range(2):
            for kind, which in ((0, b), (1, 2 + b)):
                send2b[pl.ds(2 * b + kind, N, stride=4), :] = pick(permt[which], out1)
        to_bricks(send2b, land2b, 4, ss2b, rs2b, own_sem.at[4])

    def gathered(land, kind):
        return jnp.concatenate(
            [land[pl.ds(q % 2 * 4 + q // 2 * 2 + kind, E, stride=8), :] for q in range(4)], 0
        )

    brick_wait(send2a, land2a, 4, rs2a, own_sem.at[3])
    own_h, near_h = gathered(land2a, 0), gathered(land2a, 1)
    halo = jnp.transpose(own_h)
    w_near = jnp.zeros((E, N), F32)
    t_near = jnp.zeros((E, N), F32)
    for q in range(4):
        part = near_h[q * E : (q + 1) * E]
        w_near = jnp.where(grp == q, roll(part, E * q - 64), w_near)
        t_near = jnp.where(grp == q, roll(part, E * q - 96), t_near)

    kz_own = jnp.where(up, E - 1 - lane32, lane32)
    kz_near = jnp.where(up, lane32, E - 1 - lane32)
    delta_z = w_near - s_z
    alpha_z = [corners(near_r[2][at : at + 1])[0] for at in (3, 2)]
    mark = jnp.concatenate(
        [
            jnp.where((sub8 == grp) & (lane32 == 0), 1.0, 0.0),
            jnp.where((sub8 == grp) & (lane32 == E - 1), 1.0, 0.0),
        ],
        1,
    )
    weights, cols = [], []
    for which, at, kz, rows_h, wplane in (
        (0, 3, kz_own, own_h, delta_z),
        (1, 2, kz_near, near_h, -delta_z),
    ):
        weights.append(jnp.where(sub8 == grp, column(near_r[2][at : at + 1], kz), 0.0))
        marked = dot_first(dot(weights[which], rows_h), mark)
        pl_ref[which] = marked[0:E, 0:N] + marked[E : 2 * E, N : 2 * N] + alpha_z[which] * wplane
        r1 = near_r[1][at : at + 1]
        cols.append(
            jnp.concatenate(
                [
                    jnp.where(sub8 == grp, column(r1, lane32), 0.0),
                    jnp.where(sub8 == grp, column(r1, E - 1 - lane32), 0.0),
                ],
                1,
            )
        )
        blocks_1[which] = packed_weights(inverse_blocks(r1))
    blocks_1[2] = packed_weights(inverse_blocks(own[2]))

    def on_face(plane, j):
        first = roll(plane, N - j)
        last = roll(plane, (N + E - 1 - j) & (N - 1))
        return jnp.where(face_lane, jnp.where(up, last, first), 0.0)

    pl_ref[2] = halo[0:E]
    pl_ref[3] = halo[E : 2 * E]
    pl_ref[4] = delta_z
    v0, w0 = column(own[0], row32), column(own[0], E - 1 - row32)

    brick_wait(send2b, land2b, 4, rs2b, own_sem.at[4])
    own_ab, near_ab = gathered(land2b, 0), gathered(land2b, 1)
    ab = jnp.transpose(own_ab)
    outer = []
    for which, rows_ab in ((0, own_ab), (1, near_ab)):
        ca = dot(weights[which], rows_ab)
        first_row = jnp.zeros((1, N), F32)
        last_row = jnp.zeros((1, N), F32)
        for q in range(4):
            first_row = jnp.where(grp == q, roll(ca[q : q + 1], E * q), first_row)
            last_row = jnp.where(grp == q, roll(ca[q : q + 1], E * q - E), last_row)
        pl_ref[which, 0:1, :] = pl_ref[which, 0:1, :] + first_row
        pl_ref[which, E - 1 : E, :] = pl_ref[which, E - 1 : E, :] + last_row
        sides = dot_first(ca, cols[which])
        outer.append(sides[64:96, 0:N] + sides[96:128, N : 2 * N])
    h = jnp.zeros((8, N), F32)
    for i in range(E):
        x = jnp.where(sub8 == 2, pl_ref[1, i : i + 1, :], pl_ref[0, i : i + 1, :])
        for at, p in ((4, 2), (5, 3), (6, 4)):
            x = jnp.where(sub8 == at, pl_ref[p, i : i + 1, :], x)
        h = ecm[i] * x + ece[i] * h
        e_ref[i] = h
    for i in range(E - 2, -1, -1):
        h = e_ref[i] + ece[i] * h
        e_ref[i] = h
    z_part = e_ref[:, 6, :]
    ends_z = []
    for which, at in ((0, 3), (1, 2)):
        ends_z.append(packed_dot(e_ref[:, at, :], blocks_1[which]) + outer[which])
    sigma = ends_z[0] + t_own
    tau = ends_z[1] + t_near
    c_plane = -gz * (sigma - tau) / (1.0 + gz * (alpha_z[0] + alpha_z[1]))

    ab_ref[...] = ab

    def answer(j):
        at_lower, at_upper = ab_ref[pl.ds(j, 1), :], ab_ref[pl.ds(E + j, 1), :]
        return v0 * at_lower + w0 * at_upper + on_face(z_part, j)

    solve_j(answer, ab[64:96] + e_ref[:, 4, :], ab[96:128] + e_ref[:, 5, :])
    zblocks = blocks_1[2]

    def finish(t, carry):
        d2 = []
        for m in range(8):
            at = pl.ds(pl.multiple_of((t * 8 + m) * E, E), E)
            d2.append(g_ref[at, :] + on_face(c_plane, t * 8 + m))
        d3 = packed_dot(jnp.concatenate(d2, 0), zblocks)
        at = pl.ds(pl.multiple_of(t * 8 * E, 8 * E), 8 * E)
        d3 = d3 + u_ref[at, :]
        for half in range(2):
            outs = swap_blocks(
                [d3[(half * 4 + m) * E : (half * 4 + m + 1) * E] for m in range(4)], grp
            )
            cols = pl.ds(pl.multiple_of((t * 2 + half) * N, N), N)
            for b in range(2):
                out_c[b, :, cols] = outs[2 * b]
                out_b[b, :, cols] = outs[2 * b + 1]
        return carry

    lax.fori_loop(0, 4, finish, 0)

    for at in range(2):
        gather_all(at).wait_send()
    to_owners_wait(send1b, 6, ss1b)

    def left_c(count):
        part = send1c.at[pl.ds(0, 4 * count)]
        pltpu.make_async_remote_copy(
            part, part, ss1c, ss1c, device_id=(me,), device_id_type=MESH
        ).wait_send()

    @pl.when(at_face)
    def _():
        left_c(3)

    @pl.when(jnp.logical_not(at_face))
    def _():
        left_c(4)

    @pl.when(owner)
    def _():
        to_bricks_wait(send2a, 4, ss2a)
        to_bricks_wait(send2b, 4, ss2b)


def body(calcium, buffer, fraction, rates, inverses, neighbors, ranks):
    vmem = pl.BlockSpec(memory_space=pltpu.VMEM)
    smem = pl.BlockSpec(memory_space=pltpu.SMEM)
    shape = jax.ShapeDtypeStruct(calcium.shape, F32)
    field = pltpu.VMEM((E * E, N), F32)
    return pl.pallas_call(
        step_kernel,
        out_shape=(shape, shape),
        in_specs=[smem, smem, vmem, vmem, vmem, vmem, vmem],
        out_specs=(vmem, vmem),
        scratch_shapes=[
            field,
            field,
            field,
            field,
            pltpu.VMEM((N, 1, N), F32),
            pltpu.VMEM((8 * OWNERS, N), F32),
            pltpu.VMEM((8 * N, N), F32),
            pltpu.VMEM((16, N), F32),
            pltpu.VMEM((4 * N, N), F32),
            pltpu.VMEM((4 * N, N), F32),
            pltpu.VMEM((4 * OWNERS, N), F32),
            pltpu.VMEM((4 * N, N), F32),
            pltpu.VMEM((4 * OWNERS, N), F32),
            pltpu.VMEM((3, 256, 256), BF16),
            pltpu.VMEM((3, E, N), F32),
            pltpu.VMEM((3, E, N), F32),
            pltpu.VMEM((E, 8, N), F32),
            pltpu.VMEM((E, 8, N), F32),
            pltpu.VMEM((E, 8, N), F32),
            pltpu.VMEM((5, E, N), F32),
            pltpu.VMEM((N, N), F32),
            pltpu.VMEM((4, 256, N), BF16),
            pltpu.VMEM((4, N, 256), BF16),
            pltpu.VMEM((19, 256, N), F32),
            pltpu.VMEM((12, 256, N), F32),
        ]
        + [pltpu.SemaphoreType.DMA((2,))] * 2
        + [pltpu.SemaphoreType.DMA] * 8
        + [pltpu.SemaphoreType.DMA((5,))],
        compiler_params=pltpu.CompilerParams(
            collective_id=0, has_side_effects=True, vmem_limit_bytes=60 * 1024 * 1024
        ),
    )(jnp.transpose(rates, (0, 2, 1)), neighbors, neighbors, ranks, calcium, buffer, fraction)


def solution(mesh):
    in_specs = (
        P("bricks", None, None),
        P("bricks", None, None),
        P("bricks", None, None),
        P("bricks", None, None),
        P("bricks", None, None, None, None),
        P(),
        P(),
    )
    out_specs = (P("bricks", None, None), P("bricks", None, None))
    return jax.shard_map(body, mesh=mesh, in_specs=in_specs, out_specs=out_specs, check_vma=False)
```

```python
import jax
import jax.numpy as jnp
from jax import lax
from jax.experimental import pallas as pl
from jax.experimental.pallas import tpu as pltpu
from jax.sharding import PartitionSpec as P

KON = 0.5
KOFF = 0.3
BTOT = 2.0
INFLUX = 0.1

MESH = pl.DeviceIdType.MESH
F32 = jnp.float32
BF16 = jnp.bfloat16
HIGH = lax.Precision.HIGHEST
N = 128
E = 32
OWNERS = 64


def iota(shape, axis):
    return lax.broadcasted_iota(jnp.int32, shape, axis)


def roll(x, shift, axis=-1):
    if axis < 0:
        axis += x.ndim
    if isinstance(shift, int):
        shift %= x.shape[axis]
        if shift == 0:
            return x
    return pltpu.roll(x, shift, axis)


def rho_of(r):
    h = 0.5 / r
    s = jnp.sqrt(h * (2.0 + h))
    return 1.0 + h - s, s - h


def power(log_rho, n):
    return jnp.exp(log_rho * n.astype(F32))


def corners(r):
    rho, gap = rho_of(r)
    p2 = rho * rho
    p4 = p2 * p2
    p8 = p4 * p4
    p16 = p8 * p8
    p32 = p16 * p16
    kappa = rho / (r * gap * (1.0 - p32 * p32))
    return kappa * (1.0 + p32 * p32 / rho), kappa * (p32 / rho + p32)


def column(r, index):
    rho, gap = rho_of(r)
    lr = jnp.log(rho)
    kappa = rho / (r * gap * (1.0 - jnp.exp(lr * 64.0)))
    return kappa * (power(lr, index) + power(lr, 63 - index))


def inverse_blocks(r):
    rho, gap = rho_of(r)
    lr = jnp.log(rho)
    scale = rho / (r * gap * (1.0 + rho) * (1.0 - jnp.exp(lr * 64.0)))
    row, col = iota((N, N), 0), iota((N, N), 1)
    a, b = row & 31, col & 31
    away = jnp.abs(a - b)
    total = power(lr, away) + power(lr, a + b + 1) + power(lr, 63 - a - b) + power(lr, 64 - away)
    return jnp.where((row >> 5) == (col >> 5), total * scale, 0.0)


def sweep_terms(r, index):
    rho, _ = rho_of(r)
    lr = jnp.log(rho)
    rho2 = rho * rho
    odd = power(lr, 2 * index + 1)
    ratio = rho * (1.0 + odd) / (1.0 + odd * rho2)
    last = jnp.exp(lr * 61.0)
    ratio30 = rho * (1.0 + last) / (1.0 + last * rho2)
    m = jnp.where(index == E - 1, 1.0 / (1.0 + r - r * ratio30), ratio / r)
    return m, m * r


def swap_blocks(x, grp):
    low = grp < 2
    even = (grp & 1) == 0
    y = [None] * 4
    for q in range(2):
        a, b = x[q], x[q + 2]
        y[q] = jnp.where(low, a, roll(b, 64))
        y[q + 2] = jnp.where(low, roll(a, 64), b)
    z = [None] * 4
    for q in (0, 2):
        a, b = y[q], y[q + 1]
        z[q] = jnp.where(even, a, roll(b, 32))
        z[q + 1] = jnp.where(even, roll(a, -32), b)
    return z


def split3(x):
    a = x.astype(BF16)
    rest = x - a.astype(F32)
    b = rest.astype(BF16)
    c = (rest - b.astype(F32)).astype(BF16)
    return a, b, c


def pick(select, x):
    out = None
    for part in split3(x):
        term = jnp.dot(select, part, preferred_element_type=F32)
        out = term if out is None else out + term
    return out


def pick_right(x, select):
    out = None
    for part in split3(x):
        term = jnp.dot(part, select, preferred_element_type=F32)
        out = term if out is None else out + term
    return out


def split2(x):
    a = x.astype(BF16)
    return a, (x - a.astype(F32)).astype(BF16)


def contract(a, b, dims):
    ah, al = split2(a)
    bh, bl = split2(b)
    dims = (dims, ((), ()))
    out = lax.dot_general(ah, bh, dims, preferred_element_type=F32)
    out = out + lax.dot_general(al, bh, dims, preferred_element_type=F32)
    return out + lax.dot_general(ah, bl, dims, preferred_element_type=F32)


def dot(a, b):
    return contract(a, b, ((1,), (0,)))


def dot_first(a, b):
    return contract(a, b, ((0,), (0,)))


def dot_last(a, b):
    return contract(a, b, ((1,), (1,)))


def packed_weights(w):
    h, l = split2(w)
    return jnp.concatenate(
        [jnp.concatenate([h, l], 1), jnp.concatenate([h, jnp.zeros_like(h)], 1)], 0
    )


def packed_dot(x, weights):
    out = jnp.dot(jnp.concatenate(split2(x), 1), weights, preferred_element_type=F32)
    return out[:, 0:N] + out[:, N : 2 * N]


def one_hot(cond):
    return jnp.where(cond, 1.0, 0.0).astype(BF16)


def total(x, axis):
    return jnp.sum(x, axis=axis, keepdims=True)


def step_kernel(
    rates, nbs, nbv, rkv, cal, buf, frac, out_c, out_b,
    u_ref, f_ref, t_ref, g_ref, rt, send1b, land1b, send1c, land1c,
    send2a, land2a, send2b, land2b, blocks_1,
    co0, co1, ecm, ece, e_ref, pl_ref, ab_ref, perm, permt, kk, chain,
    ss0, rs0, ss1b, rs1b, ss1c, rs1c, ss2a, rs2a, ss2b, rs2b, own_sem,
):
    me = lax.axis_index("bricks")
    barrier = pltpu.get_barrier_semaphore()

    stages = [(1, [me ^ t for t in range(1, 8)]), (8, [me ^ (8 * t) for t in range(1, 16)])]
    greeted = [to for _, group in stages for to in group]
    for to in greeted:
        pl.semaphore_signal(barrier, inc=1, device_id=(to,), device_id_type=MESH)

    lane = iota((1, N), 1)
    lane32 = lane & 31
    grp = lane >> 5
    sub8 = iota((8, N), 0)
    row32 = iota((E, N), 0)

    own = []
    for d in range(3):
        r = jnp.zeros((1, N), F32)
        for q in range(4):
            r = jnp.where(grp == q, rates[q // 2, q % 2, d], r)
        own.append(r)
    message = jnp.where(lane32 == 0, own[0], jnp.where(lane32 == 1, own[1], own[2]))
    rt[me] = message
    near = {}
    for name, d, side in (("yl", 1, 0), ("yu", 1, 1), ("zl", 2, 0), ("zu", 2, 1)):
        near[name] = [nbs[d, side, 2 * me + b] for b in range(2)]
    near["z"] = [jnp.maximum(near["zl"][b], near["zu"][b]) for b in range(2)]

    def by_brick(pair):
        return jnp.where(lane < 64, pair[0], pair[1])

    up = by_brick([jnp.where(v >= 0, 1, 0) for v in near["zu"]]) == 1
    upf = jnp.where(up, 1.0, 0.0)
    face_lane = lane32 == jnp.where(up, E - 1, 0)

    def lay(t, carry):
        cols = pl.ds(pl.multiple_of(t * N, N), N)
        us, fs = [], []
        for b in range(2):
            ca, bo, al = cal[b, :, cols], buf[b, :, cols], frac[b, :, cols]
            bind = KON * ca * (BTOT - bo) - KOFF * bo
            us += [ca, bo]
            fs += [2.0 * ca - bind + INFLUX * (1.0 - al) / al, 2.0 * bo + bind]
        us = swap_blocks(us, grp)
        fs = swap_blocks(fs, grp)
        for m in range(4):
            at = pl.ds(pl.multiple_of((t * 4 + m) * E, E), E)
            u_ref[at, :] = us[m]
            f_ref[at, :] = fs[m]
        return carry

    lax.fori_loop(0, 8, lay, 0)

    for co, r in ((co0, own[0]), (co1, own[1])):
        m, e = sweep_terms(r, row32)
        co[0] = m
        co[1] = e
        co[2] = jnp.where(row32 == E - 1, 0.0, e)

    pl.semaphore_wait(barrier, len(greeted))

    def rates_block(unit):
        return rt.at[pl.ds(me & (N - unit), unit)]

    def gather_start(at):
        unit, group = stages[at]
        for to in group:
            pltpu.make_async_remote_copy(
                rates_block(unit), rates_block(unit), ss0.at[at], rs0.at[at],
                device_id=(to,), device_id_type=MESH,
            ).start()

    def gather_all(at):
        unit, group = stages[at]
        part = rt.at[pl.ds(0, unit * len(group))]
        return pltpu.make_async_remote_copy(
            part, part, ss0.at[at], rs0.at[at], device_id=(me,), device_id_type=MESH
        )

    gather_start(0)

    def face(j, plane):
        u = u_ref[pl.ds(pl.multiple_of(j * E, E), E), :]
        first = roll(u, j)
        last = roll(u, j + (N - E + 1))
        return jnp.where(lane32 == j, jnp.where(up, last, first), plane)

    wz = lax.fori_loop(0, E, face, jnp.zeros((E, N), F32))

    cu2 = jnp.where(lane32 < E - 1, 2.0 * own[2], 0.0)
    cd2 = jnp.where(lane32 > 0, 2.0 * own[2], 0.0)
    dg2 = cu2 + cd2
    r1x2 = 2.0 * own[1]

    def right_side(t, prev):
        us = []
        for m in range(5):
            j = jnp.minimum(t * 4 + m, E - 1)
            us.append(u_ref[pl.ds(pl.multiple_of(j * E, E), E), :])
        for m in range(4):
            j = t * 4 + m
            at = pl.ds(pl.multiple_of(j * E, E), E)
            u = us[m]
            low = jnp.where(j == 0, 0.0, r1x2)
            high = jnp.where(j == E - 1, 0.0, r1x2)
            f_ref[at, :] = (
                f_ref[at, :]
                + cu2 * roll(u, -1)
                + cd2 * roll(u, 1)
                + low * prev
                + high * us[m + 1]
                - (dg2 + low + high) * u
            )
            prev = u
        return prev

    lax.fori_loop(0, E // 4, right_side, jnp.zeros((E, N), F32))

    gather_all(0).wait_recv()
    gather_start(1)

    def solve_i(load_plane_row):
        def forward(t, carry):
            g, h = carry
            for m in range(4):
                i = t * 4 + m
                at = pl.ds(i, E, stride=E)
                g = co0[0, pl.ds(i, 1), :] * f_ref[at, :] + co0[1, pl.ds(i, 1), :] * g
                t_ref[at, :] = g
                if load_plane_row is not None:
                    h = ecm[i] * load_plane_row(i) + ece[i] * h
                    e_ref[i] = h
            return g, h

        lax.fori_loop(0, E // 4, forward, (jnp.zeros((E, N), F32), jnp.zeros((8, N), F32)))

        def backward(t, carry):
            x, h = carry
            for m in range(4):
                i = E - 1 - t * 4 - m
                at = pl.ds(i, E, stride=E)
                x = t_ref[at, :] + co0[2, pl.ds(i, 1), :] * x
                t_ref[at, :] = x
                if load_plane_row is not None:
                    h = e_ref[i] + jnp.where(i == E - 1, 0.0, ece[i]) * h
                    e_ref[i] = h
            return x, h

        lax.fori_loop(0, E // 4, backward, (jnp.zeros((E, N), F32), jnp.zeros((8, N), F32)))

    def solve_j(extra, extra_first, extra_last):
        def forward(t, g):
            for m in range(4):
                j = t * 4 + m
                at = pl.ds(pl.multiple_of(j * E, E), E)
                d = t_ref[at, :] - 2.0 * u_ref[at, :]
                if extra is not None:
                    d = d + extra(j)
                if extra_first is not None and m == 0:
                    d = d + jnp.where(j == 0, extra_first, 0.0)
                if extra_last is not None and m == 3:
                    d = d + jnp.where(j == E - 1, extra_last, 0.0)
                g = co1[0, pl.ds(j, 1), :] * d + co1[1, pl.ds(j, 1), :] * g
                g_ref[at, :] = g
            return g

        lax.fori_loop(0, E // 4, forward, jnp.zeros((E, N), F32))

        def backward(t, x):
            for m in range(4):
                j = E - 1 - t * 4 - m
                at = pl.ds(pl.multiple_of(j * E, E), E)
                x = g_ref[at, :] + co1[2, pl.ds(j, 1), :] * x
                g_ref[at, :] = x
            return x

        lax.fori_loop(0, E // 4, backward, jnp.zeros((E, N), F32))

    solve_i(None)
    solve_j(None, None, None)

    rowN, colN = iota((N, N), 0), iota((N, N), 1)
    kin = rowN & 31
    weight = column(own[2], jnp.where(up, E - 1 - kin, kin))
    weight = packed_weights(jnp.where((rowN >> 5) == (colN >> 5), weight, 0.0))

    def face_mean(t, plane):
        y = packed_dot(g_ref[pl.ds(pl.multiple_of(t * 8 * E, 8 * E), 8 * E), :], weight)
        for m in range(8):
            plane = jnp.where(lane32 == t * 8 + m, y[m * E : (m + 1) * E], plane)
        return plane

    t_own = lax.fori_loop(0, 4, face_mean, jnp.zeros((E, N), F32))

    rows_a = jnp.transpose(
        jnp.concatenate(
            [
                t_ref[pl.ds(0, E, stride=E), :],
                t_ref[pl.ds(E - 1, E, stride=E), :],
                g_ref[0:E, :],
                g_ref[(E - 1) * E : E * E, :],
            ],
            0,
        )
    )
    for q in range(4):
        send1b[pl.ds(8 * (q % 2) + 3 * (q // 2), E, stride=16), :] = rows_a[q * E : (q + 1) * E]
    mine = me >> 1

    def block(ref, index, rows):
        pitch = 8 if rows == 6 else rows
        return ref.at[pl.ds(pl.multiple_of(index * pitch, pitch), rows)]

    def to_owners(src, dst, rows, send_sem, recv_sem, local_sem):
        def send(step, carry):
            o = (mine + step) & (OWNERS - 1)
            pltpu.make_async_remote_copy(
                block(src, o, rows), block(dst, me, rows), send_sem, recv_sem,
                device_id=(2 * o,), device_id_type=MESH,
            ).start()
            return carry

        lax.fori_loop(1, OWNERS, send, 0)

        @pl.when(jnp.logical_not(owner))
        def _():
            pltpu.make_async_remote_copy(
                block(src, mine, rows), block(dst, me, rows), send_sem, recv_sem,
                device_id=(2 * mine,), device_id_type=MESH,
            ).start()

        @pl.when(owner)
        def _():
            pltpu.make_async_copy(block(src, mine, rows), block(dst, me, rows), local_sem).start()

    def to_owners_wait(src, rows, send_sem):
        def left(count):
            part = src.at[pl.ds(0, count * rows)]
            pltpu.make_async_remote_copy(
                part, part, send_sem, send_sem, device_id=(me,), device_id_type=MESH
            ).wait_send()

        @pl.when(owner)
        def _():
            left(OWNERS - 1)

        @pl.when(jnp.logical_not(owner))
        def _():
            left(OWNERS)

    def owner_wait(src, dst, rows, recv_sem, local_sem):
        pltpu.make_async_copy(block(src, mine, rows), block(dst, me, rows), local_sem).wait()
        part = dst.at[pl.ds(0, rows * (N - 1))]
        pltpu.make_async_remote_copy(
            part, part, recv_sem, recv_sem, device_id=(me,), device_id_type=MESH
        ).wait_recv()

    def to_bricks(src, dst, rows, send_sem, recv_sem, local_sem):
        def send(step, carry):
            to = (me + step) & (N - 1)
            pltpu.make_async_remote_copy(
                block(src, to, rows), block(dst, mine, rows), send_sem, recv_sem,
                device_id=(to,), device_id_type=MESH,
            ).start()
            return carry

        lax.fori_loop(1, N, send, 0)
        pltpu.make_async_copy(block(src, me, rows), block(dst, mine, rows), local_sem).start()

    def to_bricks_wait(src, rows, send_sem):
        part = src.at[pl.ds(0, rows * (N - 1))]
        pltpu.make_async_remote_copy(
            part, part, send_sem, send_sem, device_id=(me,), device_id_type=MESH
        ).wait_send()

    def brick_wait(src, dst, rows, recv_sem, local_sem):
        def arrived(count):
            part = dst.at[pl.ds(0, count * rows)]
            pltpu.make_async_remote_copy(
                part, part, recv_sem, recv_sem, device_id=(me,), device_id_type=MESH
            ).wait_recv()

        @pl.when(owner)
        def _():
            pltpu.make_async_copy(block(src, me, rows), block(dst, mine, rows), local_sem).wait()
            arrived(OWNERS - 1)

        @pl.when(jnp.logical_not(owner))
        def _():
            arrived(OWNERS)

    owner = (me & 1) == 0

    @pl.when(owner)
    def _():
        s2, l2 = iota((256, 256), 0), iota((256, 256), 1)
        lane256 = iota((1, 256), 1)

        def heads(before, doublings):
            target = jnp.where(before < 0, lane256, before)
            step = one_hot(s2 == target)
            for _ in range(doublings):
                step = jnp.dot(step, step, preferred_element_type=F32).astype(BF16)
            return step

        before0, before1 = nbv[0, 0:1, :], nbv[1, 0:1, :]
        znear = jnp.maximum(nbv[2, 0:1, :], nbv[2, 1:2, :]).astype(F32)
        rank0, rank1 = rkv[0:1, :].astype(F32), rkv[1:2, :].astype(F32)
        lead = jnp.dot(heads(before1, 3), heads(before0, 5), preferred_element_type=F32)
        key = total(lead * s2.astype(F32), 0) * 32.0 + rank1
        keyed = total(jnp.where(s2 == l2, key + rank0 * 1e5, 0.0), 1)
        row = total(jnp.where(keyed < key, 1.0, 0.0), 0)
        pos = rank0 * 8.0 + row
        at = s2.astype(F32) == pos
        slot_at = total(jnp.where(at, lane256.astype(F32), 0.0), 1)
        rank_at = total(jnp.where(at, rank1, 0.0), 1)
        z_at = total(jnp.where(at, znear, 0.0), 1)
        kk[0] = jnp.where(rank_at > 0.5, 1.0, jnp.zeros((256, N), F32))
        dev = lane.astype(F32) * 2.0
        s1, l1 = iota((N, 256), 0), iota((N, 256), 1)
        lf = l1.astype(F32)
        for b in range(2):
            perm[b] = one_hot(slot_at == dev + b)
            perm[2 + b] = one_hot(z_at == dev + b)
            mine = l1 == 2 * s1 + b
            pos_b = total(jnp.where(mine, pos, 0.0), 1)
            z_b = total(jnp.where(mine, znear, 0.0), 1)
            posz_b = total(jnp.where(lf == z_b, pos + 1.0, 0.0), 1) - 1.0
            permt[b] = one_hot(lf == pos_b)
            permt[2 + b] = one_hot(lf == posz_b)

    gather_all(1).wait_recv()

    def rates_of(indices):
        rows = []
        for b in range(2):
            index = jnp.maximum(indices[b], 0)
            got = rt[index >> 1]
            cross = (index & 1) != b
            rows.append(jnp.where(cross, roll(got, 64), got))
        got = jnp.where(lane < 64, rows[0], rows[1])
        has = by_brick([jnp.where(indices[b] >= 0, 1.0, 0.0) for b in range(2)])
        return got, has

    stack = jnp.ones((8, N), F32)
    has = jnp.zeros((8, N), F32)
    for at, name in ((0, "yu"), (1, "yl"), (2, "z")):
        got, there = rates_of(near[name])
        stack = jnp.where(sub8 == at, got, stack)
        has = jnp.where(sub8 == at, there, has)
    stack = jnp.where((sub8 >= 3) & (sub8 < 7), message, stack)
    near_r = []
    for d in range(3):
        x = roll(jnp.where(lane32 == d, stack, 0.0), -d)
        for shift in (1, 2, 4, 8, 16):
            x = x + roll(x, shift)
        near_r.append(x)
    g1 = has * 2.0 * own[1] * near_r[1] / (own[1] + near_r[1])
    g2 = has * 2.0 * own[2] * near_r[2] / (own[2] + near_r[2])
    gyu, gyl, gz = g1[0:1], g1[1:2], g2[2:3]

    u_first, u_last = u_ref[0:E, :], u_ref[(E - 1) * E : E * E, :]
    s_up = 2.0 * gyu * u_last
    s_low = 2.0 * gyl * u_first
    s_z = 2.0 * gz * wz
    i8 = iota((E, 8, N), 0)
    mm, ee = sweep_terms(near_r[0][None], i8)
    ecm[...] = mm
    ece[...] = ee
    pl_ref[0] = s_up
    pl_ref[1] = s_low
    pl_ref[2] = s_z

    h = jnp.zeros((8, N), F32)
    for i in range(E):
        x_up, x_low, x_z = [pl_ref[p, i : i + 1, :] for p in range(3)]
        x = jnp.where(sub8 == 0, x_up, jnp.where(sub8 == 1, x_low, x_z))
        x = jnp.where(sub8 == 3, -x_z, jnp.where(sub8 == 4, -x_low, jnp.where(sub8 == 5, -x_up, x)))
        h = ecm[i] * x + ece[i] * h
        e_ref[i] = h
    for i in range(E - 2, -1, -1):
        h = e_ref[i] + ece[i] * h
        e_ref[i] = h
    p_up, p_low, p_z, p_out, p_first, p_last = [e_ref[:, p, :] for p in range(6)]

    rows_b = jnp.transpose(jnp.concatenate([s_up, s_low, p_up, p_low], 0))
    rows_d = jnp.transpose(jnp.concatenate([p_first, p_last], 0))
    group8 = (sub8 & 3) == grp
    ends_i = []
    for p, at in ((p_z, 2), (p_out, 3)):
        r1 = near_r[1][at : at + 1]
        ends = jnp.where(sub8 < 4, column(r1, lane32), column(r1, E - 1 - lane32))
        x = dot_last(jnp.where(group8, ends, 0.0), p)
        ends_i.append(jnp.concatenate([x, jnp.zeros((8, N - E), F32)], 1))

    def end_row(p, x, q):
        c = jnp.where(lane < 32, roll(p[0:1], -E * q), roll(p[E - 1 : E], E - E * q))
        c = jnp.where(lane < 64, c, roll(x[q : q + 1], 64))
        return jnp.where(lane < 96, c, roll(x[q + 4 : q + 5], 96))

    for q in range(4):
        b, sp = q // 2, q % 2
        mine_up = near["zu"][b] >= 0
        first_face = jnp.where(mine_up, 0.0, 1.0)
        c_near, c_own = end_row(p_z, ends_i[0], q), end_row(p_out, ends_i[1], q)
        send1c[4 * sp + 2 * b : 4 * sp + 2 * b + 1, :] = c_near * (1.0 - first_face)
        send1c[4 * sp + 2 * b + 1 : 4 * sp + 2 * b + 2, :] = c_own * first_face
        send1c[8 + 4 * sp + 2 * b : 8 + 4 * sp + 2 * b + 1, :] = c_near * first_face
        send1c[8 + 4 * sp + 2 * b + 1 : 8 + 4 * sp + 2 * b + 2, :] = c_own * (1.0 - first_face)
        send1b[pl.ds(8 * sp + 3 * b + 1, E, stride=16), :] = rows_b[q * E : (q + 1) * E]
        zt = jnp.where(lane < 96, roll(s_z, 64 - E * q), roll(t_own, 96 - E * q))
        part = jnp.concatenate([rows_d[q * E : (q + 1) * E], jnp.zeros((E, 64), F32)], 1)
        send1b[pl.ds(8 * sp + 3 * b + 2, E, stride=16), :] = jnp.where(lane < 64, part, zt)

    to_owners(send1b, land1b, 6, ss1b, rs1b, own_sem.at[1])

    face_owners = [0, 1, OWNERS - 2, OWNERS - 1]
    for c, o in enumerate(face_owners):

        @pl.when(me != 2 * o)
        def _(c=c, o=o):
            pltpu.make_async_remote_copy(
                block(send1c, c, 4), block(land1c, me, 4), ss1c, rs1c,
                device_id=(2 * o,), device_id_type=MESH,
            ).start()

        @pl.when(me == 2 * o)
        def _(c=c):
            pltpu.make_async_copy(block(send1c, c, 4), block(land1c, me, 4), own_sem.at[2]).start()

    at_face = jnp.logical_and(owner, jnp.logical_or(mine < 2, mine >= OWNERS - 2))

    @pl.when(owner)
    def _():
        sp32 = (mine & 1) * 32
        table = rt[:, 0, :]
        ordered = pick(perm[0], table) + pick(perm[1], roll(table, 64))
        pick_at = iota((N, 2 * N), 0)
        pick_to = iota((N, 2 * N), 1) >> 7
        both = pick_right(ordered, one_hot(pick_at == sp32 + pick_to))
        r0, r1 = both[:, 0:N], both[:, N : 2 * N]
        p256 = iota((256, N), 0)
        linked = kk[0]
        dims = []
        for d, r in ((0, r0), (1, r1)):
            alpha, eps = corners(r)
            if d == 0:
                before = jnp.concatenate([r[0:8], r[0:248]], 0)
                gl = jnp.where(p256 >= 8, 2.0 * r * before / (r + before), 0.0)
                gr = jnp.concatenate([gl[8:256], jnp.zeros((8, N), F32)], 0)
            else:
                before = roll(r, 1, 0)
                gl = linked * 2.0 * r * before / (r + before)
                gr = roll(gl, -1, 0)
            dims.append((alpha, eps, gl, gr))
            chain[0 + 4 * d] = alpha
            chain[1 + 4 * d] = eps
            chain[2 + 4 * d] = gl
            chain[3 + 4 * d] = gr

        def elimination(alpha, eps, gl, gr, fq):
            b00 = 1.0 + gl * alpha * (1.0 + fq)
            b10 = gl * eps * (1.0 + fq)
            det = b00 * (1.0 + gr * alpha) - gr * eps * b10
            return b00, b10, 1.0 / det

        def along(x, fq):
            at = pl.ds(pl.multiple_of(x * 8, 8), 8)
            alpha, eps, gl, gr = [chain[c, at, :] for c in range(4)]
            kk[1, at, :] = fq
            b00, b10, inv = elimination(alpha, eps, gl, gr, fq)
            return -gr * (b00 * alpha - b10 * eps) * inv

        lax.fori_loop(0, E, along, jnp.zeros((8, N), F32))
        alpha, eps, gl, gr = dims[1]
        fq = jnp.zeros((256, N), F32)
        for _ in range(7):
            b00, b10, inv = elimination(alpha, eps, gl, gr, fq)
            fq = linked * roll(-gr * (b00 * alpha - b10 * eps) * inv, 1, 0)
        kk[2] = fq

        def terms(d, fq):
            alpha, eps, gl, gr = [chain[4 * d + c] for c in range(4)]
            b00, b10, inv = elimination(alpha, eps, gl, gr, fq)
            a01, a11 = gr * eps, 1.0 + gr * alpha
            base = 3 + 8 * d
            kk[base] = b00 * inv
            kk[base + 1] = -b10 * inv
            kk[base + 2] = a11 * inv
            kk[base + 3] = -a01 * inv
            kk[base + 4] = gl * (a11 * alpha - a01 * eps) * inv
            kk[base + 5] = -gr * (b00 * alpha - b10 * eps) * inv
            kk[base + 6] = gl * (b00 * eps - b10 * alpha) * inv
            kk[base + 7] = gr * eps * inv

        terms(0, kk[1])
        terms(1, kk[2])
        both_l = lane32 + 0 * p256
        j_of = jnp.where((grp & 1) == 0, both_l, E - 1 - both_l)
        chain[8] = column(r1, j_of)
        chain[9] = column(r0, both_l)
        chain[10] = column(r0, E - 1 - both_l)

        def ordered_rows(land, row, which):
            rows = land.shape[0] // N
            second = 3 if rows == 8 else 2
            return pick(perm[which], land[pl.ds(row, N, stride=rows), :]) + pick(
                perm[which + 1], land[pl.ds(row + second, N, stride=rows), :]
            )

        kk[0] = linked
        owner_wait(send1b, land1b, 6, rs1b, own_sem.at[1])
        yb = ordered_rows(land1b, 1, 0)
        yd = ordered_rows(land1b, 2, 0)
        bl = linked * roll(yb, 1, 0)
        bu = roll(linked, -1, 0) * roll(yb, -1, 0)
        swap = jnp.where(lane < 32, roll(yb, -32), roll(yb, 32))
        out2 = jnp.where(lane < 64, jnp.where(lane < 32, bl, bu) - swap, yd)
        for b in range(2):
            for kind, which in ((0, b), (1, 2 + b)):
                send2a[pl.ds(2 * b + kind, N, stride=4), :] = pick(permt[which], out2)
        to_bricks(send2a, land2a, 4, ss2a, rs2a, own_sem.at[3])
        straight = jnp.where(lane < 96, bl, bu) + roll(yd, 64)
        crossed = jnp.where(lane < 96, roll(straight, -32), roll(straight, 32))
        ends0 = jnp.where(
            (lane == 0) | (lane == 63),
            roll(straight, 64),
            jnp.where(lane == 32, roll(straight, 65), jnp.where(lane == 31, roll(straight, 63), 0.0)),
        )
        chain[11] = ordered_rows(land1b, 0, 0) + jnp.where(
            lane >= 64, chain[4] * straight + chain[5] * crossed, ends0
        )

        @pl.when(at_face)
        def _():
            pltpu.make_async_copy(block(send1c, 0, 4), block(land1c, me, 4), own_sem.at[2]).wait()
            part = land1c.at[pl.ds(0, 4 * (N - 1))]
            pltpu.make_async_remote_copy(
                part, part, rs1c, rs1c, device_id=(me,), device_id_type=MESH
            ).wait_recv()
            chain[11] = chain[11] + ordered_rows(land1c, 0, 2) + ordered_rows(land1c, 1, 0)

        ya = chain[11]

        def before_x(v, n):
            return jnp.concatenate([jnp.zeros((8 * n, N), F32), v[0 : 256 - 8 * n]], 0)

        def after_x(v, n):
            return jnp.concatenate([v[8 * n : 256], jnp.zeros((8 * n, N), F32)], 0)

        def before_y(v, n):
            return roll(v, n, 0)

        def after_y(v, n):
            return roll(v, -n, 0)

        def chains(y0, y1, d, gl, gr, before, after, steps):
            base = 3 + 8 * d
            e1 = kk[base] * y1 + kk[base + 1] * y0
            slope = kk[base + 6]
            for n in steps:
                e1 = e1 + slope * before(e1, n)
                slope = slope * before(slope, n)
            e0 = kk[base + 2] * y0 + kk[base + 3] * y1 + kk[base + 4] * before(e1, 1)
            slope = kk[base + 7]
            zp = e0
            for n in steps:
                zp = zp + slope * after(zp, n)
                slope = slope * after(slope, n)
            zp_next = after(zp, 1)
            zq = e1 + -kk[base + 5] * zp_next
            return -gl * (zp - before(zq, 1)), -gr * (zq - zp_next)

        al, ar = chains(
            ya, roll(ya, -32), 0, chain[2], chain[3], before_x, after_x, (1, 2, 4, 8, 16)
        )
        spread = jnp.where(
            lane < 64,
            jnp.where(lane < 32, al, roll(al, 32)),
            jnp.where(lane < 96, roll(ar, 64), roll(ar, 96)),
        )
        src = iota((N, 2 * N), 0) >> 5
        dst = iota((N, 2 * N), 1)
        side, part = dst >> 7, (dst >> 5) & 3
        sums = pick_right(
            spread * chain[8], one_hot((part >= 2) & (src == 2 * side + part - 2))
        )
        ya = ya + chain[9] * sums[:, 0:N] + chain[10] * sums[:, N : 2 * N]
        bl_c, br_c = chains(ya, roll(ya, -32), 1, chain[6], chain[7], before_y, after_y, (1, 2, 4))
        out1 = jnp.where(
            lane < 64,
            jnp.where(lane < 32, al, roll(ar, 32)),
            jnp.where(lane < 96, bl_c, roll(br_c, 32)),
        )
        for b in range(2):
            for kind, which in ((0, b), (1, 2 + b)):
                send2b[pl.ds(2 * b + kind, N, stride=4), :] = pick(permt[which], out1)
        to_bricks(send2b, land2b, 4, ss2b, rs2b, own_sem.at[4])

    def gathered(land, kind):
        return jnp.concatenate(
            [land[pl.ds(q % 2 * 4 + q // 2 * 2 + kind, E, stride=8), :] for q in range(4)], 0
        )

    brick_wait(send2a, land2a, 4, rs2a, own_sem.at[3])
    own_h, near_h = gathered(land2a, 0), gathered(land2a, 1)
    halo = jnp.transpose(own_h)
    w_near = jnp.zeros((E, N), F32)
    t_near = jnp.zeros((E, N), F32)
    for q in range(4):
        part = near_h[q * E : (q + 1) * E]
        w_near = jnp.where(grp == q, roll(part, E * q - 64), w_near)
        t_near = jnp.where(grp == q, roll(part, E * q - 96), t_near)

    kz_own = jnp.where(up, E - 1 - lane32, lane32)
    kz_near = jnp.where(up, lane32, E - 1 - lane32)
    delta_z = w_near - s_z
    alpha_z = [corners(near_r[2][at : at + 1])[0] for at in (3, 2)]
    mark = jnp.concatenate(
        [
            jnp.where((sub8 == grp) & (lane32 == 0), 1.0, 0.0),
            jnp.where((sub8 == grp) & (lane32 == E - 1), 1.0, 0.0),
        ],
        1,
    )
    weights, cols = [], []
    for which, at, kz, rows_h, wplane in (
        (0, 3, kz_own, own_h, delta_z),
        (1, 2, kz_near, near_h, -delta_z),
    ):
        weights.append(jnp.where(sub8 == grp, column(near_r[2][at : at + 1], kz), 0.0))
        marked = dot_first(dot(weights[which], rows_h), mark)
        pl_ref[which] = marked[0:E, 0:N] + marked[E : 2 * E, N : 2 * N] + alpha_z[which] * wplane
        r1 = near_r[1][at : at + 1]
        cols.append(
            jnp.concatenate(
                [
                    jnp.where(sub8 == grp, column(r1, lane32), 0.0),
                    jnp.where(sub8 == grp, column(r1, E - 1 - lane32), 0.0),
                ],
                1,
            )
        )
        blocks_1[which] = packed_weights(inverse_blocks(r1))
    blocks_1[2] = packed_weights(inverse_blocks(own[2]))

    def on_face(plane, j):
        first = roll(plane, N - j)
        last = roll(plane, (N + E - 1 - j) & (N - 1))
        return jnp.where(face_lane, jnp.where(up, last, first), 0.0)

    pl_ref[2] = halo[0:E]
    pl_ref[3] = halo[E : 2 * E]
    pl_ref[4] = delta_z
    v0, w0 = column(own[0], row32), column(own[0], E - 1 - row32)

    brick_wait(send2b, land2b, 4, rs2b, own_sem.at[4])
    own_ab, near_ab = gathered(land2b, 0), gathered(land2b, 1)
    ab = jnp.transpose(own_ab)
    outer = []
    for which, rows_ab in ((0, own_ab), (1, near_ab)):
        ca = dot(weights[which], rows_ab)
        first_row = jnp.zeros((1, N), F32)
        last_row = jnp.zeros((1, N), F32)
        for q in range(4):
            first_row = jnp.where(grp == q, roll(ca[q : q + 1], E * q), first_row)
            last_row = jnp.where(grp == q, roll(ca[q : q + 1], E * q - E), last_row)
        pl_ref[which, 0:1, :] = pl_ref[which, 0:1, :] + first_row
        pl_ref[which, E - 1 : E, :] = pl_ref[which, E - 1 : E, :] + last_row
        sides = dot_first(ca, cols[which])
        outer.append(sides[64:96, 0:N] + sides[96:128, N : 2 * N])
    h = jnp.zeros((8, N), F32)
    for i in range(E):
        x = jnp.where(sub8 == 2, pl_ref[1, i : i + 1, :], pl_ref[0, i : i + 1, :])
        for at, p in ((4, 2), (5, 3), (6, 4)):
            x = jnp.where(sub8 == at, pl_ref[p, i : i + 1, :], x)
        h = ecm[i] * x + ece[i] * h
        e_ref[i] = h
    for i in range(E - 2, -1, -1):
        h = e_ref[i] + ece[i] * h
        e_ref[i] = h
    z_part = e_ref[:, 6, :]
    ends_z = []
    for which, at in ((0, 3), (1, 2)):
        ends_z.append(packed_dot(e_ref[:, at, :], blocks_1[which]) + outer[which])
    sigma = ends_z[0] + t_own
    tau = ends_z[1] + t_near
    c_plane = -gz * (sigma - tau) / (1.0 + gz * (alpha_z[0] + alpha_z[1]))

    ab_ref[...] = ab

    def answer(j):
        at_lower, at_upper = ab_ref[pl.ds(j, 1), :], ab_ref[pl.ds(E + j, 1), :]
        return v0 * at_lower + w0 * at_upper + on_face(z_part, j)

    solve_j(answer, ab[64:96] + e_ref[:, 4, :], ab[96:128] + e_ref[:, 5, :])
    zblocks = blocks_1[2]

    def finish(t, carry):
        d2 = []
        for m in range(8):
            at = pl.ds(pl.multiple_of((t * 8 + m) * E, E), E)
            d2.append(g_ref[at, :] + on_face(c_plane, t * 8 + m))
        d3 = packed_dot(jnp.concatenate(d2, 0), zblocks)
        at = pl.ds(pl.multiple_of(t * 8 * E, 8 * E), 8 * E)
        d3 = d3 + u_ref[at, :]
        for half in range(2):
            outs = swap_blocks(
                [d3[(half * 4 + m) * E : (half * 4 + m + 1) * E] for m in range(4)], grp
            )
            cols = pl.ds(pl.multiple_of((t * 2 + half) * N, N), N)
            for b in range(2):
                out_c[b, :, cols] = outs[2 * b]
                out_b[b, :, cols] = outs[2 * b + 1]
        return carry

    lax.fori_loop(0, 4, finish, 0)

    for at in range(2):
        gather_all(at).wait_send()
    to_owners_wait(send1b, 6, ss1b)

    def left_c(count):
        part = send1c.at[pl.ds(0, 4 * count)]
        pltpu.make_async_remote_copy(
            part, part, ss1c, ss1c, device_id=(me,), device_id_type=MESH
        ).wait_send()

    @pl.when(at_face)
    def _():
        left_c(3)

    @pl.when(jnp.logical_not(at_face))
    def _():
        left_c(4)

    @pl.when(owner)
    def _():
        to_bricks_wait(send2a, 4, ss2a)
        to_bricks_wait(send2b, 4, ss2b)


def body(calcium, buffer, fraction, rates, inverses, neighbors, ranks):
    vmem = pl.BlockSpec(memory_space=pltpu.VMEM)
    smem = pl.BlockSpec(memory_space=pltpu.SMEM)
    shape = jax.ShapeDtypeStruct(calcium.shape, F32)
    field = pltpu.VMEM((E * E, N), F32)
    return pl.pallas_call(
        step_kernel,
        out_shape=(shape, shape),
        in_specs=[smem, smem, vmem, vmem, vmem, vmem, vmem],
        out_specs=(vmem, vmem),
        scratch_shapes=[
            field,
            field,
            field,
            field,
            pltpu.VMEM((N, 1, N), F32),
            pltpu.VMEM((8 * OWNERS, N), F32),
            pltpu.VMEM((8 * N, N), F32),
            pltpu.VMEM((16, N), F32),
            pltpu.VMEM((4 * N, N), F32),
            pltpu.VMEM((4 * N, N), F32),
            pltpu.VMEM((4 * OWNERS, N), F32),
            pltpu.VMEM((4 * N, N), F32),
            pltpu.VMEM((4 * OWNERS, N), F32),
            pltpu.VMEM((3, 256, 256), BF16),
            pltpu.VMEM((3, E, N), F32),
            pltpu.VMEM((3, E, N), F32),
            pltpu.VMEM((E, 8, N), F32),
            pltpu.VMEM((E, 8, N), F32),
            pltpu.VMEM((E, 8, N), F32),
            pltpu.VMEM((5, E, N), F32),
            pltpu.VMEM((N, N), F32),
            pltpu.VMEM((4, 256, N), BF16),
            pltpu.VMEM((4, N, 256), BF16),
            pltpu.VMEM((19, 256, N), F32),
            pltpu.VMEM((12, 256, N), F32),
        ]
        + [pltpu.SemaphoreType.DMA((2,))] * 2
        + [pltpu.SemaphoreType.DMA] * 8
        + [pltpu.SemaphoreType.DMA((5,))],
        compiler_params=pltpu.CompilerParams(
            collective_id=0, has_side_effects=True, vmem_limit_bytes=60 * 1024 * 1024
        ),
    )(jnp.transpose(rates, (0, 2, 1)), neighbors, neighbors, ranks, calcium, buffer, fraction)


def solution(mesh):
    in_specs = (
        P("bricks", None, None),
        P("bricks", None, None),
        P("bricks", None, None),
        P("bricks", None, None),
        P("bricks", None, None, None, None),
        P(),
        P(),
    )
    out_specs = (P("bricks", None, None), P("bricks", None, None))
    return jax.shard_map(body, mesh=mesh, in_specs=in_specs, out_specs=out_specs, check_vma=False)
```

```python
import jax
import jax.numpy as jnp
from jax import lax
from jax.experimental import pallas as pl
from jax.experimental.pallas import tpu as pltpu
from jax.sharding import PartitionSpec as P

KON = 0.5
KOFF = 0.3
BTOT = 2.0
INFLUX = 0.1

MESH = pl.DeviceIdType.MESH
F32 = jnp.float32
BF16 = jnp.bfloat16
HIGH = lax.Precision.HIGHEST
N = 128
E = 32
OWNERS = 64


def iota(shape, axis):
    return lax.broadcasted_iota(jnp.int32, shape, axis)


def roll(x, shift, axis=-1):
    if axis < 0:
        axis += x.ndim
    if isinstance(shift, int):
        shift %= x.shape[axis]
        if shift == 0:
            return x
    return pltpu.roll(x, shift, axis)


def rho_of(r):
    h = 0.5 / r
    s = jnp.sqrt(h * (2.0 + h))
    return 1.0 + h - s, s - h


def power(log_rho, n):
    return jnp.exp(log_rho * n.astype(F32))


def corners(r):
    rho, gap = rho_of(r)
    p2 = rho * rho
    p4 = p2 * p2
    p8 = p4 * p4
    p16 = p8 * p8
    p32 = p16 * p16
    kappa = rho / (r * gap * (1.0 - p32 * p32))
    return kappa * (1.0 + p32 * p32 / rho), kappa * (p32 / rho + p32)


def column(r, index):
    rho, gap = rho_of(r)
    lr = jnp.log(rho)
    kappa = rho / (r * gap * (1.0 - jnp.exp(lr * 64.0)))
    return kappa * (power(lr, index) + power(lr, 63 - index))


def inverse_blocks(r):
    rho, gap = rho_of(r)
    lr = jnp.log(rho)
    scale = rho / (r * gap * (1.0 + rho) * (1.0 - jnp.exp(lr * 64.0)))
    row, col = iota((N, N), 0), iota((N, N), 1)
    a, b = row & 31, col & 31
    away = jnp.abs(a - b)
    total = power(lr, away) + power(lr, a + b + 1) + power(lr, 63 - a - b) + power(lr, 64 - away)
    return jnp.where((row >> 5) == (col >> 5), total * scale, 0.0)


def sweep_terms(r, index):
    rho, _ = rho_of(r)
    lr = jnp.log(rho)
    rho2 = rho * rho
    odd = power(lr, 2 * index + 1)
    ratio = rho * (1.0 + odd) / (1.0 + odd * rho2)
    last = jnp.exp(lr * 61.0)
    ratio30 = rho * (1.0 + last) / (1.0 + last * rho2)
    m = jnp.where(index == E - 1, 1.0 / (1.0 + r - r * ratio30), ratio / r)
    return m, m * r


def swap_blocks(x, grp):
    low = grp < 2
    even = (grp & 1) == 0
    y = [None] * 4
    for q in range(2):
        a, b = x[q], x[q + 2]
        y[q] = jnp.where(low, a, roll(b, 64))
        y[q + 2] = jnp.where(low, roll(a, 64), b)
    z = [None] * 4
    for q in (0, 2):
        a, b = y[q], y[q + 1]
        z[q] = jnp.where(even, a, roll(b, 32))
        z[q + 1] = jnp.where(even, roll(a, -32), b)
    return z


def split3(x):
    a = x.astype(BF16)
    rest = x - a.astype(F32)
    b = rest.astype(BF16)
    c = (rest - b.astype(F32)).astype(BF16)
    return a, b, c


def pick(select, x):
    out = None
    for part in split3(x):
        term = jnp.dot(select, part, preferred_element_type=F32)
        out = term if out is None else out + term
    return out


def pick_right(x, select):
    out = None
    for part in split3(x):
        term = jnp.dot(part, select, preferred_element_type=F32)
        out = term if out is None else out + term
    return out


def split2(x):
    a = x.astype(BF16)
    return a, (x - a.astype(F32)).astype(BF16)


def contract(a, b, dims):
    ah, al = split2(a)
    bh, bl = split2(b)
    dims = (dims, ((), ()))
    out = lax.dot_general(ah, bh, dims, preferred_element_type=F32)
    out = out + lax.dot_general(al, bh, dims, preferred_element_type=F32)
    return out + lax.dot_general(ah, bl, dims, preferred_element_type=F32)


def dot(a, b):
    return contract(a, b, ((1,), (0,)))


def dot_first(a, b):
    return contract(a, b, ((0,), (0,)))


def dot_last(a, b):
    return contract(a, b, ((1,), (1,)))


def packed_weights(w):
    h, l = split2(w)
    return jnp.concatenate(
        [jnp.concatenate([h, l], 1), jnp.concatenate([h, jnp.zeros_like(h)], 1)], 0
    )


def packed_dot(x, weights):
    out = jnp.dot(jnp.concatenate(split2(x), 1), weights, preferred_element_type=F32)
    return out[:, 0:N] + out[:, N : 2 * N]


def one_hot(cond):
    return jnp.where(cond, 1.0, 0.0).astype(BF16)


def total(x, axis):
    return jnp.sum(x, axis=axis, keepdims=True)


def step_kernel(
    rates, nbs, nbv, rkv, cal, buf, frac, out_c, out_b,
    u_ref, f_ref, t_ref, g_ref, rt, send1b, land1b, send1c, land1c,
    send2a, land2a, send2b, land2b, blocks_1,
    co0, co1, ecm, ece, e_ref, pl_ref, ab_ref, perm, permt, kk, chain,
    ss0, rs0, ss1b, rs1b, ss1c, rs1c, ss2a, rs2a, ss2b, rs2b, own_sem,
):
    me = lax.axis_index("bricks")
    barrier = pltpu.get_barrier_semaphore()

    stages = [(1, [me ^ t for t in range(1, 8)]), (8, [me ^ (8 * t) for t in range(1, 16)])]
    greeted = [to for _, group in stages for to in group]
    for to in greeted:
        pl.semaphore_signal(barrier, inc=1, device_id=(to,), device_id_type=MESH)

    lane = iota((1, N), 1)
    lane32 = lane & 31
    grp = lane >> 5
    sub8 = iota((8, N), 0)
    row32 = iota((E, N), 0)

    own = []
    for d in range(3):
        r = jnp.zeros((1, N), F32)
        for q in range(4):
            r = jnp.where(grp == q, rates[q // 2, q % 2, d], r)
        own.append(r)
    message = jnp.where(lane32 == 0, own[0], jnp.where(lane32 == 1, own[1], own[2]))
    rt[me] = message
    near = {}
    for name, d, side in (("yl", 1, 0), ("yu", 1, 1), ("zl", 2, 0), ("zu", 2, 1)):
        near[name] = [nbs[d, side, 2 * me + b] for b in range(2)]
    near["z"] = [jnp.maximum(near["zl"][b], near["zu"][b]) for b in range(2)]

    def by_brick(pair):
        return jnp.where(lane < 64, pair[0], pair[1])

    up = by_brick([jnp.where(v >= 0, 1, 0) for v in near["zu"]]) == 1
    upf = jnp.where(up, 1.0, 0.0)
    face_lane = lane32 == jnp.where(up, E - 1, 0)

    def lay(t, carry):
        cols = pl.ds(pl.multiple_of(t * N, N), N)
        us, fs = [], []
        for b in range(2):
            ca, bo, al = cal[b, :, cols], buf[b, :, cols], frac[b, :, cols]
            bind = KON * ca * (BTOT - bo) - KOFF * bo
            us += [ca, bo]
            fs += [2.0 * ca - bind + INFLUX * (1.0 - al) / al, 2.0 * bo + bind]
        us = swap_blocks(us, grp)
        fs = swap_blocks(fs, grp)
        for m in range(4):
            at = pl.ds(pl.multiple_of((t * 4 + m) * E, E), E)
            u_ref[at, :] = us[m]
            f_ref[at, :] = fs[m]
        return carry

    lax.fori_loop(0, 8, lay, 0)

    for co, r in ((co0, own[0]), (co1, own[1])):
        m, e = sweep_terms(r, row32)
        co[0] = m
        co[1] = e
        co[2] = jnp.where(row32 == E - 1, 0.0, e)

    owner = (me & 1) == 0
    @pl.when(owner)
    def _():
        s2, l2 = iota((256, 256), 0), iota((256, 256), 1)
        lane256 = iota((1, 256), 1)

        def heads(before, doublings):
            target = jnp.where(before < 0, lane256, before)
            step = one_hot(s2 == target)
            for _ in range(doublings):
                step = jnp.dot(step, step, preferred_element_type=F32).astype(BF16)
            return step

        before0, before1 = nbv[0, 0:1, :], nbv[1, 0:1, :]
        znear = jnp.maximum(nbv[2, 0:1, :], nbv[2, 1:2, :]).astype(F32)
        rank0, rank1 = rkv[0:1, :].astype(F32), rkv[1:2, :].astype(F32)
        lead = jnp.dot(heads(before1, 3), heads(before0, 5), preferred_element_type=F32)
        key = total(lead * s2.astype(F32), 0) * 32.0 + rank1
        keyed = total(jnp.where(s2 == l2, key + rank0 * 1e5, 0.0), 1)
        row = total(jnp.where(keyed < key, 1.0, 0.0), 0)
        pos = rank0 * 8.0 + row
        at = s2.astype(F32) == pos
        slot_at = total(jnp.where(at, lane256.astype(F32), 0.0), 1)
        rank_at = total(jnp.where(at, rank1, 0.0), 1)
        z_at = total(jnp.where(at, znear, 0.0), 1)
        kk[0] = jnp.where(rank_at > 0.5, 1.0, jnp.zeros((256, N), F32))
        dev = lane.astype(F32) * 2.0
        s1, l1 = iota((N, 256), 0), iota((N, 256), 1)
        lf = l1.astype(F32)
        for b in range(2):
            perm[b] = one_hot(slot_at == dev + b)
            perm[2 + b] = one_hot(z_at == dev + b)
            mine = l1 == 2 * s1 + b
            pos_b = total(jnp.where(mine, pos, 0.0), 1)
            z_b = total(jnp.where(mine, znear, 0.0), 1)
            posz_b = total(jnp.where(lf == z_b, pos + 1.0, 0.0), 1) - 1.0
            permt[b] = one_hot(lf == pos_b)
            permt[2 + b] = one_hot(lf == posz_b)

    pl.semaphore_wait(barrier, len(greeted))

    def rates_block(unit):
        return rt.at[pl.ds(me & (N - unit), unit)]

    def gather_start(at):
        unit, group = stages[at]
        for to in group:
            pltpu.make_async_remote_copy(
                rates_block(unit), rates_block(unit), ss0.at[at], rs0.at[at],
                device_id=(to,), device_id_type=MESH,
            ).start()

    def gather_all(at):
        unit, group = stages[at]
        part = rt.at[pl.ds(0, unit * len(group))]
        return pltpu.make_async_remote_copy(
            part, part, ss0.at[at], rs0.at[at], device_id=(me,), device_id_type=MESH
        )

    gather_start(0)

    def face(j, plane):
        u = u_ref[pl.ds(pl.multiple_of(j * E, E), E), :]
        first = roll(u, j)
        last = roll(u, j + (N - E + 1))
        return jnp.where(lane32 == j, jnp.where(up, last, first), plane)

    wz = lax.fori_loop(0, E, face, jnp.zeros((E, N), F32))

    cu2 = jnp.where(lane32 < E - 1, 2.0 * own[2], 0.0)
    cd2 = jnp.where(lane32 > 0, 2.0 * own[2], 0.0)
    dg2 = cu2 + cd2
    r1x2 = 2.0 * own[1]

    def right_side(t, prev):
        us = []
        for m in range(5):
            j = jnp.minimum(t * 4 + m, E - 1)
            us.append(u_ref[pl.ds(pl.multiple_of(j * E, E), E), :])
        for m in range(4):
            j = t * 4 + m
            at = pl.ds(pl.multiple_of(j * E, E), E)
            u = us[m]
            low = jnp.where(j == 0, 0.0, r1x2)
            high = jnp.where(j == E - 1, 0.0, r1x2)
            f_ref[at, :] = (
                f_ref[at, :]
                + cu2 * roll(u, -1)
                + cd2 * roll(u, 1)
                + low * prev
                + high * us[m + 1]
                - (dg2 + low + high) * u
            )
            prev = u
        return prev

    lax.fori_loop(0, E // 4, right_side, jnp.zeros((E, N), F32))

    gather_all(0).wait_recv()
    gather_start(1)

    def solve_i(load_plane_row):
        def forward(t, carry):
            g, h = carry
            for m in range(4):
                i = t * 4 + m
                at = pl.ds(i, E, stride=E)
                g = co0[0, pl.ds(i, 1), :] * f_ref[at, :] + co0[1, pl.ds(i, 1), :] * g
                t_ref[at, :] = g
                if load_plane_row is not None:
                    h = ecm[i] * load_plane_row(i) + ece[i] * h
                    e_ref[i] = h
            return g, h

        lax.fori_loop(0, E // 4, forward, (jnp.zeros((E, N), F32), jnp.zeros((8, N), F32)))

        def backward(t, carry):
            x, h = carry
            for m in range(4):
                i = E - 1 - t * 4 - m
                at = pl.ds(i, E, stride=E)
                x = t_ref[at, :] + co0[2, pl.ds(i, 1), :] * x
                t_ref[at, :] = x
                if load_plane_row is not None:
                    h = e_ref[i] + jnp.where(i == E - 1, 0.0, ece[i]) * h
                    e_ref[i] = h
            return x, h

        lax.fori_loop(0, E // 4, backward, (jnp.zeros((E, N), F32), jnp.zeros((8, N), F32)))

    def solve_j(extra, extra_first, extra_last):
        def forward(t, g):
            for m in range(4):
                j = t * 4 + m
                at = pl.ds(pl.multiple_of(j * E, E), E)
                d = t_ref[at, :] - 2.0 * u_ref[at, :]
                if extra is not None:
                    d = d + extra(j)
                if extra_first is not None and m == 0:
                    d = d + jnp.where(j == 0, extra_first, 0.0)
                if extra_last is not None and m == 3:
                    d = d + jnp.where(j == E - 1, extra_last, 0.0)
                g = co1[0, pl.ds(j, 1), :] * d + co1[1, pl.ds(j, 1), :] * g
                g_ref[at, :] = g
            return g

        lax.fori_loop(0, E // 4, forward, jnp.zeros((E, N), F32))

        def backward(t, x):
            for m in range(4):
                j = E - 1 - t * 4 - m
                at = pl.ds(pl.multiple_of(j * E, E), E)
                x = g_ref[at, :] + co1[2, pl.ds(j, 1), :] * x
                g_ref[at, :] = x
            return x

        lax.fori_loop(0, E // 4, backward, jnp.zeros((E, N), F32))

    solve_i(None)
    solve_j(None, None, None)

    rowN, colN = iota((N, N), 0), iota((N, N), 1)
    kin = rowN & 31
    weight = column(own[2], jnp.where(up, E - 1 - kin, kin))
    weight = packed_weights(jnp.where((rowN >> 5) == (colN >> 5), weight, 0.0))

    def face_mean(t, plane):
        y = packed_dot(g_ref[pl.ds(pl.multiple_of(t * 8 * E, 8 * E), 8 * E), :], weight)
        for m in range(8):
            plane = jnp.where(lane32 == t * 8 + m, y[m * E : (m + 1) * E], plane)
        return plane

    t_own = lax.fori_loop(0, 4, face_mean, jnp.zeros((E, N), F32))

    rows_a = jnp.transpose(
        jnp.concatenate(
            [
                t_ref[pl.ds(0, E, stride=E), :],
                t_ref[pl.ds(E - 1, E, stride=E), :],
                g_ref[0:E, :],
                g_ref[(E - 1) * E : E * E, :],
            ],
            0,
        )
    )
    for q in range(4):
        send1b[pl.ds(8 * (q % 2) + 3 * (q // 2), E, stride=16), :] = rows_a[q * E : (q + 1) * E]
    mine = me >> 1

    def block(ref, index, rows):
        pitch = 8 if rows == 6 else rows
        return ref.at[pl.ds(pl.multiple_of(index * pitch, pitch), rows)]

    def to_owners(src, dst, rows, send_sem, recv_sem, local_sem):
        def send(step, carry):
            o = (mine + step) & (OWNERS - 1)
            pltpu.make_async_remote_copy(
                block(src, o, rows), block(dst, me, rows), send_sem, recv_sem,
                device_id=(2 * o,), device_id_type=MESH,
            ).start()
            return carry

        lax.fori_loop(1, OWNERS, send, 0)

        @pl.when(jnp.logical_not(owner))
        def _():
            pltpu.make_async_remote_copy(
                block(src, mine, rows), block(dst, me, rows), send_sem, recv_sem,
                device_id=(2 * mine,), device_id_type=MESH,
            ).start()

        @pl.when(owner)
        def _():
            pltpu.make_async_copy(block(src, mine, rows), block(dst, me, rows), local_sem).start()

    def to_owners_wait(src, rows, send_sem):
        def left(count):
            part = src.at[pl.ds(0, count * rows)]
            pltpu.make_async_remote_copy(
                part, part, send_sem, send_sem, device_id=(me,), device_id_type=MESH
            ).wait_send()

        @pl.when(owner)
        def _():
            left(OWNERS - 1)

        @pl.when(jnp.logical_not(owner))
        def _():
            left(OWNERS)

    def owner_wait(src, dst, rows, recv_sem, local_sem):
        pltpu.make_async_copy(block(src, mine, rows), block(dst, me, rows), local_sem).wait()
        part = dst.at[pl.ds(0, rows * (N - 1))]
        pltpu.make_async_remote_copy(
            part, part, recv_sem, recv_sem, device_id=(me,), device_id_type=MESH
        ).wait_recv()

    def to_bricks(src, dst, rows, send_sem, recv_sem, local_sem):
        def send(step, carry):
            to = (me + step) & (N - 1)
            pltpu.make_async_remote_copy(
                block(src, to, rows), block(dst, mine, rows), send_sem, recv_sem,
                device_id=(to,), device_id_type=MESH,
            ).start()
            return carry

        lax.fori_loop(1, N, send, 0)
        pltpu.make_async_copy(block(src, me, rows), block(dst, mine, rows), local_sem).start()

    def to_bricks_wait(src, rows, send_sem):
        part = src.at[pl.ds(0, rows * (N - 1))]
        pltpu.make_async_remote_copy(
            part, part, send_sem, send_sem, device_id=(me,), device_id_type=MESH
        ).wait_send()

    def brick_wait(src, dst, rows, recv_sem, local_sem):
        def arrived(count):
            part = dst.at[pl.ds(0, count * rows)]
            pltpu.make_async_remote_copy(
                part, part, recv_sem, recv_sem, device_id=(me,), device_id_type=MESH
            ).wait_recv()

        @pl.when(owner)
        def _():
            pltpu.make_async_copy(block(src, me, rows), block(dst, mine, rows), local_sem).wait()
            arrived(OWNERS - 1)

        @pl.when(jnp.logical_not(owner))
        def _():
            arrived(OWNERS)


    gather_all(1).wait_recv()

    def rates_of(indices):
        rows = []
        for b in range(2):
            index = jnp.maximum(indices[b], 0)
            got = rt[index >> 1]
            cross = (index & 1) != b
            rows.append(jnp.where(cross, roll(got, 64), got))
        got = jnp.where(lane < 64, rows[0], rows[1])
        has = by_brick([jnp.where(indices[b] >= 0, 1.0, 0.0) for b in range(2)])
        return got, has

    stack = jnp.ones((8, N), F32)
    has = jnp.zeros((8, N), F32)
    for at, name in ((0, "yu"), (1, "yl"), (2, "z")):
        got, there = rates_of(near[name])
        stack = jnp.where(sub8 == at, got, stack)
        has = jnp.where(sub8 == at, there, has)
    stack = jnp.where((sub8 >= 3) & (sub8 < 7), message, stack)
    near_r = []
    for d in range(3):
        x = roll(jnp.where(lane32 == d, stack, 0.0), -d)
        for shift in (1, 2, 4, 8, 16):
            x = x + roll(x, shift)
        near_r.append(x)
    g1 = has * 2.0 * own[1] * near_r[1] / (own[1] + near_r[1])
    g2 = has * 2.0 * own[2] * near_r[2] / (own[2] + near_r[2])
    gyu, gyl, gz = g1[0:1], g1[1:2], g2[2:3]

    u_first, u_last = u_ref[0:E, :], u_ref[(E - 1) * E : E * E, :]
    s_up = 2.0 * gyu * u_last
    s_low = 2.0 * gyl * u_first
    s_z = 2.0 * gz * wz
    i8 = iota((E, 8, N), 0)
    mm, ee = sweep_terms(near_r[0][None], i8)
    ecm[...] = mm
    ece[...] = ee
    pl_ref[0] = s_up
    pl_ref[1] = s_low
    pl_ref[2] = s_z

    h = jnp.zeros((8, N), F32)
    for i in range(E):
        x_up, x_low, x_z = [pl_ref[p, i : i + 1, :] for p in range(3)]
        x = jnp.where(sub8 == 0, x_up, jnp.where(sub8 == 1, x_low, x_z))
        x = jnp.where(sub8 == 3, -x_z, jnp.where(sub8 == 4, -x_low, jnp.where(sub8 == 5, -x_up, x)))
        h = ecm[i] * x + ece[i] * h
        e_ref[i] = h
    for i in range(E - 2, -1, -1):
        h = e_ref[i] + ece[i] * h
        e_ref[i] = h
    p_up, p_low, p_z, p_out, p_first, p_last = [e_ref[:, p, :] for p in range(6)]

    rows_b = jnp.transpose(jnp.concatenate([s_up, s_low, p_up, p_low], 0))
    rows_d = jnp.transpose(jnp.concatenate([p_first, p_last], 0))
    group8 = (sub8 & 3) == grp
    ends_i = []
    for p, at in ((p_z, 2), (p_out, 3)):
        r1 = near_r[1][at : at + 1]
        ends = jnp.where(sub8 < 4, column(r1, lane32), column(r1, E - 1 - lane32))
        x = dot_last(jnp.where(group8, ends, 0.0), p)
        ends_i.append(jnp.concatenate([x, jnp.zeros((8, N - E), F32)], 1))

    def end_row(p, x, q):
        c = jnp.where(lane < 32, roll(p[0:1], -E * q), roll(p[E - 1 : E], E - E * q))
        c = jnp.where(lane < 64, c, roll(x[q : q + 1], 64))
        return jnp.where(lane < 96, c, roll(x[q + 4 : q + 5], 96))

    for q in range(4):
        b, sp = q // 2, q % 2
        mine_up = near["zu"][b] >= 0
        first_face = jnp.where(mine_up, 0.0, 1.0)
        c_near, c_own = end_row(p_z, ends_i[0], q), end_row(p_out, ends_i[1], q)
        send1c[4 * sp + 2 * b : 4 * sp + 2 * b + 1, :] = c_near * (1.0 - first_face)
        send1c[4 * sp + 2 * b + 1 : 4 * sp + 2 * b + 2, :] = c_own * first_face
        send1c[8 + 4 * sp + 2 * b : 8 + 4 * sp + 2 * b + 1, :] = c_near * first_face
        send1c[8 + 4 * sp + 2 * b + 1 : 8 + 4 * sp + 2 * b + 2, :] = c_own * (1.0 - first_face)
        send1b[pl.ds(8 * sp + 3 * b + 1, E, stride=16), :] = rows_b[q * E : (q + 1) * E]
        zt = jnp.where(lane < 96, roll(s_z, 64 - E * q), roll(t_own, 96 - E * q))
        part = jnp.concatenate([rows_d[q * E : (q + 1) * E], jnp.zeros((E, 64), F32)], 1)
        send1b[pl.ds(8 * sp + 3 * b + 2, E, stride=16), :] = jnp.where(lane < 64, part, zt)

    to_owners(send1b, land1b, 6, ss1b, rs1b, own_sem.at[1])

    face_owners = [0, 1, OWNERS - 2, OWNERS - 1]
    for c, o in enumerate(face_owners):

        @pl.when(me != 2 * o)
        def _(c=c, o=o):
            pltpu.make_async_remote_copy(
                block(send1c, c, 4), block(land1c, me, 4), ss1c, rs1c,
                device_id=(2 * o,), device_id_type=MESH,
            ).start()

        @pl.when(me == 2 * o)
        def _(c=c):
            pltpu.make_async_copy(block(send1c, c, 4), block(land1c, me, 4), own_sem.at[2]).start()

    at_face = jnp.logical_and(owner, jnp.logical_or(mine < 2, mine >= OWNERS - 2))

    @pl.when(owner)
    def _():
        sp32 = (mine & 1) * 32
        table = rt[:, 0, :]
        ordered = pick(perm[0], table) + pick(perm[1], roll(table, 64))
        pick_at = iota((N, 2 * N), 0)
        pick_to = iota((N, 2 * N), 1) >> 7
        both = pick_right(ordered, one_hot(pick_at == sp32 + pick_to))
        r0, r1 = both[:, 0:N], both[:, N : 2 * N]
        p256 = iota((256, N), 0)
        linked = kk[0]
        dims = []
        for d, r in ((0, r0), (1, r1)):
            alpha, eps = corners(r)
            if d == 0:
                before = jnp.concatenate([r[0:8], r[0:248]], 0)
                gl = jnp.where(p256 >= 8, 2.0 * r * before / (r + before), 0.0)
                gr = jnp.concatenate([gl[8:256], jnp.zeros((8, N), F32)], 0)
            else:
                before = roll(r, 1, 0)
                gl = linked * 2.0 * r * before / (r + before)
                gr = roll(gl, -1, 0)
            dims.append((alpha, eps, gl, gr))
            chain[0 + 4 * d] = alpha
            chain[1 + 4 * d] = eps
            chain[2 + 4 * d] = gl
            chain[3 + 4 * d] = gr

        def elimination(alpha, eps, gl, gr, fq):
            b00 = 1.0 + gl * alpha * (1.0 + fq)
            b10 = gl * eps * (1.0 + fq)
            det = b00 * (1.0 + gr * alpha) - gr * eps * b10
            return b00, b10, 1.0 / det

        def along(x, fq):
            at = pl.ds(pl.multiple_of(x * 8, 8), 8)
            alpha, eps, gl, gr = [chain[c, at, :] for c in range(4)]
            kk[1, at, :] = fq
            b00, b10, inv = elimination(alpha, eps, gl, gr, fq)
            return -gr * (b00 * alpha - b10 * eps) * inv

        lax.fori_loop(0, E, along, jnp.zeros((8, N), F32))
        alpha, eps, gl, gr = dims[1]
        fq = jnp.zeros((256, N), F32)
        for _ in range(7):
            b00, b10, inv = elimination(alpha, eps, gl, gr, fq)
            fq = linked * roll(-gr * (b00 * alpha - b10 * eps) * inv, 1, 0)
        kk[2] = fq

        def terms(d, fq):
            alpha, eps, gl, gr = [chain[4 * d + c] for c in range(4)]
            b00, b10, inv = elimination(alpha, eps, gl, gr, fq)
            a01, a11 = gr * eps, 1.0 + gr * alpha
            base = 3 + 8 * d
            kk[base] = b00 * inv
            kk[base + 1] = -b10 * inv
            kk[base + 2] = a11 * inv
            kk[base + 3] = -a01 * inv
            kk[base + 4] = gl * (a11 * alpha - a01 * eps) * inv
            kk[base + 5] = -gr * (b00 * alpha - b10 * eps) * inv
            kk[base + 6] = gl * (b00 * eps - b10 * alpha) * inv
            kk[base + 7] = gr * eps * inv

        terms(0, kk[1])
        terms(1, kk[2])
        both_l = lane32 + 0 * p256
        j_of = jnp.where((grp & 1) == 0, both_l, E - 1 - both_l)
        chain[8] = column(r1, j_of)
        chain[9] = column(r0, both_l)
        chain[10] = column(r0, E - 1 - both_l)

        def ordered_rows(land, row, which):
            rows = land.shape[0] // N
            second = 3 if rows == 8 else 2
            return pick(perm[which], land[pl.ds(row, N, stride=rows), :]) + pick(
                perm[which + 1], land[pl.ds(row + second, N, stride=rows), :]
            )

        kk[0] = linked
        owner_wait(send1b, land1b, 6, rs1b, own_sem.at[1])
        yb = ordered_rows(land1b, 1, 0)
        yd = ordered_rows(land1b, 2, 0)
        bl = linked * roll(yb, 1, 0)
        bu = roll(linked, -1, 0) * roll(yb, -1, 0)
        swap = jnp.where(lane < 32, roll(yb, -32), roll(yb, 32))
        out2 = jnp.where(lane < 64, jnp.where(lane < 32, bl, bu) - swap, yd)
        for b in range(2):
            for kind, which in ((0, b), (1, 2 + b)):
                send2a[pl.ds(2 * b + kind, N, stride=4), :] = pick(permt[which], out2)
        to_bricks(send2a, land2a, 4, ss2a, rs2a, own_sem.at[3])
        straight = jnp.where(lane < 96, bl, bu) + roll(yd, 64)
        crossed = jnp.where(lane < 96, roll(straight, -32), roll(straight, 32))
        ends0 = jnp.where(
            (lane == 0) | (lane == 63),
            roll(straight, 64),
            jnp.where(lane == 32, roll(straight, 65), jnp.where(lane == 31, roll(straight, 63), 0.0)),
        )
        chain[11] = ordered_rows(land1b, 0, 0) + jnp.where(
            lane >= 64, chain[4] * straight + chain[5] * crossed, ends0
        )

        @pl.when(at_face)
        def _():
            pltpu.make_async_copy(block(send1c, 0, 4), block(land1c, me, 4), own_sem.at[2]).wait()
            part = land1c.at[pl.ds(0, 4 * (N - 1))]
            pltpu.make_async_remote_copy(
                part, part, rs1c, rs1c, device_id=(me,), device_id_type=MESH
            ).wait_recv()
            chain[11] = chain[11] + ordered_rows(land1c, 0, 2) + ordered_rows(land1c, 1, 0)

        ya = chain[11]

        def before_x(v, n):
            return jnp.concatenate([jnp.zeros((8 * n, N), F32), v[0 : 256 - 8 * n]], 0)

        def after_x(v, n):
            return jnp.concatenate([v[8 * n : 256], jnp.zeros((8 * n, N), F32)], 0)

        def before_y(v, n):
            return roll(v, n, 0)

        def after_y(v, n):
            return roll(v, -n, 0)

        def chains(y0, y1, d, gl, gr, before, after, steps):
            base = 3 + 8 * d
            e1 = kk[base] * y1 + kk[base + 1] * y0
            slope = kk[base + 6]
            for n in steps:
                e1 = e1 + slope * before(e1, n)
                slope = slope * before(slope, n)
            e0 = kk[base + 2] * y0 + kk[base + 3] * y1 + kk[base + 4] * before(e1, 1)
            slope = kk[base + 7]
            zp = e0
            for n in steps:
                zp = zp + slope * after(zp, n)
                slope = slope * after(slope, n)
            zp_next = after(zp, 1)
            zq = e1 + -kk[base + 5] * zp_next
            return -gl * (zp - before(zq, 1)), -gr * (zq - zp_next)

        al, ar = chains(
            ya, roll(ya, -32), 0, chain[2], chain[3], before_x, after_x, (1, 2, 4, 8, 16)
        )
        spread = jnp.where(
            lane < 64,
            jnp.where(lane < 32, al, roll(al, 32)),
            jnp.where(lane < 96, roll(ar, 64), roll(ar, 96)),
        )
        src = iota((N, 2 * N), 0) >> 5
        dst = iota((N, 2 * N), 1)
        side, part = dst >> 7, (dst >> 5) & 3
        sums = pick_right(
            spread * chain[8], one_hot((part >= 2) & (src == 2 * side + part - 2))
        )
        ya = ya + chain[9] * sums[:, 0:N] + chain[10] * sums[:, N : 2 * N]
        bl_c, br_c = chains(ya, roll(ya, -32), 1, chain[6], chain[7], before_y, after_y, (1, 2, 4))
        out1 = jnp.where(
            lane < 64,
            jnp.where(lane < 32, al, roll(ar, 32)),
            jnp.where(lane < 96, bl_c, roll(br_c, 32)),
        )
        for b in range(2):
            for kind, which in ((0, b), (1, 2 + b)):
                send2b[pl.ds(2 * b + kind, N, stride=4), :] = pick(permt[which], out1)
        to_bricks(send2b, land2b, 4, ss2b, rs2b, own_sem.at[4])

    def gathered(land, kind):
        return jnp.concatenate(
            [land[pl.ds(q % 2 * 4 + q // 2 * 2 + kind, E, stride=8), :] for q in range(4)], 0
        )

    brick_wait(send2a, land2a, 4, rs2a, own_sem.at[3])
    own_h, near_h = gathered(land2a, 0), gathered(land2a, 1)
    halo = jnp.transpose(own_h)
    w_near = jnp.zeros((E, N), F32)
    t_near = jnp.zeros((E, N), F32)
    for q in range(4):
        part = near_h[q * E : (q + 1) * E]
        w_near = jnp.where(grp == q, roll(part, E * q - 64), w_near)
        t_near = jnp.where(grp == q, roll(part, E * q - 96), t_near)

    kz_own = jnp.where(up, E - 1 - lane32, lane32)
    kz_near = jnp.where(up, lane32, E - 1 - lane32)
    delta_z = w_near - s_z
    alpha_z = [corners(near_r[2][at : at + 1])[0] for at in (3, 2)]
    mark = jnp.concatenate(
        [
            jnp.where((sub8 == grp) & (lane32 == 0), 1.0, 0.0),
            jnp.where((sub8 == grp) & (lane32 == E - 1), 1.0, 0.0),
        ],
        1,
    )
    weights, cols = [], []
    for which, at, kz, rows_h, wplane in (
        (0, 3, kz_own, own_h, delta_z),
        (1, 2, kz_near, near_h, -delta_z),
    ):
        weights.append(jnp.where(sub8 == grp, column(near_r[2][at : at + 1], kz), 0.0))
        marked = dot_first(dot(weights[which], rows_h), mark)
        pl_ref[which] = marked[0:E, 0:N] + marked[E : 2 * E, N : 2 * N] + alpha_z[which] * wplane
        r1 = near_r[1][at : at + 1]
        cols.append(
            jnp.concatenate(
                [
                    jnp.where(sub8 == grp, column(r1, lane32), 0.0),
                    jnp.where(sub8 == grp, column(r1, E - 1 - lane32), 0.0),
                ],
                1,
            )
        )
        blocks_1[which] = packed_weights(inverse_blocks(r1))
    blocks_1[2] = packed_weights(inverse_blocks(own[2]))

    def on_face(plane, j):
        first = roll(plane, N - j)
        last = roll(plane, (N + E - 1 - j) & (N - 1))
        return jnp.where(face_lane, jnp.where(up, last, first), 0.0)

    pl_ref[2] = halo[0:E]
    pl_ref[3] = halo[E : 2 * E]
    pl_ref[4] = delta_z
    v0, w0 = column(own[0], row32), column(own[0], E - 1 - row32)

    brick_wait(send2b, land2b, 4, rs2b, own_sem.at[4])
    own_ab, near_ab = gathered(land2b, 0), gathered(land2b, 1)
    ab = jnp.transpose(own_ab)
    outer = []
    for which, rows_ab in ((0, own_ab), (1, near_ab)):
        ca = dot(weights[which], rows_ab)
        first_row = jnp.zeros((1, N), F32)
        last_row = jnp.zeros((1, N), F32)
        for q in range(4):
            first_row = jnp.where(grp == q, roll(ca[q : q + 1], E * q), first_row)
            last_row = jnp.where(grp == q, roll(ca[q : q + 1], E * q - E), last_row)
        pl_ref[which, 0:1, :] = pl_ref[which, 0:1, :] + first_row
        pl_ref[which, E - 1 : E, :] = pl_ref[which, E - 1 : E, :] + last_row
        sides = dot_first(ca, cols[which])
        outer.append(sides[64:96, 0:N] + sides[96:128, N : 2 * N])
    h = jnp.zeros((8, N), F32)
    for i in range(E):
        x = jnp.where(sub8 == 2, pl_ref[1, i : i + 1, :], pl_ref[0, i : i + 1, :])
        for at, p in ((4, 2), (5, 3), (6, 4)):
            x = jnp.where(sub8 == at, pl_ref[p, i : i + 1, :], x)
        h = ecm[i] * x + ece[i] * h
        e_ref[i] = h
    for i in range(E - 2, -1, -1):
        h = e_ref[i] + ece[i] * h
        e_ref[i] = h
    z_part = e_ref[:, 6, :]
    ends_z = []
    for which, at in ((0, 3), (1, 2)):
        ends_z.append(packed_dot(e_ref[:, at, :], blocks_1[which]) + outer[which])
    sigma = ends_z[0] + t_own
    tau = ends_z[1] + t_near
    c_plane = -gz * (sigma - tau) / (1.0 + gz * (alpha_z[0] + alpha_z[1]))

    ab_ref[...] = ab

    def answer(j):
        at_lower, at_upper = ab_ref[pl.ds(j, 1), :], ab_ref[pl.ds(E + j, 1), :]
        return v0 * at_lower + w0 * at_upper + on_face(z_part, j)

    solve_j(answer, ab[64:96] + e_ref[:, 4, :], ab[96:128] + e_ref[:, 5, :])
    zblocks = blocks_1[2]

    def finish(t, carry):
        d2 = []
        for m in range(8):
            at = pl.ds(pl.multiple_of((t * 8 + m) * E, E), E)
            d2.append(g_ref[at, :] + on_face(c_plane, t * 8 + m))
        d3 = packed_dot(jnp.concatenate(d2, 0), zblocks)
        at = pl.ds(pl.multiple_of(t * 8 * E, 8 * E), 8 * E)
        d3 = d3 + u_ref[at, :]
        for half in range(2):
            outs = swap_blocks(
                [d3[(half * 4 + m) * E : (half * 4 + m + 1) * E] for m in range(4)], grp
            )
            cols = pl.ds(pl.multiple_of((t * 2 + half) * N, N), N)
            for b in range(2):
                out_c[b, :, cols] = outs[2 * b]
                out_b[b, :, cols] = outs[2 * b + 1]
        return carry

    lax.fori_loop(0, 4, finish, 0)

    for at in range(2):
        gather_all(at).wait_send()
    to_owners_wait(send1b, 6, ss1b)

    def left_c(count):
        part = send1c.at[pl.ds(0, 4 * count)]
        pltpu.make_async_remote_copy(
            part, part, ss1c, ss1c, device_id=(me,), device_id_type=MESH
        ).wait_send()

    @pl.when(at_face)
    def _():
        left_c(3)

    @pl.when(jnp.logical_not(at_face))
    def _():
        left_c(4)

    @pl.when(owner)
    def _():
        to_bricks_wait(send2a, 4, ss2a)
        to_bricks_wait(send2b, 4, ss2b)


def body(calcium, buffer, fraction, rates, inverses, neighbors, ranks):
    vmem = pl.BlockSpec(memory_space=pltpu.VMEM)
    smem = pl.BlockSpec(memory_space=pltpu.SMEM)
    shape = jax.ShapeDtypeStruct(calcium.shape, F32)
    field = pltpu.VMEM((E * E, N), F32)
    return pl.pallas_call(
        step_kernel,
        out_shape=(shape, shape),
        in_specs=[smem, smem, vmem, vmem, vmem, vmem, vmem],
        out_specs=(vmem, vmem),
        scratch_shapes=[
            field,
            field,
            field,
            field,
            pltpu.VMEM((N, 1, N), F32),
            pltpu.VMEM((8 * OWNERS, N), F32),
            pltpu.VMEM((8 * N, N), F32),
            pltpu.VMEM((16, N), F32),
            pltpu.VMEM((4 * N, N), F32),
            pltpu.VMEM((4 * N, N), F32),
            pltpu.VMEM((4 * OWNERS, N), F32),
            pltpu.VMEM((4 * N, N), F32),
            pltpu.VMEM((4 * OWNERS, N), F32),
            pltpu.VMEM((3, 256, 256), BF16),
            pltpu.VMEM((3, E, N), F32),
            pltpu.VMEM((3, E, N), F32),
            pltpu.VMEM((E, 8, N), F32),
            pltpu.VMEM((E, 8, N), F32),
            pltpu.VMEM((E, 8, N), F32),
            pltpu.VMEM((5, E, N), F32),
            pltpu.VMEM((N, N), F32),
            pltpu.VMEM((4, 256, N), BF16),
            pltpu.VMEM((4, N, 256), BF16),
            pltpu.VMEM((19, 256, N), F32),
            pltpu.VMEM((12, 256, N), F32),
        ]
        + [pltpu.SemaphoreType.DMA((2,))] * 2
        + [pltpu.SemaphoreType.DMA] * 8
        + [pltpu.SemaphoreType.DMA((5,))],
        compiler_params=pltpu.CompilerParams(
            collective_id=0, has_side_effects=True, vmem_limit_bytes=60 * 1024 * 1024
        ),
    )(jnp.transpose(rates, (0, 2, 1)), neighbors, neighbors, ranks, calcium, buffer, fraction)


def solution(mesh):
    in_specs = (
        P("bricks", None, None),
        P("bricks", None, None),
        P("bricks", None, None),
        P("bricks", None, None),
        P("bricks", None, None, None, None),
        P(),
        P(),
    )
    out_specs = (P("bricks", None, None), P("bricks", None, None))
    return jax.shard_map(body, mesh=mesh, in_specs=in_specs, out_specs=out_specs, check_vma=False)
```
